32 devices in a mesh: dp: 4 (over y, x), seq: 8 (over z, core).
Axes of the slice: x: 2, y: 2, z: 4, core: 2. Of those that a mesh axis runs over, the one named last changes fastest.
Arguments:
- inputs: bfloat16 [4096, 1536], P(('dp', 'seq')), may hold values from -6 to 6
- cotangent: bfloat16 [4096, 1536], P(('dp', 'seq')), may hold values from -6 to 6
- doc_ids: int32 [4096], P(('dp', 'seq')), may hold values from 0 to 7, as said below
- positions: int32 [4096], P(('dp', 'seq')), may hold values from 0 to 1023, as said below
- gain_first: bfloat16 [1536], P(('dp', 'seq')), may hold values from 0.099609375 to 1.8984375
- query_weight: bfloat16 [1536, 1536], P(('dp', 'seq')), may hold values from -0.21875 to 0.21875
- key_weight: bfloat16 [1536, 768], P(('dp', 'seq')), may hold values from -0.15625 to 0.15625
- value_weight: bfloat16 [1536, 768], P(('dp', 'seq')), may hold values from -0.15625 to 0.15625
- output_weight: bfloat16 [1536, 1536], P(('dp', 'seq')), may hold values from -1.5 to 1.5
- gain_second: bfloat16 [1536], P(('dp', 'seq')), may hold values from 0.099609375 to 1.8984375
- gate_weight: bfloat16 [1536, 4096], P(('dp', 'seq')), may hold values from -0.15625 to 0.15625
- up_weight: bfloat16 [1536, 4096], P(('dp', 'seq')), may hold values from -0.15625 to 0.15625
- down_weight: bfloat16 [4096, 1536], P(('dp', 'seq')), may hold values from -0.09375 to 0.09375
Outputs:
- outputs: bfloat16 [4096, 1536], P(('dp', 'seq'))
- inputs_grad: bfloat16 [4096, 1536], P(('dp', 'seq'))
- first_grad: float32 [1536], P(('dp', 'seq'))
- query_grad: float32 [1536, 1536], P(('dp', 'seq'))
- key_grad: float32 [1536, 768], P(('dp', 'seq'))
- value_grad: float32 [1536, 768], P(('dp', 'seq'))
- output_grad: float32 [1536, 1536], P(('dp', 'seq'))
- second_grad: float32 [1536], P(('dp', 'seq'))
- gate_grad: float32 [1536, 4096], P(('dp', 'seq'))
- up_grad: float32 [1536, 4096], P(('dp', 'seq'))
- down_grad: float32 [4096, 1536], P(('dp', 'seq'))
The draws below stay inside these ranges and needn't reach their ends.
Inputs may be any that keep to these rules, and one draw needn't show every extreme that they name: `doc_ids`: within each sequence of 1024 rows the id is 0 at the first row and rises by 0 or 1 from one row to the next; all rows of the first sequence share one id, and every other sequence holds exactly 8 documents of ragged lengths. `positions`: A row's offset from the first row of its document (the rows of its sequence with its id).
All inputs are finite; a program needn't handle non-finite values.
Results may differ from the reference program's by a relative error of at most 0.025.
Values may be sent and summed in bfloat16 or wider, within the bound.
No kernel may reach another device: no remote copies, remote signals or barrier semaphores. Data moves between devices by JAX's collectives and lax.ppermute only.
A program may use at most 256 MiB of HBM per device.

```python
import math
import jax
import jax.numpy as jnp
from jax import lax

D = 1536
HEADS = 16
KV_HEADS = 8
HEAD = 96
FF = 4096
SEQS = 4
LENGTH = 1024
TOKENS = 4096


def layout(key):
    seeded = jax.random.fold_in(key, 11)
    seq_keys = jax.random.split(seeded, SEQS)
    shuffled = jax.vmap(lambda single: jax.random.permutation(single, LENGTH - 1))(seq_keys) + 1
    chosen = shuffled[:, :7].astype(jnp.int32)
    row_index = jnp.arange(LENGTH, dtype=jnp.int32)
    hit = jnp.any(row_index[None, None, :] == chosen[:, :, None], axis=1)
    later_seq = jnp.arange(SEQS, dtype=jnp.int32)[:, None] > 0
    starts = hit & later_seq | (row_index[None, :] == 0)
    starts_int = starts.astype(jnp.int32)
    documents = jnp.cumsum(starts_int, axis=1) - 1
    begins = lax.cummax(jnp.where(starts, row_index[None, :], 0), axis=1)
    within = row_index[None, :] - begins
    return (documents.reshape(-1).astype(jnp.int32), within.reshape(-1).astype(jnp.int32))


def draw_doc_ids(key, part):
    return layout(key)[0]


def draw_positions(key, part):
    return layout(key)[1]


def raised(drawn, own_key, source, target, shards_of, factor):
    def block_of(axis_at):
        return (jnp.arange(drawn.shape[axis_at]) // (drawn.shape[axis_at] // shards_of)).reshape((-1,) + (1,) * (drawn.ndim - 1 - axis_at))

    one_side = jax.random.permutation(own_key, shards_of)[block_of(target)]
    other_side = (block_of(target) + shards_of // 2) % shards_of
    return jnp.where((block_of(source) == one_side) | (block_of(source) == other_side), factor * drawn, drawn)


def steps_of(stream_key, extent, cuts, least, largest):
    def one(position, shards_of):
        heights = jax.random.uniform(jax.random.fold_in(jax.random.fold_in(stream_key, 6), position), (shards_of,), jnp.float32, least / len(cuts), largest / len(cuts))
        return jnp.repeat(jnp.exp(heights), extent[position] // shards_of).reshape((-1,) + (1,) * (len(extent) - position - 1))

    factor_of = one(*cuts[0])
    for cut in cuts[1:]:
        factor_of = factor_of * one(*cut)
    return factor_of


def normal_values(key, dims, width, reach, cuts=(), kind=jnp.bfloat16):
    drawn = jax.random.normal(key, dims, jnp.float32) * width
    if len(cuts) > 0:
        drawn = steps_of(key, dims, cuts, -0.22, 0.18) * drawn
    return jnp.clip(drawn, min=-reach, max=reach).astype(kind)


def gaussian_with(stream_key, dims, width, most, pieces, heavy, kind=jnp.bfloat16):
    values = width * jax.random.normal(stream_key, dims, jnp.float32)
    if pieces:
        values = values * steps_of(stream_key, dims, pieces, -0.22, 0.18)
    return jnp.clip(raised(values, jax.random.fold_in(stream_key, 3), *heavy), -most, most).astype(kind)


def setup_inputs(seed: int = 0) -> dict:
    streams_of = jax.random.split(jax.random.key(seed), 14)
    return {
        "inputs": gaussian_with(streams_of[0], (TOKENS, D), 1.0, 6.0, ((0, 32),), (0, 1, 32, 2.75)),
        "cotangent": normal_values(streams_of[1], (TOKENS, D), 1.0, 6.0, ((0, 32),)),
        "doc_ids": draw_doc_ids(jax.random.fold_in(streams_of[13], 71), 0),
        "positions": draw_positions(jax.random.fold_in(streams_of[13], 71), 0),
        "gain_first": jnp.clip(1.0 + 0.18 * jax.random.normal(streams_of[4], (D,), jnp.float32), 0.099609375, 1.8984375).astype(jnp.bfloat16),
        "query_weight": normal_values(streams_of[5], (D, D), (D // 2) ** -0.5, 0.21875, ((0, 32),)),
        "key_weight": normal_values(streams_of[6], (D, KV_HEADS * HEAD), D ** -0.5, 0.15625, ((0, 32),)),
        "value_weight": normal_values(streams_of[7], (D, KV_HEADS * HEAD), D ** -0.5, 0.15625, ((0, 32),)),
        "output_weight": normal_values(streams_of[8], (D, D), 16 ** -0.5, 1.5, ((0, 32),)),
        "gain_second": jnp.clip(1.0 + 0.18 * jax.random.normal(streams_of[9], (D,), jnp.float32), 0.099609375, 1.8984375).astype(jnp.bfloat16),
        "gate_weight": normal_values(streams_of[10], (D, FF), D ** -0.5, 0.15625, ((0, 32),)),
        "up_weight": normal_values(streams_of[11], (D, FF), D ** -0.5, 0.15625, ((0, 32),)),
        "down_weight": normal_values(streams_of[12], (FF, D), FF ** -0.5, 0.09375, ((0, 32),)),
    }


@jax.custom_vjp
def low(v):
    return lax.optimization_barrier(v.astype(jnp.bfloat16)).astype(jnp.float32)

@jax.custom_vjp
def low_back(v):
    return v

def low_keep(v):
    return (low(v), None)

def low_pass(kept, grad):
    return (grad,)

def back_keep(v):
    return (v, None)

def back_low(kept, grad):
    return (low(grad),)
low.defvjp(low_keep, low_pass)
low_back.defvjp(back_keep, back_low)
norm_epsilon = 1e-05
rotary_base = 100000.0
highest = lax.Precision.HIGHEST

def product(left, right):
    return jnp.dot(left, right, precision=highest)

def normalize(values_in, gain):
    return values_in * lax.rsqrt(lax.optimization_barrier(jnp.mean(values_in * values_in, axis=-1, keepdims=True)) + norm_epsilon) * gain

def rotate(matrix, positions, heads_count):
    halfway = HEAD // 2
    inverse_freq = rotary_base ** (-jnp.arange(halfway, dtype=jnp.float32) * 2.0 / HEAD)
    angles = positions.astype(jnp.float32)[:, None] * inverse_freq[None, :]
    cosine = jnp.cos(angles)[:, None, :]
    sine_table = jnp.sin(angles)[:, None, :]
    shaped = matrix.reshape(matrix.shape[0], heads_count, HEAD)
    first_half = shaped[..., :halfway]
    second_half = shaped[..., halfway:]
    turned = jnp.concatenate([first_half * cosine - second_half * sine_table, second_half * cosine + first_half * sine_table], axis=-1)
    return turned.reshape(matrix.shape)

def block_attention(query_block, keys_all, values_all, query_docs, key_docs, first_row):
    block_size = query_block.shape[0]
    logits = low_back(jnp.einsum('qgrd,kgd->grqk', query_block, keys_all, precision=highest))
    query_rows = first_row + jnp.arange(block_size, dtype=jnp.int32)
    key_rows = jnp.arange(keys_all.shape[0], dtype=jnp.int32)
    allowed = (key_rows[None, :] <= query_rows[:, None]) & (key_docs[None, :] == query_docs[:, None])
    scaled = jnp.where(allowed, logits * (1.0 / math.sqrt(HEAD)), -1e+30)
    weights_rounded = low(jax.nn.softmax(scaled, axis=-1))
    return jnp.einsum('grqk,kgd->qgrd', weights_rounded, values_all, precision=highest)
checked_attention = jax.checkpoint(block_attention)

def attention(queries, keys_rot, values_low, doc_ids):
    group_size = HEADS // KV_HEADS
    block_size = math.gcd(512, LENGTH)
    blocks = LENGTH // block_size
    query_seq = queries.reshape(SEQS, blocks, block_size, KV_HEADS, group_size, HEAD)
    key_seq = keys_rot.reshape(SEQS, LENGTH, KV_HEADS, HEAD)
    value_seq = values_low.reshape(SEQS, LENGTH, KV_HEADS, HEAD)
    doc_seq = doc_ids.reshape(SEQS, LENGTH)
    first_rows = jnp.arange(blocks, dtype=jnp.int32) * block_size

    def one_sequence(members):
        seq_queries, seq_keys, seq_values, seq_docs = members
        doc_blocks = seq_docs.reshape(blocks, block_size)

        def one_block(block_members):
            return checked_attention(block_members[0], seq_keys, seq_values, block_members[1], seq_docs, block_members[2])
        return lax.map(one_block, (seq_queries, doc_blocks, first_rows))
    mixed = lax.map(one_sequence, (query_seq, key_seq, value_seq, doc_seq))
    return mixed.reshape(queries.shape[0], HEADS * HEAD)

def reference(inputs, cotangent, doc_ids, positions, gain_first, query_weight, key_weight, value_weight, output_weight, gain_second, gate_weight, up_weight, down_weight):

    def forward(x_float, gain_one, w_query, w_key, w_value, w_output, gain_two, w_gate, w_up, w_down):
        normed = low(normalize(x_float, gain_one))
        queries = low(rotate(low_back(product(normed, w_query)), positions, HEADS))
        keys_rot = low(rotate(low_back(product(normed, w_key)), positions, KV_HEADS))
        values_low = low(low_back(product(normed, w_value)))
        mixed = low(low_back(attention(queries, keys_rot, values_low, doc_ids)))
        middle = x_float + low_back(product(mixed, w_output))
        normed_two = low(normalize(middle, gain_two))
        gate = low_back(product(normed_two, w_gate))
        upward = low_back(product(normed_two, w_up))
        hidden = low(jax.nn.silu(gate) * upward)
        return middle + low_back(product(hidden, w_down))
    f32 = jnp.float32
    result, pullback = jax.vjp(forward, inputs.astype(f32), gain_first.astype(f32), query_weight.astype(f32), key_weight.astype(f32), value_weight.astype(f32), output_weight.astype(f32), gain_second.astype(f32), gate_weight.astype(f32), up_weight.astype(f32), down_weight.astype(f32))
    grads = pullback(cotangent.astype(f32))
    return (result.astype(jnp.bfloat16), grads[0].astype(jnp.bfloat16), grads[1], grads[2], grads[3], grads[4], grads[5], grads[6], grads[7], grads[8], grads[9])
```

```python
import math

import jax
import jax.numpy as jnp
from jax import lax
from jax.experimental import pallas as pl
from jax.experimental.pallas import tpu as pltpu
from jax.sharding import PartitionSpec as P

D = 1536
HEADS = 16
KV_HEADS = 8
HEAD = 96


norm_epsilon = 1e-05
rotary_base = 100000.0


def normalize(values_in, gain):
    return (
        values_in
        * lax.rsqrt(jnp.mean(values_in * values_in, axis=-1, keepdims=True) + norm_epsilon)
        * gain
    )


def swish_product(gate, upward):
    return jax.nn.silu(gate) * upward


def rotate(matrix, positions, heads_count, direction):
    halfway = HEAD // 2
    inverse_freq = rotary_base ** (-jnp.arange(halfway, dtype=jnp.float32) * 2.0 / HEAD)
    angles = positions.astype(jnp.float32)[:, None] * inverse_freq[None, :]
    cosine = jnp.cos(angles)[:, None, :]
    sine_table = direction * jnp.sin(angles)[:, None, :]
    shaped = matrix.reshape(matrix.shape[0], heads_count, HEAD)
    first_half = shaped[..., :halfway]
    second_half = shaped[..., halfway:]
    turned = jnp.concatenate(
        [
            first_half * cosine - second_half * sine_table,
            second_half * cosine + first_half * sine_table,
        ],
        axis=-1,
    )
    return turned.reshape(matrix.shape)


def times_transposed(left, right):
    return lax.dot_general(
        left, right, (((1,), (1,)), ((), ())), preferred_element_type=jnp.float32
    )


def transposed_times(left, right):
    return lax.dot_general(
        left, right, (((0,), (0,)), ((), ())), preferred_element_type=jnp.float32
    )


def matrix_product(left, right):
    return jnp.dot(left, right, preferred_element_type=jnp.float32)


def block_rows(total_rows):
    size_rows = min(total_rows, 1024)
    while total_rows % size_rows:
        size_rows -= 1
    return size_rows


def fold_local(block_step, initial, arrays):
    total_rows = arrays[0].shape[0]
    size_rows = block_rows(total_rows)

    def one_turn(turn_index, state_in):
        begin_row = turn_index * size_rows
        pieces = tuple(
            (lax.dynamic_slice_in_dim(member, begin_row, size_rows, 0) for member in arrays)
        )
        return block_step(state_in, pieces, begin_row)

    return lax.fori_loop(0, total_rows // size_rows, one_turn, initial)


def piece_fold(block_step, state_in, pieces):
    return fold_local(block_step, state_in, pieces)


def keep_state(state_now):
    return state_now


def body(
    inputs,
    cotangent,
    doc_ids,
    positions,
    gain_first,
    query_weight,
    key_weight,
    value_weight,
    output_weight,
    gain_second,
    gate_weight,
    up_weight,
    down_weight,
):
    f32 = jnp.float32
    bf16 = jnp.bfloat16
    attend_set = (
        lax.all_gather(gain_first, ("dp", "seq"), axis=0, tiled=True),
        lax.all_gather(query_weight, ("dp", "seq"), axis=0, tiled=True),
        lax.all_gather(key_weight, ("dp", "seq"), axis=0, tiled=True),
        lax.all_gather(value_weight, ("dp", "seq"), axis=0, tiled=True),
        lax.all_gather(output_weight, ("dp", "seq"), axis=0, tiled=True),
    )
    feed_set = (
        lax.all_gather(gain_second, ("dp", "seq"), axis=0, tiled=True),
        lax.all_gather(gate_weight, ("dp", "seq"), axis=0, tiled=True),
        lax.all_gather(up_weight, ("dp", "seq"), axis=0, tiled=True),
        lax.all_gather(down_weight, ("dp", "seq"), axis=0, tiled=True),
    )
    gain_one, w_query, w_key, w_value, w_output = attend_set
    gain_two, w_gate, w_up, w_down = feed_set
    row_count = inputs.shape[0]
    group_size = HEADS // KV_HEADS
    kv_width = KV_HEADS * HEAD
    score_scale = 1.0 / math.sqrt(HEAD)
    query_rows = lax.axis_index("seq") * row_count + jnp.arange(row_count, dtype=jnp.int32)
    x_float = inputs.astype(f32)
    gain_one_float = gain_one.astype(f32)
    normed = normalize(x_float, gain_one_float).astype(bf16)
    query_rot = rotate(matrix_product(normed, w_query), positions, HEADS, 1.0).astype(bf16)
    key_rot = rotate(matrix_product(normed, w_key), positions, KV_HEADS, 1.0).astype(bf16)
    value_low = matrix_product(normed, w_value).astype(bf16)
    query_four = query_rot.reshape(row_count, KV_HEADS, group_size, HEAD)

    def mask_for(docs_part, first_key, piece_rows):
        key_rows = first_key + jnp.arange(piece_rows, dtype=jnp.int32)
        return (key_rows[None, :] <= query_rows[:, None]) & (docs_part[None, :] == doc_ids[:, None])

    def forward_step(state_in, pieces, first_key):
        keys_part, values_part, docs_part = pieces
        piece_rows = keys_part.shape[0]
        allowed = mask_for(docs_part, first_key, piece_rows)

        def forward_compute(state_now):
            accumulated, running, totals = state_now
            logits = (
                jnp.einsum(
                    "qgrd,kgd->grqk",
                    query_four,
                    keys_part.reshape(piece_rows, KV_HEADS, HEAD),
                    preferred_element_type=f32,
                )
                * score_scale
            )
            logits = jnp.where(allowed, logits, -1e30)
            new_max = jnp.maximum(running, jnp.max(logits, axis=-1))
            weights_block = jnp.where(allowed, jnp.exp(logits - new_max[..., None]), 0.0)
            factor = jnp.exp(running - new_max)
            totals = totals * factor + jnp.sum(weights_block, axis=-1)
            update = jnp.einsum(
                "grqk,kgd->qgrd",
                weights_block.astype(bf16),
                values_part.reshape(piece_rows, KV_HEADS, HEAD),
                preferred_element_type=f32,
            )
            accumulated = accumulated * jnp.transpose(factor, (2, 0, 1))[..., None] + update
            return (accumulated, new_max, totals)

        return lax.cond(jnp.any(allowed), forward_compute, keep_state, state_in)

    forward_init = (
        jnp.zeros((row_count, KV_HEADS, group_size, HEAD), f32),
        jnp.full((KV_HEADS, group_size, row_count), -1e30, f32),
        jnp.zeros((KV_HEADS, group_size, row_count), f32),
    )
    forward_state = piece_fold(
        forward_step,
        forward_init,
        (
            lax.all_gather(key_rot, "seq", axis=0, tiled=True),
            lax.all_gather(value_low, "seq", axis=0, tiled=True),
            lax.all_gather(doc_ids, "seq", axis=0, tiled=True),
        ),
    )
    accumulated, running, totals = forward_state
    attend_float = accumulated / jnp.transpose(totals, (2, 0, 1))[..., None]
    log_totals = running + jnp.log(totals)
    mixed = attend_float.reshape(row_count, D).astype(bf16)
    middle = x_float + matrix_product(mixed, w_output)
    gain_two_float = gain_two.astype(f32)
    normed_two = normalize(middle, gain_two_float).astype(bf16)
    gate = matrix_product(normed_two, w_gate)
    upward = matrix_product(normed_two, w_up)
    hidden = swish_product(gate, upward).astype(bf16)
    outputs = (middle + matrix_product(hidden, w_down)).astype(bf16)
    feed_back = (
        lax.all_gather(gain_second, ("dp", "seq"), axis=0, tiled=True),
        lax.all_gather(gate_weight, ("dp", "seq"), axis=0, tiled=True),
        lax.all_gather(up_weight, ("dp", "seq"), axis=0, tiled=True),
        lax.all_gather(down_weight, ("dp", "seq"), axis=0, tiled=True),
    )
    attend_back = (
        lax.all_gather(gain_first, ("dp", "seq"), axis=0, tiled=True),
        lax.all_gather(query_weight, ("dp", "seq"), axis=0, tiled=True),
        lax.all_gather(key_weight, ("dp", "seq"), axis=0, tiled=True),
        lax.all_gather(value_weight, ("dp", "seq"), axis=0, tiled=True),
        lax.all_gather(output_weight, ("dp", "seq"), axis=0, tiled=True),
    )
    unused_gain_two, back_gate, back_up, back_down = feed_back
    unused_gain_one, back_query, back_key, back_value, back_output = attend_back
    cot_float = cotangent.astype(f32)
    cot_low = cot_float.astype(bf16)
    down_term = transposed_times(hidden, cot_low)
    grad_hidden = times_transposed(cot_low, back_down)
    unused_swish, swish_back = jax.vjp(swish_product, gate, upward)
    grad_gate, grad_up = swish_back(grad_hidden)
    grad_gate_low = grad_gate.astype(bf16)
    grad_up_low = grad_up.astype(bf16)
    gate_term = transposed_times(normed_two, grad_gate_low)
    up_term = transposed_times(normed_two, grad_up_low)
    grad_normed_two = times_transposed(grad_gate_low, back_gate) + times_transposed(
        grad_up_low, back_up
    )
    unused_norm_two, norm_two_back = jax.vjp(normalize, middle, gain_two_float)
    grad_middle_part, gain_two_term = norm_two_back(grad_normed_two)
    second_grad, gate_grad, up_grad, down_grad = (
        lax.psum_scatter(gain_two_term, ("dp", "seq"), scatter_dimension=0, tiled=True),
        lax.psum_scatter(gate_term, ("dp", "seq"), scatter_dimension=0, tiled=True),
        lax.psum_scatter(up_term, ("dp", "seq"), scatter_dimension=0, tiled=True),
        lax.psum_scatter(down_term, ("dp", "seq"), scatter_dimension=0, tiled=True),
    )
    grad_middle = cot_float + grad_middle_part
    middle_low = grad_middle.astype(bf16)
    output_term = transposed_times(mixed, middle_low)
    grad_mixed = times_transposed(middle_low, back_output).astype(bf16)
    dout_four = grad_mixed.reshape(row_count, KV_HEADS, group_size, HEAD)
    delta_rows = jnp.einsum("qgrd,qgrd->grq", dout_four.astype(f32), attend_float)

    def query_grad_block(allowed, keys_three, values_three):
        logits = (
            jnp.einsum("qgrd,kgd->grqk", query_four, keys_three, preferred_element_type=f32)
            * score_scale
        )
        logits = jnp.where(allowed, logits, -1e30)
        weights_block = jnp.where(allowed, jnp.exp(logits - log_totals[..., None]), 0.0)
        grad_weights = jnp.einsum(
            "qgrd,kgd->grqk", dout_four, values_three, preferred_element_type=f32
        )
        grad_logits = (weights_block * (grad_weights - delta_rows[..., None]) * score_scale).astype(
            bf16
        )
        return (weights_block, grad_logits)

    def query_step(state_in, pieces, first_key):
        keys_part, values_part, docs_part = pieces
        piece_rows = keys_part.shape[0]
        allowed = mask_for(docs_part, first_key, piece_rows)

        def query_compute(grad_query):
            keys_three = keys_part.reshape(piece_rows, KV_HEADS, HEAD)
            values_three = values_part.reshape(piece_rows, KV_HEADS, HEAD)
            unused_weights, grad_logits = query_grad_block(allowed, keys_three, values_three)
            return grad_query + jnp.einsum(
                "grqk,kgd->qgrd", grad_logits, keys_three, preferred_element_type=f32
            )

        return lax.cond(jnp.any(allowed), query_compute, keep_state, state_in)

    grad_query_rot = piece_fold(
        query_step,
        jnp.zeros((row_count, KV_HEADS, group_size, HEAD), f32),
        (
            lax.all_gather(key_rot, "seq", axis=0, tiled=True),
            lax.all_gather(value_low, "seq", axis=0, tiled=True),
            lax.all_gather(doc_ids, "seq", axis=0, tiled=True),
        ),
    )
    lse_rows = jnp.transpose(log_totals, (2, 0, 1)).reshape(row_count, HEADS)
    delta_flat = jnp.transpose(delta_rows, (2, 0, 1)).reshape(row_count, HEADS)
    lse_all, delta_all = (
        lax.all_gather(lse_rows, "seq", axis=0, tiled=True),
        lax.all_gather(delta_flat, "seq", axis=0, tiled=True),
    )
    keys_mine = key_rot.reshape(row_count, KV_HEADS, HEAD)
    values_mine = value_low.reshape(row_count, KV_HEADS, HEAD)

    def key_step(state_in, pieces, first_query):
        queries_part, dout_part, docs_part = pieces
        piece_rows = queries_part.shape[0]
        other_rows = first_query + jnp.arange(piece_rows, dtype=jnp.int32)
        allowed = (query_rows[None, :] <= other_rows[:, None]) & (
            doc_ids[None, :] == docs_part[:, None]
        )

        def key_compute(state_now):
            grad_keys, grad_values = state_now
            lse_part = lax.dynamic_slice_in_dim(lse_all, first_query, piece_rows, 0)
            delta_part = lax.dynamic_slice_in_dim(delta_all, first_query, piece_rows, 0)
            lse_three = jnp.transpose(lse_part.reshape(piece_rows, KV_HEADS, group_size), (1, 2, 0))
            delta_three = jnp.transpose(
                delta_part.reshape(piece_rows, KV_HEADS, group_size), (1, 2, 0)
            )
            queries_four = queries_part.reshape(piece_rows, KV_HEADS, group_size, HEAD)
            douts_four = dout_part.reshape(piece_rows, KV_HEADS, group_size, HEAD)
            logits = (
                jnp.einsum("qgrd,kgd->grqk", queries_four, keys_mine, preferred_element_type=f32)
                * score_scale
            )
            logits = jnp.where(allowed, logits, -1e30)
            weights_block = jnp.where(allowed, jnp.exp(logits - lse_three[..., None]), 0.0)
            grad_weights = jnp.einsum(
                "qgrd,kgd->grqk", douts_four, values_mine, preferred_element_type=f32
            )
            grad_logits = (
                weights_block * (grad_weights - delta_three[..., None]) * score_scale
            ).astype(bf16)
            grad_keys = grad_keys + jnp.einsum(
                "grqk,qgrd->kgd", grad_logits, queries_four, preferred_element_type=f32
            )
            grad_values = grad_values + jnp.einsum(
                "grqk,qgrd->kgd", weights_block.astype(bf16), douts_four, preferred_element_type=f32
            )
            return (grad_keys, grad_values)

        return lax.cond(jnp.any(allowed), key_compute, keep_state, state_in)

    key_init = (
        jnp.zeros((row_count, KV_HEADS, HEAD), f32),
        jnp.zeros((row_count, KV_HEADS, HEAD), f32),
    )
    grad_keys_three, grad_values_three = piece_fold(
        key_step,
        key_init,
        (
            lax.all_gather(query_rot, "seq", axis=0, tiled=True),
            lax.all_gather(grad_mixed, "seq", axis=0, tiled=True),
            lax.all_gather(doc_ids, "seq", axis=0, tiled=True),
        ),
    )
    grad_keys_mine = grad_keys_three.reshape(row_count, kv_width)
    grad_values_mine = grad_values_three.reshape(row_count, kv_width)
    grad_query_low = rotate(grad_query_rot.reshape(row_count, D), positions, HEADS, -1.0).astype(
        bf16
    )
    grad_key_low = rotate(grad_keys_mine, positions, KV_HEADS, -1.0).astype(bf16)
    grad_value_low = grad_values_mine.astype(bf16)
    query_term = transposed_times(normed, grad_query_low)
    key_term_all = transposed_times(normed, grad_key_low)
    value_term_all = transposed_times(normed, grad_value_low)
    grad_normed = (
        times_transposed(grad_query_low, back_query)
        + times_transposed(grad_key_low, back_key)
        + times_transposed(grad_value_low, back_value)
    )
    unused_norm_one, norm_one_back = jax.vjp(normalize, x_float, gain_one_float)
    grad_input_part, gain_one_term = norm_one_back(grad_normed)
    inputs_grad = (grad_middle + grad_input_part).astype(bf16)
    first_grad, query_grad, key_grad, value_grad, output_grad = (
        lax.psum_scatter(gain_one_term, ("dp", "seq"), scatter_dimension=0, tiled=True),
        lax.psum_scatter(query_term, ("dp", "seq"), scatter_dimension=0, tiled=True),
        lax.psum_scatter(key_term_all, ("dp", "seq"), scatter_dimension=0, tiled=True),
        lax.psum_scatter(value_term_all, ("dp", "seq"), scatter_dimension=0, tiled=True),
        lax.psum_scatter(output_term, ("dp", "seq"), scatter_dimension=0, tiled=True),
    )
    return (
        outputs,
        inputs_grad,
        first_grad,
        query_grad,
        key_grad,
        value_grad,
        output_grad,
        second_grad,
        gate_grad,
        up_grad,
        down_grad,
    )

BOTH = ("dp", "seq")
BIT_Y, BIT_X, BIT_ZH, BIT_ZL, BIT_C = 16, 8, 4, 2, 1
PAIR = 2
LANES = 128
QUERY_COLS = PAIR * HEAD
HEAD_COLS = QUERY_COLS + 2 * HEAD
PAD_COLS = (PAIR + 2) * LANES
BLOCK = 256
f32 = jnp.float32
bf16 = jnp.bfloat16
VMEM_BYTES = 60 * 1024 * 1024


def swap(value, bit):
    return lax.ppermute(value, BOTH, [(i, i ^ bit) for i in range(32)])


def my_bit(bit):
    flat = lax.axis_index("dp") * 8 + lax.axis_index("seq")
    return (flat // bit) % 2


def pick(value, index, axis):
    return lax.dynamic_index_in_dim(value, index, axis, keepdims=False)


def paired(mine, other, bit, axis):
    low_first = my_bit(bit) == 0
    return jnp.stack(
        [jnp.where(low_first, mine, other), jnp.where(low_first, other, mine)], axis
    )


def gather_bit(value, bit, axis):
    return paired(value, swap(value, bit), bit, axis)


def trade_bit(value, bit, axis):
    mine = my_bit(bit)
    keep = pick(value, mine, axis)
    other = swap(pick(value, 1 - mine, axis), bit)
    return paired(keep, other, bit, axis)


def reduce_bit(value, bit, axis):
    mine = my_bit(bit)
    keep = pick(value, mine, axis)
    other = swap(pick(value, 1 - mine, axis).astype(bf16), bit)
    return keep.astype(f32) + other.astype(f32)


def gather_square(value):
    half = value.shape[0] // 2
    from_x = swap(value, BIT_X)
    from_z = swap(value, BIT_ZL)
    far_low = swap(from_z[:half], BIT_X)
    far_high = swap(from_x[half:], BIT_ZL)
    chip = jnp.concatenate([value, from_x, from_z, far_low, far_high])
    return jnp.concatenate([chip, swap(chip, BIT_C)])


def scatter_square(parts):
    rows = parts.shape[0] // 8
    half = rows // 2
    mine = parts[: 4 * rows].astype(f32) + swap(parts[4 * rows :], BIT_C).astype(f32)
    own, to_x, to_z, far = (mine[i * rows : (i + 1) * rows] for i in range(4))
    far = far.astype(bf16)
    in_z = swap(far[:half], BIT_X).astype(f32)
    in_x = swap(far[half:], BIT_ZL).astype(f32)
    to_z = jnp.concatenate([to_z[:half] + in_z, to_z[half:]]).astype(bf16)
    to_x = jnp.concatenate([to_x[:half], to_x[half:] + in_x]).astype(bf16)
    return own + swap(to_x, BIT_X).astype(f32) + swap(to_z, BIT_ZL).astype(f32)


def across(value):
    pairs = []
    for i in range(32):
        y, x, zh, zl, c = (i >> 4) & 1, (i >> 3) & 1, (i >> 2) & 1, (i >> 1) & 1, i & 1
        pairs.append((i, c * 16 + zl * 8 + zh * 4 + x * 2 + y))
    return lax.ppermute(value, BOTH, pairs)


def gather_rows(value):
    return lax.all_gather(value, "seq", axis=0, tiled=True)


def scatter_rows(value):
    return lax.psum_scatter(value, "seq", scatter_dimension=0, tiled=True)


GROUP_OF = [((s & 1) << 2) | (s & 2) | (s >> 2) for s in range(8)]


def dot_nn(left, right):
    return jnp.dot(left, right, preferred_element_type=f32)


def dot_nt(left, right):
    return lax.dot_general(left, right, (((1,), (1,)), ((), ())), preferred_element_type=f32)


def dot_tn(left, right):
    return lax.dot_general(left, right, (((0,), (0,)), ((), ())), preferred_element_type=f32)


def whole(*shape):
    return pl.BlockSpec(shape, lambda i: (0,) * len(shape), pipeline_mode=pl.Buffered(1))


def rows_of(rows, cols):
    return pl.BlockSpec((rows, cols), lambda i: (i, 0))


def turn(matrix, cosine, sine):
    return matrix * cosine + pltpu.roll(matrix, LANES // 2, 1) * sine


def project_kernel(x_ref, w_ref, freq_ref, hn_ref, q_ref, k_ref, v_ref, cos_ref, sin_ref):
    x = x_ref[:, :D].astype(f32)
    scale = lax.rsqrt(jnp.mean(x * x, axis=-1, keepdims=True) + norm_epsilon)
    normed = (x * scale).astype(bf16)
    hn_ref[...] = normed
    extra = x_ref[:, D:].astype(f32)
    place = extra[:, 1:2] * 128.0 + extra[:, 2:3]
    angles = place * freq_ref[...]
    lane = lax.broadcasted_iota(jnp.int32, angles.shape, 1)
    cosine = jnp.cos(angles)
    sine = jnp.where(lane < LANES // 2, -jnp.sin(angles), jnp.sin(angles))
    cos_ref[...] = cosine
    sin_ref[...] = sine
    full = dot_nn(normed, w_ref[...])
    for h in range(PAIR):
        part = full[:, h * LANES : (h + 1) * LANES]
        q_ref[:, h * LANES : (h + 1) * LANES] = turn(part, cosine, sine).astype(bf16)
    k_ref[...] = turn(full[:, PAIR * LANES : (PAIR + 1) * LANES], cosine, sine).astype(bf16)
    v_ref[...] = full[:, (PAIR + 1) * LANES :].astype(bf16)


def project(rows_all, weights):
    total, width = rows_all.shape
    lane = jnp.arange(LANES) % (LANES // 2)
    freq = rotary_base ** (-lane.astype(f32) * 2.0 / HEAD)
    freq = jnp.where(lane < HEAD // 2, freq, 0.0).reshape(1, LANES)
    shapes = [(D, bf16), (PAIR * LANES, bf16), (LANES, bf16), (LANES, bf16), (LANES, f32), (LANES, f32)]
    return pl.pallas_call(
        project_kernel,
        grid=(total // BLOCK,),
        in_specs=[rows_of(BLOCK, width), whole(D, PAD_COLS), whole(1, LANES)],
        out_specs=[rows_of(BLOCK, n) for n, t in shapes],
        out_shape=[jax.ShapeDtypeStruct((total, n), t) for n, t in shapes],
        compiler_params=pltpu.CompilerParams(vmem_limit_bytes=VMEM_BYTES),
        name="project",
    )(rows_all, weights, freq)


def allowed_pairs(dcol_ref, drow_ref, first, keys):
    shape = (BLOCK, keys)
    query_at = first + lax.broadcasted_iota(jnp.int32, shape, 0)
    key_at = lax.broadcasted_iota(jnp.int32, shape, 1)
    return (key_at <= query_at) & (dcol_ref[...] == drow_ref[:, :keys])


def attend_kernel(q_ref, k_ref, v_ref, dcol_ref, drow_ref, w_ref, a_ref, lse_ref, o_ref):
    blocks = k_ref.shape[0] // BLOCK

    def run(b):
        keys = (b + 1) * BLOCK
        allowed = allowed_pairs(dcol_ref, drow_ref, b * BLOCK, keys)
        for h in range(PAIR):
            cols = slice(h * LANES, (h + 1) * LANES)
            logits = dot_nt(q_ref[:, cols], k_ref[:keys, :]) * (1.0 / math.sqrt(HEAD))
            logits = jnp.where(allowed, logits, -1e30)
            top = jnp.max(logits, axis=-1, keepdims=True)
            weights = jnp.exp(logits - top)
            total = jnp.sum(weights, axis=-1, keepdims=True)
            mixed = dot_nn(weights.astype(bf16), v_ref[:keys, :]) / total
            a_ref[:, cols] = mixed.astype(bf16)
            lse_ref[:, h : h + 1] = top + jnp.log(total)

    for b in range(blocks):
        pl.when(pl.program_id(0) == b)(lambda b=b: run(b))
    o_ref[...] = dot_nn(a_ref[...], w_ref[...]).astype(bf16)


def attend(query, key, value, docs_col, docs_row, weights):
    total = query.shape[0]
    shapes = [(PAIR * LANES, bf16), (PAIR, f32), (D, bf16)]
    return pl.pallas_call(
        attend_kernel,
        grid=(total // BLOCK,),
        in_specs=[
            rows_of(BLOCK, PAIR * LANES),
            whole(total, LANES),
            whole(total, LANES),
            rows_of(BLOCK, 1),
            whole(1, total),
            whole(PAIR * LANES, D),
        ],
        out_specs=[rows_of(BLOCK, n) for n, t in shapes],
        out_shape=[jax.ShapeDtypeStruct((total, n), t) for n, t in shapes],
        compiler_params=pltpu.CompilerParams(vmem_limit_bytes=VMEM_BYTES),
        name="attend",
    )(query, key, value, docs_col, docs_row, weights)


def attend_back_kernel(
    mb_ref, w_ref, q_ref, k_ref, v_ref, a_ref, lse_ref, dcol_ref, drow_ref, cos_ref, sin_ref,
    dq_ref, dkv_ref, dk_acc, dv_acc, dq_acc
):
    step = pl.program_id(0)
    blocks = k_ref.shape[0] // BLOCK

    @pl.when(step == 0)
    def _():
        dk_acc[...] = jnp.zeros_like(dk_acc)
        dv_acc[...] = jnp.zeros_like(dv_acc)

    grad_mixed = dot_nt(mb_ref[...], w_ref[...]).astype(bf16)
    scale = 1.0 / math.sqrt(HEAD)

    def run(b):
        keys = (b + 1) * BLOCK
        allowed = allowed_pairs(dcol_ref, drow_ref, b * BLOCK, keys)
        for h in range(PAIR):
            cols = slice(h * LANES, (h + 1) * LANES)
            query = q_ref[:, cols]
            grad = grad_mixed[:, cols]
            delta = jnp.sum(
                grad.astype(f32) * a_ref[:, cols].astype(f32), axis=-1, keepdims=True
            )
            logits = dot_nt(query, k_ref[:keys, :]) * scale
            logits = jnp.where(allowed, logits, -1e30)
            weights = jnp.exp(logits - lse_ref[:, h : h + 1])
            grad_weights = dot_nt(grad, v_ref[:keys, :])
            grad_logits = (weights * (grad_weights - delta) * scale).astype(bf16)
            dq_acc[:, cols] = dot_nn(grad_logits, k_ref[:keys, :])
            dk_acc[:keys, :] += dot_tn(grad_logits, query)
            dv_acc[:keys, :] += dot_tn(weights.astype(bf16), grad)

    for b in range(blocks):
        pl.when(step == b)(lambda b=b: run(b))

    rows = pl.ds(pl.multiple_of(step * BLOCK, BLOCK), BLOCK)
    for h in range(PAIR):
        cols = slice(h * LANES, (h + 1) * LANES)
        dq_ref[:, cols] = turn(dq_acc[:, cols], cos_ref[rows, :], -sin_ref[rows, :]).astype(bf16)

    @pl.when(step == blocks - 1)
    def _():
        dkv_ref[:, :LANES] = turn(dk_acc[...], cos_ref[...], -sin_ref[...]).astype(bf16)
        dkv_ref[:, LANES:] = dv_acc[...].astype(bf16)


def attend_back(mb, weights, query, key, value, mixed, lse, docs_col, docs_row, cosine, sine):
    total = query.shape[0]
    return pl.pallas_call(
        attend_back_kernel,
        grid=(total // BLOCK,),
        in_specs=[
            rows_of(BLOCK, D),
            whole(PAIR * LANES, D),
            rows_of(BLOCK, PAIR * LANES),
            whole(total, LANES),
            whole(total, LANES),
            rows_of(BLOCK, PAIR * LANES),
            rows_of(BLOCK, PAIR),
            rows_of(BLOCK, 1),
            whole(1, total),
            whole(total, LANES),
            whole(total, LANES),
        ],
        out_specs=[rows_of(BLOCK, PAIR * LANES), whole(total, 2 * LANES)],
        out_shape=[
            jax.ShapeDtypeStruct((total, PAIR * LANES), bf16),
            jax.ShapeDtypeStruct((total, 2 * LANES), bf16),
        ],
        scratch_shapes=[
            pltpu.VMEM((total, LANES), f32),
            pltpu.VMEM((total, LANES), f32),
            pltpu.VMEM((BLOCK, PAIR * LANES), f32),
        ],
        compiler_params=pltpu.CompilerParams(vmem_limit_bytes=VMEM_BYTES),
        name="attend_back",
    )(mb, weights, query, key, value, mixed, lse, docs_col, docs_row, cosine, sine)


def feed_kernel(hn_ref, cb_ref, wgu_ref, wd_ref, f_ref, dgu_ref, o_ref, e_ref):
    hidden = wd_ref.shape[0]
    both = dot_nn(hn_ref[...], wgu_ref[...])
    gate, up = both[:, :hidden], both[:, hidden:]
    sig = 1.0 / (1.0 + jnp.exp(-gate))
    swish = gate * sig
    inner = (swish * up).astype(bf16)
    f_ref[...] = inner
    o_ref[...] = dot_nn(inner, wd_ref[...]).astype(bf16)
    grad = dot_nt(cb_ref[...], wd_ref[...])
    dgu_ref[:, :hidden] = (grad * up * sig * (1.0 + gate * (1.0 - sig))).astype(bf16)
    dgu_ref[:, hidden:] = (grad * swish).astype(bf16)
    e_ref[...] = dot_nt(dgu_ref[...], wgu_ref[...]).astype(bf16)


def feed(normed, cot, w_both, w_down):
    total, hidden = normed.shape[0], w_down.shape[0]
    shapes = [(hidden, bf16), (2 * hidden, bf16), (D, bf16), (D, bf16)]
    return pl.pallas_call(
        feed_kernel,
        grid=(total // BLOCK,),
        in_specs=[rows_of(BLOCK, D), rows_of(BLOCK, D), whole(D, 2 * hidden), whole(hidden, D)],
        out_specs=[rows_of(BLOCK, n) for n, t in shapes],
        out_shape=[jax.ShapeDtypeStruct((total, n), t) for n, t in shapes],
        compiler_params=pltpu.CompilerParams(vmem_limit_bytes=VMEM_BYTES),
        name="feed",
    )(normed, cot, w_both, w_down)


def inverse_norm(values):
    return lax.rsqrt(jnp.mean(values * values, axis=-1, keepdims=True) + norm_epsilon)


def norm_back(values, inverse, grad):
    return inverse * grad - values * inverse**3 * jnp.mean(grad * values, axis=-1, keepdims=True)


def pad_heads(matrix):
    rows, cols = matrix.shape
    split = matrix.reshape(rows, cols // (HEAD // 2), HEAD // 2)
    return jnp.pad(split, ((0, 0), (0, 0), (0, LANES // 2 - HEAD // 2))).reshape(rows, -1)


def cut_heads(matrix):
    rows, cols = matrix.shape
    split = matrix.reshape(rows, cols // (LANES // 2), LANES // 2)
    return split[..., : HEAD // 2].reshape(rows, -1)


def body_fast(
    inputs,
    cotangent,
    doc_ids,
    positions,
    gain_first,
    query_weight,
    key_weight,
    value_weight,
    output_weight,
    gain_second,
    gate_weight,
    up_weight,
    down_weight,
):
    rows = inputs.shape[0]
    own = query_weight.shape[0]
    hidden_block = down_weight.shape[0]
    gain_one = gain_first.astype(f32)[:, None]
    gain_two = gain_second.astype(f32)[:, None]

    marks = jnp.stack([doc_ids, positions // 128, positions % 128], axis=1).astype(bf16)
    marks = jnp.pad(marks, ((0, 0), (0, LANES - 3)))
    rows_all = gather_rows(jnp.concatenate([inputs, marks], axis=1))
    docs = rows_all[:, D].astype(f32)
    docs_col, docs_row = docs[:, None], docs[None, :]

    parts = jnp.concatenate(
        [
            (query_weight.astype(f32) * gain_one).astype(bf16).reshape(own, KV_HEADS, QUERY_COLS),
            (key_weight.astype(f32) * gain_one).astype(bf16).reshape(own, KV_HEADS, HEAD),
            (value_weight.astype(f32) * gain_one).astype(bf16).reshape(own, KV_HEADS, HEAD),
        ],
        axis=-1,
    )
    parts = jnp.stack([parts[:, g] for g in GROUP_OF])
    parts = lax.all_to_all(parts, "seq", 0, 0, tiled=True)
    w_heads = lax.all_gather(parts, "dp", axis=0, tiled=True).reshape(D, HEAD_COLS)
    w_heads = pad_heads(w_heads)

    block = gather_bit(gather_bit(output_weight, BIT_C, 0), BIT_ZL, 0)
    w_out = across(block.reshape(PAIR, 2, HEAD // 2, D))
    w_out = jnp.pad(w_out, ((0, 0), (0, 0), (0, LANES // 2 - HEAD // 2), (0, 0)))
    w_out = w_out.reshape(PAIR * LANES, D)

    both = jnp.stack(
        [
            (gate_weight.astype(f32) * gain_two).astype(bf16),
            (up_weight.astype(f32) * gain_two).astype(bf16),
        ]
    ).reshape(2, own, 2, 2, 2, 2, 2, hidden_block)
    both = both.transpose(3, 5, 6, 1, 0, 2, 4, 7)
    for axis, bit in ((2, BIT_C), (0, BIT_X), (1, BIT_ZL)):
        both = trade_bit(both, bit, axis)
    both = both.reshape(2, 4 * own, 8 * hidden_block)
    both = gather_bit(both, BIT_ZH, 1)
    both = gather_bit(both, BIT_Y, 0)
    w_both = both.reshape(D, 8 * hidden_block)
    w_down = gather_bit(gather_bit(down_weight, BIT_ZH, 0), BIT_Y, 0).reshape(4 * hidden_block, D)

    cot_all = gather_square(cotangent)

    normed, query, key, value, cosine, sine = project(rows_all, w_heads)
    mixed, lse, term = attend(query, key, value, docs_col, docs_row, w_out)
    x_float = inputs.astype(f32)
    middle = x_float + scatter_rows(term).astype(f32)

    inverse_two = inverse_norm(middle)
    normed_two = gather_square((middle * inverse_two).astype(bf16))
    inner, grad_both, out_term, back_term = feed(normed_two, cot_all, w_both, w_down)
    grad_two = scatter_square(back_term)
    cot_float = cotangent.astype(f32)
    grad_middle = cot_float + norm_back(middle, inverse_two, grad_two)
    middle_all = gather_rows(grad_middle.astype(bf16))
    outputs = (middle + scatter_square(out_term)).astype(bf16)

    down_term = dot_tn(inner, cot_all).astype(bf16).reshape(2, 2, hidden_block, D)
    down_grad = reduce_bit(reduce_bit(down_term, BIT_Y, 0), BIT_ZH, 0)
    both_term = dot_tn(normed_two, grad_both).astype(bf16).reshape(2, 2, 2, 4 * own, 8 * hidden_block)
    both_sum = reduce_bit(reduce_bit(both_term, BIT_Y, 0), BIT_ZH, 1)
    both_sum = both_sum.astype(bf16).reshape(2, 2, 2, own, 2, 2, 2, hidden_block)
    for axis, bit in ((2, BIT_C), (0, BIT_X), (1, BIT_ZL)):
        both_sum = trade_bit(both_sum, bit, axis)
    both_sum = both_sum.transpose(4, 3, 5, 0, 6, 1, 2, 7).reshape(2, own, -1).astype(f32)
    gate_grad, up_grad = both_sum[0] * gain_two, both_sum[1] * gain_two
    second_grad = jnp.sum(
        gate_weight.astype(f32) * gate_grad + up_weight.astype(f32) * up_grad, axis=-1
    ) / gain_two[:, 0]

    grad_query, grad_kv = attend_back(
        middle_all, w_out, query, key, value, mixed, lse, docs_col, docs_row, cosine, sine
    )
    grad_heads = jnp.concatenate([grad_query, grad_kv], axis=1)
    first_sum = scatter_rows(dot_nt(grad_heads, w_heads).astype(bf16)).astype(f32)
    inputs_grad = (grad_middle + norm_back(x_float, inverse_norm(x_float), first_sum)).astype(bf16)

    out_part = dot_tn(mixed, middle_all).astype(bf16).reshape(PAIR * 2, LANES // 2, D)
    out_part = out_part[:, : HEAD // 2].reshape(2, 2, own, D).transpose(1, 0, 2, 3)
    out_part = lax.psum_scatter(out_part.reshape(4 * own, D), "dp", scatter_dimension=0, tiled=True)
    output_grad = across(out_part).astype(f32)

    head_term = cut_heads(dot_tn(normed, grad_heads).astype(bf16))
    head_term = lax.psum_scatter(head_term, "dp", scatter_dimension=0, tiled=True)
    head_term = lax.all_to_all(head_term.reshape(8, own, HEAD_COLS), "seq", 0, 0, tiled=True)
    head_term = jnp.stack([head_term[GROUP_OF.index(g)] for g in range(8)], axis=1)
    head_term = head_term.astype(f32) * gain_one[:, :, None]
    query_grad = head_term[..., :QUERY_COLS].reshape(own, D)
    key_grad = head_term[..., QUERY_COLS : QUERY_COLS + HEAD].reshape(own, KV_HEADS * HEAD)
    value_grad = head_term[..., QUERY_COLS + HEAD :].reshape(own, KV_HEADS * HEAD)
    first_grad = (
        jnp.sum(query_weight.astype(f32) * query_grad, axis=-1)
        + jnp.sum(key_weight.astype(f32) * key_grad, axis=-1)
        + jnp.sum(value_weight.astype(f32) * value_grad, axis=-1)
    ) / gain_one[:, 0]
    return (
        outputs,
        inputs_grad,
        first_grad,
        query_grad,
        key_grad,
        value_grad,
        output_grad,
        second_grad,
        gate_grad,
        up_grad,
        down_grad,
    )


def solution(mesh):
    placed = (
        P(("dp", "seq"), None),
        P(("dp", "seq"), None),
        P(("dp", "seq")),
        P(("dp", "seq")),
        P(("dp", "seq")),
        P(("dp", "seq"), None),
        P(("dp", "seq"), None),
        P(("dp", "seq"), None),
        P(("dp", "seq"), None),
        P(("dp", "seq")),
        P(("dp", "seq"), None),
        P(("dp", "seq"), None),
        P(("dp", "seq"), None),
    )
    shape = dict(mesh.shape)
    tensor_parallel = shape["dp"] == 4 and shape["seq"] == KV_HEADS
    return jax.shard_map(
        body_fast if tensor_parallel else body,
        mesh=mesh,
        in_specs=placed,
        out_specs=(
            P(("dp", "seq"), None),
            P(("dp", "seq"), None),
            P(("dp", "seq")),
            P(("dp", "seq"), None),
            P(("dp", "seq"), None),
            P(("dp", "seq"), None),
            P(("dp", "seq"), None),
            P(("dp", "seq")),
            P(("dp", "seq"), None),
            P(("dp", "seq"), None),
            P(("dp", "seq"), None),
        ),
        check_vma=False,
    )
```

```python
import math

import jax
import jax.numpy as jnp
from jax import lax
from jax.experimental import pallas as pl
from jax.experimental.pallas import tpu as pltpu
from jax.sharding import PartitionSpec as P

D = 1536
HEADS = 16
KV_HEADS = 8
HEAD = 96


norm_epsilon = 1e-05
rotary_base = 100000.0


def normalize(values_in, gain):
    return (
        values_in
        * lax.rsqrt(jnp.mean(values_in * values_in, axis=-1, keepdims=True) + norm_epsilon)
        * gain
    )


def swish_product(gate, upward):
    return jax.nn.silu(gate) * upward


def rotate(matrix, positions, heads_count, direction):
    halfway = HEAD // 2
    inverse_freq = rotary_base ** (-jnp.arange(halfway, dtype=jnp.float32) * 2.0 / HEAD)
    angles = positions.astype(jnp.float32)[:, None] * inverse_freq[None, :]
    cosine = jnp.cos(angles)[:, None, :]
    sine_table = direction * jnp.sin(angles)[:, None, :]
    shaped = matrix.reshape(matrix.shape[0], heads_count, HEAD)
    first_half = shaped[..., :halfway]
    second_half = shaped[..., halfway:]
    turned = jnp.concatenate(
        [
            first_half * cosine - second_half * sine_table,
            second_half * cosine + first_half * sine_table,
        ],
        axis=-1,
    )
    return turned.reshape(matrix.shape)


def times_transposed(left, right):
    return lax.dot_general(
        left, right, (((1,), (1,)), ((), ())), preferred_element_type=jnp.float32
    )


def transposed_times(left, right):
    return lax.dot_general(
        left, right, (((0,), (0,)), ((), ())), preferred_element_type=jnp.float32
    )


def matrix_product(left, right):
    return jnp.dot(left, right, preferred_element_type=jnp.float32)


def block_rows(total_rows):
    size_rows = min(total_rows, 1024)
    while total_rows % size_rows:
        size_rows -= 1
    return size_rows


def fold_local(block_step, initial, arrays):
    total_rows = arrays[0].shape[0]
    size_rows = block_rows(total_rows)

    def one_turn(turn_index, state_in):
        begin_row = turn_index * size_rows
        pieces = tuple(
            (lax.dynamic_slice_in_dim(member, begin_row, size_rows, 0) for member in arrays)
        )
        return block_step(state_in, pieces, begin_row)

    return lax.fori_loop(0, total_rows // size_rows, one_turn, initial)


def piece_fold(block_step, state_in, pieces):
    return fold_local(block_step, state_in, pieces)


def keep_state(state_now):
    return state_now


def body(
    inputs,
    cotangent,
    doc_ids,
    positions,
    gain_first,
    query_weight,
    key_weight,
    value_weight,
    output_weight,
    gain_second,
    gate_weight,
    up_weight,
    down_weight,
):
    f32 = jnp.float32
    bf16 = jnp.bfloat16
    attend_set = (
        lax.all_gather(gain_first, ("dp", "seq"), axis=0, tiled=True),
        lax.all_gather(query_weight, ("dp", "seq"), axis=0, tiled=True),
        lax.all_gather(key_weight, ("dp", "seq"), axis=0, tiled=True),
        lax.all_gather(value_weight, ("dp", "seq"), axis=0, tiled=True),
        lax.all_gather(output_weight, ("dp", "seq"), axis=0, tiled=True),
    )
    feed_set = (
        lax.all_gather(gain_second, ("dp", "seq"), axis=0, tiled=True),
        lax.all_gather(gate_weight, ("dp", "seq"), axis=0, tiled=True),
        lax.all_gather(up_weight, ("dp", "seq"), axis=0, tiled=True),
        lax.all_gather(down_weight, ("dp", "seq"), axis=0, tiled=True),
    )
    gain_one, w_query, w_key, w_value, w_output = attend_set
    gain_two, w_gate, w_up, w_down = feed_set
    row_count = inputs.shape[0]
    group_size = HEADS // KV_HEADS
    kv_width = KV_HEADS * HEAD
    score_scale = 1.0 / math.sqrt(HEAD)
    query_rows = lax.axis_index("seq") * row_count + jnp.arange(row_count, dtype=jnp.int32)
    x_float = inputs.astype(f32)
    gain_one_float = gain_one.astype(f32)
    normed = normalize(x_float, gain_one_float).astype(bf16)
    query_rot = rotate(matrix_product(normed, w_query), positions, HEADS, 1.0).astype(bf16)
    key_rot = rotate(matrix_product(normed, w_key), positions, KV_HEADS, 1.0).astype(bf16)
    value_low = matrix_product(normed, w_value).astype(bf16)
    query_four = query_rot.reshape(row_count, KV_HEADS, group_size, HEAD)

    def mask_for(docs_part, first_key, piece_rows):
        key_rows = first_key + jnp.arange(piece_rows, dtype=jnp.int32)
        return (key_rows[None, :] <= query_rows[:, None]) & (docs_part[None, :] == doc_ids[:, None])

    def forward_step(state_in, pieces, first_key):
        keys_part, values_part, docs_part = pieces
        piece_rows = keys_part.shape[0]
        allowed = mask_for(docs_part, first_key, piece_rows)

        def forward_compute(state_now):
            accumulated, running, totals = state_now
            logits = (
                jnp.einsum(
                    "qgrd,kgd->grqk",
                    query_four,
                    keys_part.reshape(piece_rows, KV_HEADS, HEAD),
                    preferred_element_type=f32,
                )
                * score_scale
            )
            logits = jnp.where(allowed, logits, -1e30)
            new_max = jnp.maximum(running, jnp.max(logits, axis=-1))
            weights_block = jnp.where(allowed, jnp.exp(logits - new_max[..., None]), 0.0)
            factor = jnp.exp(running - new_max)
            totals = totals * factor + jnp.sum(weights_block, axis=-1)
            update = jnp.einsum(
                "grqk,kgd->qgrd",
                weights_block.astype(bf16),
                values_part.reshape(piece_rows, KV_HEADS, HEAD),
                preferred_element_type=f32,
            )
            accumulated = accumulated * jnp.transpose(factor, (2, 0, 1))[..., None] + update
            return (accumulated, new_max, totals)

        return lax.cond(jnp.any(allowed), forward_compute, keep_state, state_in)

    forward_init = (
        jnp.zeros((row_count, KV_HEADS, group_size, HEAD), f32),
        jnp.full((KV_HEADS, group_size, row_count), -1e30, f32),
        jnp.zeros((KV_HEADS, group_size, row_count), f32),
    )
    forward_state = piece_fold(
        forward_step,
        forward_init,
        (
            lax.all_gather(key_rot, "seq", axis=0, tiled=True),
            lax.all_gather(value_low, "seq", axis=0, tiled=True),
            lax.all_gather(doc_ids, "seq", axis=0, tiled=True),
        ),
    )
    accumulated, running, totals = forward_state
    attend_float = accumulated / jnp.transpose(totals, (2, 0, 1))[..., None]
    log_totals = running + jnp.log(totals)
    mixed = attend_float.reshape(row_count, D).astype(bf16)
    middle = x_float + matrix_product(mixed, w_output)
    gain_two_float = gain_two.astype(f32)
    normed_two = normalize(middle, gain_two_float).astype(bf16)
    gate = matrix_product(normed_two, w_gate)
    upward = matrix_product(normed_two, w_up)
    hidden = swish_product(gate, upward).astype(bf16)
    outputs = (middle + matrix_product(hidden, w_down)).astype(bf16)
    feed_back = (
        lax.all_gather(gain_second, ("dp", "seq"), axis=0, tiled=True),
        lax.all_gather(gate_weight, ("dp", "seq"), axis=0, tiled=True),
        lax.all_gather(up_weight, ("dp", "seq"), axis=0, tiled=True),
        lax.all_gather(down_weight, ("dp", "seq"), axis=0, tiled=True),
    )
    attend_back = (
        lax.all_gather(gain_first, ("dp", "seq"), axis=0, tiled=True),
        lax.all_gather(query_weight, ("dp", "seq"), axis=0, tiled=True),
        lax.all_gather(key_weight, ("dp", "seq"), axis=0, tiled=True),
        lax.all_gather(value_weight, ("dp", "seq"), axis=0, tiled=True),
        lax.all_gather(output_weight, ("dp", "seq"), axis=0, tiled=True),
    )
    unused_gain_two, back_gate, back_up, back_down = feed_back
    unused_gain_one, back_query, back_key, back_value, back_output = attend_back
    cot_float = cotangent.astype(f32)
    cot_low = cot_float.astype(bf16)
    down_term = transposed_times(hidden, cot_low)
    grad_hidden = times_transposed(cot_low, back_down)
    unused_swish, swish_back = jax.vjp(swish_product, gate, upward)
    grad_gate, grad_up = swish_back(grad_hidden)
    grad_gate_low = grad_gate.astype(bf16)
    grad_up_low = grad_up.astype(bf16)
    gate_term = transposed_times(normed_two, grad_gate_low)
    up_term = transposed_times(normed_two, grad_up_low)
    grad_normed_two = times_transposed(grad_gate_low, back_gate) + times_transposed(
        grad_up_low, back_up
    )
    unused_norm_two, norm_two_back = jax.vjp(normalize, middle, gain_two_float)
    grad_middle_part, gain_two_term = norm_two_back(grad_normed_two)
    second_grad, gate_grad, up_grad, down_grad = (
        lax.psum_scatter(gain_two_term, ("dp", "seq"), scatter_dimension=0, tiled=True),
        lax.psum_scatter(gate_term, ("dp", "seq"), scatter_dimension=0, tiled=True),
        lax.psum_scatter(up_term, ("dp", "seq"), scatter_dimension=0, tiled=True),
        lax.psum_scatter(down_term, ("dp", "seq"), scatter_dimension=0, tiled=True),
    )
    grad_middle = cot_float + grad_middle_part
    middle_low = grad_middle.astype(bf16)
    output_term = transposed_times(mixed, middle_low)
    grad_mixed = times_transposed(middle_low, back_output).astype(bf16)
    dout_four = grad_mixed.reshape(row_count, KV_HEADS, group_size, HEAD)
    delta_rows = jnp.einsum("qgrd,qgrd->grq", dout_four.astype(f32), attend_float)

    def query_grad_block(allowed, keys_three, values_three):
        logits = (
            jnp.einsum("qgrd,kgd->grqk", query_four, keys_three, preferred_element_type=f32)
            * score_scale
        )
        logits = jnp.where(allowed, logits, -1e30)
        weights_block = jnp.where(allowed, jnp.exp(logits - log_totals[..., None]), 0.0)
        grad_weights = jnp.einsum(
            "qgrd,kgd->grqk", dout_four, values_three, preferred_element_type=f32
        )
        grad_logits = (weights_block * (grad_weights - delta_rows[..., None]) * score_scale).astype(
            bf16
        )
        return (weights_block, grad_logits)

    def query_step(state_in, pieces, first_key):
        keys_part, values_part, docs_part = pieces
        piece_rows = keys_part.shape[0]
        allowed = mask_for(docs_part, first_key, piece_rows)

        def query_compute(grad_query):
            keys_three = keys_part.reshape(piece_rows, KV_HEADS, HEAD)
            values_three = values_part.reshape(piece_rows, KV_HEADS, HEAD)
            unused_weights, grad_logits = query_grad_block(allowed, keys_three, values_three)
            return grad_query + jnp.einsum(
                "grqk,kgd->qgrd", grad_logits, keys_three, preferred_element_type=f32
            )

        return lax.cond(jnp.any(allowed), query_compute, keep_state, state_in)

    grad_query_rot = piece_fold(
        query_step,
        jnp.zeros((row_count, KV_HEADS, group_size, HEAD), f32),
        (
            lax.all_gather(key_rot, "seq", axis=0, tiled=True),
            lax.all_gather(value_low, "seq", axis=0, tiled=True),
            lax.all_gather(doc_ids, "seq", axis=0, tiled=True),
        ),
    )
    lse_rows = jnp.transpose(log_totals, (2, 0, 1)).reshape(row_count, HEADS)
    delta_flat = jnp.transpose(delta_rows, (2, 0, 1)).reshape(row_count, HEADS)
    lse_all, delta_all = (
        lax.all_gather(lse_rows, "seq", axis=0, tiled=True),
        lax.all_gather(delta_flat, "seq", axis=0, tiled=True),
    )
    keys_mine = key_rot.reshape(row_count, KV_HEADS, HEAD)
    values_mine = value_low.reshape(row_count, KV_HEADS, HEAD)

    def key_step(state_in, pieces, first_query):
        queries_part, dout_part, docs_part = pieces
        piece_rows = queries_part.shape[0]
        other_rows = first_query + jnp.arange(piece_rows, dtype=jnp.int32)
        allowed = (query_rows[None, :] <= other_rows[:, None]) & (
            doc_ids[None, :] == docs_part[:, None]
        )

        def key_compute(state_now):
            grad_keys, grad_values = state_now
            lse_part = lax.dynamic_slice_in_dim(lse_all, first_query, piece_rows, 0)
            delta_part = lax.dynamic_slice_in_dim(delta_all, first_query, piece_rows, 0)
            lse_three = jnp.transpose(lse_part.reshape(piece_rows, KV_HEADS, group_size), (1, 2, 0))
            delta_three = jnp.transpose(
                delta_part.reshape(piece_rows, KV_HEADS, group_size), (1, 2, 0)
            )
            queries_four = queries_part.reshape(piece_rows, KV_HEADS, group_size, HEAD)
            douts_four = dout_part.reshape(piece_rows, KV_HEADS, group_size, HEAD)
            logits = (
                jnp.einsum("qgrd,kgd->grqk", queries_four, keys_mine, preferred_element_type=f32)
                * score_scale
            )
            logits = jnp.where(allowed, logits, -1e30)
            weights_block = jnp.where(allowed, jnp.exp(logits - lse_three[..., None]), 0.0)
            grad_weights = jnp.einsum(
                "qgrd,kgd->grqk", douts_four, values_mine, preferred_element_type=f32
            )
            grad_logits = (
                weights_block * (grad_weights - delta_three[..., None]) * score_scale
            ).astype(bf16)
            grad_keys = grad_keys + jnp.einsum(
                "grqk,qgrd->kgd", grad_logits, queries_four, preferred_element_type=f32
            )
            grad_values = grad_values + jnp.einsum(
                "grqk,qgrd->kgd", weights_block.astype(bf16), douts_four, preferred_element_type=f32
            )
            return (grad_keys, grad_values)

        return lax.cond(jnp.any(allowed), key_compute, keep_state, state_in)

    key_init = (
        jnp.zeros((row_count, KV_HEADS, HEAD), f32),
        jnp.zeros((row_count, KV_HEADS, HEAD), f32),
    )
    grad_keys_three, grad_values_three = piece_fold(
        key_step,
        key_init,
        (
            lax.all_gather(query_rot, "seq", axis=0, tiled=True),
            lax.all_gather(grad_mixed, "seq", axis=0, tiled=True),
            lax.all_gather(doc_ids, "seq", axis=0, tiled=True),
        ),
    )
    grad_keys_mine = grad_keys_three.reshape(row_count, kv_width)
    grad_values_mine = grad_values_three.reshape(row_count, kv_width)
    grad_query_low = rotate(grad_query_rot.reshape(row_count, D), positions, HEADS, -1.0).astype(
        bf16
    )
    grad_key_low = rotate(grad_keys_mine, positions, KV_HEADS, -1.0).astype(bf16)
    grad_value_low = grad_values_mine.astype(bf16)
    query_term = transposed_times(normed, grad_query_low)
    key_term_all = transposed_times(normed, grad_key_low)
    value_term_all = transposed_times(normed, grad_value_low)
    grad_normed = (
        times_transposed(grad_query_low, back_query)
        + times_transposed(grad_key_low, back_key)
        + times_transposed(grad_value_low, back_value)
    )
    unused_norm_one, norm_one_back = jax.vjp(normalize, x_float, gain_one_float)
    grad_input_part, gain_one_term = norm_one_back(grad_normed)
    inputs_grad = (grad_middle + grad_input_part).astype(bf16)
    first_grad, query_grad, key_grad, value_grad, output_grad = (
        lax.psum_scatter(gain_one_term, ("dp", "seq"), scatter_dimension=0, tiled=True),
        lax.psum_scatter(query_term, ("dp", "seq"), scatter_dimension=0, tiled=True),
        lax.psum_scatter(key_term_all, ("dp", "seq"), scatter_dimension=0, tiled=True),
        lax.psum_scatter(value_term_all, ("dp", "seq"), scatter_dimension=0, tiled=True),
        lax.psum_scatter(output_term, ("dp", "seq"), scatter_dimension=0, tiled=True),
    )
    return (
        outputs,
        inputs_grad,
        first_grad,
        query_grad,
        key_grad,
        value_grad,
        output_grad,
        second_grad,
        gate_grad,
        up_grad,
        down_grad,
    )

BOTH = ("dp", "seq")
BIT_Y, BIT_X, BIT_ZH, BIT_ZL, BIT_C = 16, 8, 4, 2, 1
PAIR = 2
LANES = 128
PAD_COLS = (PAIR + 2) * LANES
BLOCK = 256
f32 = jnp.float32
bf16 = jnp.bfloat16
VMEM_BYTES = 60 * 1024 * 1024


def swap(value, bit):
    return lax.ppermute(value, BOTH, [(i, i ^ bit) for i in range(32)])


def my_bit(bit):
    flat = lax.axis_index("dp") * 8 + lax.axis_index("seq")
    return (flat // bit) % 2


def pick(value, index, axis):
    return lax.dynamic_index_in_dim(value, index, axis, keepdims=False)


def paired(mine, other, bit, axis):
    low_first = my_bit(bit) == 0
    return jnp.stack(
        [jnp.where(low_first, mine, other), jnp.where(low_first, other, mine)], axis
    )


def gather_bit(value, bit, axis):
    return paired(value, swap(value, bit), bit, axis)


def trade_bit(value, bit, axis):
    mine = my_bit(bit)
    keep = pick(value, mine, axis)
    other = swap(pick(value, 1 - mine, axis), bit)
    return paired(keep, other, bit, axis)


def after(value, *earlier):
    return lax.optimization_barrier((value,) + earlier)[0]


def halves(value, bit, axis):
    mine = my_bit(bit)
    return pick(value, mine, axis), swap(pick(value, 1 - mine, axis).astype(bf16), bit)


def total(pair, *earlier):
    keep, other = pair
    if earlier:
        other = after(other, *earlier)
    return keep.astype(f32) + other.astype(f32)


def reduce_bit(value, bit, axis):
    return total(halves(value, bit, axis))


def gather_square(value):
    half = value.shape[0] // 2
    from_x = swap(value, BIT_X)
    from_z = swap(value, BIT_ZL)
    far_low = swap(from_z[:half], BIT_X)
    far_high = swap(from_x[half:], BIT_ZL)
    chip = jnp.concatenate([value, from_x, from_z, far_low, far_high])
    return jnp.concatenate([chip, swap(chip, BIT_C)])


def chip_sums(parts):
    middle = parts.shape[0] // 2
    return parts[:middle].astype(f32) + swap(parts[middle:], BIT_C).astype(f32)


def scatter_square(sums):
    rows = sums.shape[0] // 4
    half = rows // 2
    own, to_x, to_z, far = (sums[i * rows : (i + 1) * rows] for i in range(4))
    far = far.astype(bf16)
    in_z = swap(far[:half], BIT_X).astype(f32)
    in_x = swap(far[half:], BIT_ZL).astype(f32)
    to_z = jnp.concatenate([to_z[:half] + in_z, to_z[half:]]).astype(bf16)
    to_x = jnp.concatenate([to_x[:half], to_x[half:] + in_x]).astype(bf16)
    return own + swap(to_x, BIT_X).astype(f32) + swap(to_z, BIT_ZL).astype(f32)


def across(value):
    pairs = []
    for i in range(32):
        y, x, zh, zl, c = (i >> 4) & 1, (i >> 3) & 1, (i >> 2) & 1, (i >> 1) & 1, i & 1
        pairs.append((i, c * 16 + zl * 8 + zh * 4 + x * 2 + y))
    return lax.ppermute(value, BOTH, pairs)


def gather_rows(value):
    return lax.all_gather(value, "seq", axis=0, tiled=True)


def scatter_rows(value):
    return lax.psum_scatter(value, "seq", scatter_dimension=0, tiled=True)


def dot_nn(left, right):
    return jnp.dot(left, right, preferred_element_type=f32)


def dot_nt(left, right):
    return lax.dot_general(left, right, (((1,), (1,)), ((), ())), preferred_element_type=f32)


def dot_tn(left, right):
    return lax.dot_general(left, right, (((0,), (0,)), ((), ())), preferred_element_type=f32)


def whole(*shape):
    return pl.BlockSpec(shape, lambda i: (0,) * len(shape), pipeline_mode=pl.Buffered(1))


def rows_of(rows, cols):
    return pl.BlockSpec((rows, cols), lambda i: (i, 0))


def turn(matrix, cosine, sine):
    return matrix * cosine + pltpu.roll(matrix, LANES // 2, 1) * sine


def project_kernel(x_ref, wq_ref, wkv_ref, freq_ref, hn_ref, q_ref, k_ref, v_ref, cos_ref, sin_ref):
    x = x_ref[:, :D].astype(f32)
    scale = lax.rsqrt(jnp.mean(x * x, axis=-1, keepdims=True) + norm_epsilon)
    normed = (x * scale).astype(bf16)
    hn_ref[...] = normed
    extra = x_ref[:, D:].astype(f32)
    place = extra[:, 1:2] * 128.0 + extra[:, 2:3]
    angles = place * freq_ref[...]
    lane = lax.broadcasted_iota(jnp.int32, angles.shape, 1)
    cosine = jnp.cos(angles)
    sine = jnp.where(lane < LANES // 2, -jnp.sin(angles), jnp.sin(angles))
    cos_ref[...] = cosine
    sin_ref[...] = sine
    full = dot_nn(normed, wq_ref[...])
    for h in range(PAIR):
        part = full[:, h * LANES : (h + 1) * LANES]
        q_ref[:, h * LANES : (h + 1) * LANES] = turn(part, cosine, sine).astype(bf16)
    full = dot_nn(normed, wkv_ref[...])
    k_ref[...] = turn(full[:, :LANES], cosine, sine).astype(bf16)
    v_ref[...] = full[:, LANES:].astype(bf16)


def project(rows_all, w_query, w_kv):
    total, width = rows_all.shape
    lane = jnp.arange(LANES) % (LANES // 2)
    freq = rotary_base ** (-lane.astype(f32) * 2.0 / HEAD)
    freq = jnp.where(lane < HEAD // 2, freq, 0.0).reshape(1, LANES)
    shapes = [(D, bf16), (PAIR * LANES, bf16), (LANES, bf16), (LANES, bf16), (LANES, f32), (LANES, f32)]
    return pl.pallas_call(
        project_kernel,
        grid=(total // BLOCK,),
        in_specs=[
            rows_of(BLOCK, width),
            whole(D, PAIR * LANES),
            whole(D, 2 * LANES),
            whole(1, LANES),
        ],
        out_specs=[rows_of(BLOCK, n) for n, t in shapes],
        out_shape=[jax.ShapeDtypeStruct((total, n), t) for n, t in shapes],
        compiler_params=pltpu.CompilerParams(vmem_limit_bytes=VMEM_BYTES),
        name="project",
    )(rows_all, w_query, w_kv, freq)


def allowed_pairs(dcol_ref, drow_ref, first, keys):
    shape = (BLOCK, keys)
    query_at = first + lax.broadcasted_iota(jnp.int32, shape, 0)
    key_at = lax.broadcasted_iota(jnp.int32, shape, 1)
    return (key_at <= query_at) & (dcol_ref[...] == drow_ref[:, :keys])


def attend_kernel(q_ref, k_ref, v_ref, dcol_ref, drow_ref, w_ref, a_ref, lse_ref, o_ref):
    blocks = k_ref.shape[0] // BLOCK

    def run(b):
        keys = (b + 1) * BLOCK
        allowed = allowed_pairs(dcol_ref, drow_ref, b * BLOCK, keys)
        for h in range(PAIR):
            cols = slice(h * LANES, (h + 1) * LANES)
            logits = dot_nt(q_ref[:, cols], k_ref[:keys, :]) * (1.0 / math.sqrt(HEAD))
            logits = jnp.where(allowed, logits, -1e30)
            top = jnp.max(logits, axis=-1, keepdims=True)
            weights = jnp.exp(logits - top)
            total = jnp.sum(weights, axis=-1, keepdims=True)
            mixed = dot_nn(weights.astype(bf16), v_ref[:keys, :]) / total
            a_ref[:, cols] = mixed.astype(bf16)
            lse_ref[:, h : h + 1] = top + jnp.log(total)

    for b in range(blocks):
        pl.when(pl.program_id(0) == b)(lambda b=b: run(b))
    o_ref[...] = dot_nn(a_ref[...], w_ref[...]).astype(bf16)


def attend(query, key, value, docs_col, docs_row, weights):
    total = query.shape[0]
    shapes = [(PAIR * LANES, bf16), (PAIR, f32), (D, bf16)]
    return pl.pallas_call(
        attend_kernel,
        grid=(total // BLOCK,),
        in_specs=[
            rows_of(BLOCK, PAIR * LANES),
            whole(total, LANES),
            whole(total, LANES),
            rows_of(BLOCK, 1),
            whole(1, total),
            whole(PAIR * LANES, D),
        ],
        out_specs=[rows_of(BLOCK, n) for n, t in shapes],
        out_shape=[jax.ShapeDtypeStruct((total, n), t) for n, t in shapes],
        compiler_params=pltpu.CompilerParams(vmem_limit_bytes=VMEM_BYTES),
        name="attend",
    )(query, key, value, docs_col, docs_row, weights)


def attend_back_kernel(
    mb_ref, w_ref, q_ref, k_ref, v_ref, a_ref, lse_ref, dcol_ref, drow_ref, cos_ref, sin_ref,
    dq_ref, dkv_ref, dk_acc, dv_acc, dq_acc
):
    step = pl.program_id(0)
    blocks = k_ref.shape[0] // BLOCK

    @pl.when(step == 0)
    def _():
        dk_acc[...] = jnp.zeros_like(dk_acc)
        dv_acc[...] = jnp.zeros_like(dv_acc)

    grad_mixed = dot_nt(mb_ref[...], w_ref[...]).astype(bf16)
    scale = 1.0 / math.sqrt(HEAD)

    def run(b):
        keys = (b + 1) * BLOCK
        allowed = allowed_pairs(dcol_ref, drow_ref, b * BLOCK, keys)
        for h in range(PAIR):
            cols = slice(h * LANES, (h + 1) * LANES)
            query = q_ref[:, cols]
            grad = grad_mixed[:, cols]
            delta = jnp.sum(
                grad.astype(f32) * a_ref[:, cols].astype(f32), axis=-1, keepdims=True
            )
            logits = dot_nt(query, k_ref[:keys, :]) * scale
            logits = jnp.where(allowed, logits, -1e30)
            weights = jnp.exp(logits - lse_ref[:, h : h + 1])
            grad_weights = dot_nt(grad, v_ref[:keys, :])
            grad_logits = (weights * (grad_weights - delta) * scale).astype(bf16)
            dq_acc[:, cols] = dot_nn(grad_logits, k_ref[:keys, :])
            dk_acc[:keys, :] += dot_tn(grad_logits, query)
            dv_acc[:keys, :] += dot_tn(weights.astype(bf16), grad)

    for b in range(blocks):
        pl.when(step == b)(lambda b=b: run(b))

    rows = pl.ds(pl.multiple_of(step * BLOCK, BLOCK), BLOCK)
    for h in range(PAIR):
        cols = slice(h * LANES, (h + 1) * LANES)
        dq_ref[:, cols] = turn(dq_acc[:, cols], cos_ref[rows, :], -sin_ref[rows, :]).astype(bf16)

    @pl.when(step == blocks - 1)
    def _():
        dkv_ref[:, :LANES] = turn(dk_acc[...], cos_ref[...], -sin_ref[...]).astype(bf16)
        dkv_ref[:, LANES:] = dv_acc[...].astype(bf16)


def attend_back(mb, weights, query, key, value, mixed, lse, docs_col, docs_row, cosine, sine):
    total = query.shape[0]
    return pl.pallas_call(
        attend_back_kernel,
        grid=(total // BLOCK,),
        in_specs=[
            rows_of(BLOCK, D),
            whole(PAIR * LANES, D),
            rows_of(BLOCK, PAIR * LANES),
            whole(total, LANES),
            whole(total, LANES),
            rows_of(BLOCK, PAIR * LANES),
            rows_of(BLOCK, PAIR),
            rows_of(BLOCK, 1),
            whole(1, total),
            whole(total, LANES),
            whole(total, LANES),
        ],
        out_specs=[rows_of(BLOCK, PAIR * LANES), whole(total, 2 * LANES)],
        out_shape=[
            jax.ShapeDtypeStruct((total, PAIR * LANES), bf16),
            jax.ShapeDtypeStruct((total, 2 * LANES), bf16),
        ],
        scratch_shapes=[
            pltpu.VMEM((total, LANES), f32),
            pltpu.VMEM((total, LANES), f32),
            pltpu.VMEM((BLOCK, PAIR * LANES), f32),
        ],
        compiler_params=pltpu.CompilerParams(vmem_limit_bytes=VMEM_BYTES),
        name="attend_back",
    )(mb, weights, query, key, value, mixed, lse, docs_col, docs_row, cosine, sine)


def feed_kernel(hn_ref, cb_ref, wg_ref, wu_ref, wd_ref, f_ref, dgu_ref, o_ref, e_ref):
    hidden = wd_ref.shape[0]
    gate = dot_nn(hn_ref[...], wg_ref[...])
    up = dot_nn(hn_ref[...], wu_ref[...])
    sig = 1.0 / (1.0 + jnp.exp(-gate))
    swish = gate * sig
    inner = (swish * up).astype(bf16)
    f_ref[...] = inner
    o_ref[...] = dot_nn(inner, wd_ref[...]).astype(bf16)
    grad = dot_nt(cb_ref[...], wd_ref[...])
    dgu_ref[:, :hidden] = (grad * up * sig * (1.0 + gate * (1.0 - sig))).astype(bf16)
    dgu_ref[:, hidden:] = (grad * swish).astype(bf16)
    back = dot_nt(dgu_ref[:, :hidden], wg_ref[...]) + dot_nt(dgu_ref[:, hidden:], wu_ref[...])
    e_ref[...] = back.astype(bf16)


def feed(normed, cot, w_gate, w_up, w_down):
    total, hidden = normed.shape[0], w_down.shape[0]
    shapes = [(hidden, bf16), (2 * hidden, bf16), (D, bf16), (D, bf16)]
    return pl.pallas_call(
        feed_kernel,
        grid=(total // BLOCK,),
        in_specs=[
            rows_of(BLOCK, D),
            rows_of(BLOCK, D),
            whole(D, hidden),
            whole(D, hidden),
            whole(hidden, D),
        ],
        out_specs=[rows_of(BLOCK, n) for n, t in shapes],
        out_shape=[jax.ShapeDtypeStruct((total, n), t) for n, t in shapes],
        compiler_params=pltpu.CompilerParams(vmem_limit_bytes=VMEM_BYTES),
        name="feed",
    )(normed, cot, w_gate, w_up, w_down)


def inverse_norm(values):
    return lax.rsqrt(jnp.mean(values * values, axis=-1, keepdims=True) + norm_epsilon)


def norm_back(values, inverse, grad):
    return inverse * grad - values * inverse**3 * jnp.mean(grad * values, axis=-1, keepdims=True)


def pad_heads(matrix):
    rows, cols = matrix.shape
    split = matrix.reshape(rows, cols // (HEAD // 2), HEAD // 2)
    return jnp.pad(split, ((0, 0), (0, 0), (0, LANES // 2 - HEAD // 2))).reshape(rows, -1)


def cut_heads(matrix):
    rows, cols = matrix.shape
    split = matrix.reshape(rows, cols // (LANES // 2), LANES // 2)
    return split[..., : HEAD // 2].reshape(rows, -1)


def body_fast(
    inputs,
    cotangent,
    doc_ids,
    positions,
    gain_first,
    query_weight,
    key_weight,
    value_weight,
    output_weight,
    gain_second,
    gate_weight,
    up_weight,
    down_weight,
):
    rows = inputs.shape[0]
    own = query_weight.shape[0]
    hidden_block = down_weight.shape[0]
    gain_one = gain_first.astype(f32)[:, None]
    gain_two = gain_second.astype(f32)[:, None]

    marks = jnp.stack([doc_ids, positions // 128, positions % 128], axis=1).astype(bf16)
    marks = jnp.pad(marks, ((0, 0), (0, LANES - 3)))
    rows_all = gather_rows(jnp.concatenate([inputs, marks], axis=1))
    def heads_of(weight, each):
        scaled = pad_heads((weight.astype(f32) * gain_one).astype(bf16))
        return scaled.reshape(own, KV_HEADS, each * LANES)

    parts = jnp.concatenate(
        [heads_of(query_weight, PAIR), heads_of(key_weight, 1), heads_of(value_weight, 1)], axis=-1
    )
    parts = parts.reshape(own, 2, 2, 2, PAD_COLS).transpose(3, 2, 1, 0, 4)
    first_parts = parts
    for axis, bit in ((2, BIT_C), (1, BIT_ZL), (0, BIT_ZH)):
        parts = trade_bit(parts, bit, axis)
    parts = parts.reshape(8 * own, PAD_COLS)
    w_query, w_kv = parts[:, : PAIR * LANES], parts[:, PAIR * LANES :]
    w_query = gather_bit(gather_bit(w_query, BIT_Y, 0), BIT_X, 1).reshape(D, PAIR * LANES)
    w_kv = gather_bit(gather_bit(w_kv, BIT_X, 0), BIT_Y, 0).reshape(D, 2 * LANES)

    block = gather_bit(gather_bit(output_weight, BIT_C, 0), BIT_ZL, 0)
    w_out = across(after(block, parts))
    w_out = jnp.pad(w_out, ((0, 0), (0, 0), (0, LANES // 2 - own), (0, 0)))
    w_out = w_out.reshape(PAIR * LANES, D)

    both = jnp.stack(
        [
            (gate_weight.astype(f32) * gain_two).astype(bf16),
            (up_weight.astype(f32) * gain_two).astype(bf16),
        ]
    ).reshape(2, own, 2, 2, 2, 2, 2, hidden_block)
    both = after(both.transpose(3, 5, 6, 0, 1, 2, 4, 7), first_parts)
    both = trade_bit(trade_bit(both, BIT_C, 2), BIT_X, 0)
    both = trade_bit(after(both, parts), BIT_ZL, 1)
    both = both.reshape(2, 2, 2, 2, own, 4 * hidden_block).transpose(3, 0, 1, 2, 4, 5)
    rows_all = after(rows_all, both)
    w_gate, w_up = both.reshape(2, 2, 4 * own, 4 * hidden_block)
    w_gate = gather_bit(after(w_gate, w_kv), BIT_ZH, 1)
    w_up = gather_bit(after(w_up, w_gate), BIT_ZH, 1)
    w_down = gather_bit(after(down_weight, w_up), BIT_ZH, 0)

    docs = rows_all[:, D].astype(f32)
    docs_col, docs_row = docs[:, None], docs[None, :]
    normed, query, key, value, cosine, sine = project(rows_all, w_query, w_kv)
    mixed, lse, term = attend(query, key, value, docs_col, docs_row, w_out)
    x_float = inputs.astype(f32)
    term, w_gate = lax.optimization_barrier((term, w_gate))
    w_gate = gather_bit(w_gate, BIT_Y, 0).reshape(D, -1)
    cot_all = gather_square(after(cotangent, term))
    attended = after(scatter_rows(term), w_gate, w_up, cot_all)
    w_up = gather_bit(w_up, BIT_Y, 0).reshape(D, -1)
    w_down = gather_bit(w_down, BIT_Y, 0).reshape(-1, D)
    middle = x_float + attended.astype(f32)

    inverse_two = inverse_norm(middle)
    normed_two = gather_square((middle * inverse_two).astype(bf16))
    inner, grad_both, out_term, back_term = feed(
        normed_two, cot_all, w_gate, w_up, w_down
    )
    width = 4 * hidden_block
    sums = chip_sums(back_term)
    grad_two = scatter_square(sums)
    late_two = after(normed_two, sums)
    gate_term = dot_tn(late_two, grad_both[:, :width]).astype(bf16)
    grad_two = after(grad_two, gate_term)
    cot_float = cotangent.astype(f32)
    grad_middle = cot_float + norm_back(middle, inverse_two, grad_two)
    middle_low = grad_middle.astype(bf16)
    middle_all = gather_rows(middle_low)

    gate_pair = halves(gate_term.reshape(2, 2, 2, 4 * own, width), BIT_Y, 0)
    up_term = dot_tn(late_two, grad_both[:, width:]).astype(bf16)
    down_term = dot_tn(inner, cot_all).astype(bf16)
    up_term, down_term = after(up_term, middle_low), after(down_term, middle_low)
    up_pair = halves(up_term.reshape(2, 2, 2, 4 * own, width), BIT_Y, 0)
    down_pair = halves(down_term.reshape(2, 2, hidden_block, D), BIT_Y, 0)
    gate_pair = halves(total(gate_pair, middle_low), BIT_ZH, 1)
    out_sums = chip_sums(after(out_term, middle_low))
    outputs = (middle + scatter_square(out_sums)).astype(bf16)

    grad_query, grad_kv = attend_back(
        middle_all, w_out, query, key, value, mixed, lse, docs_col, docs_row, cosine, sine
    )
    up_pair = halves(total(up_pair, middle_all), BIT_ZH, 1)
    down_pair = halves(total(down_pair, middle_all), BIT_ZH, 0)
    first_term = (dot_nt(grad_query, w_query) + dot_nt(grad_kv, w_kv)).astype(bf16)
    first_sum = scatter_rows(first_term).astype(f32)
    inputs_grad = (grad_middle + norm_back(x_float, inverse_norm(x_float), first_sum)).astype(bf16)

    query_term = dot_tn(normed, grad_query).astype(bf16).reshape(2, 2, 8 * own, PAIR * LANES)
    kv_term = dot_tn(normed, grad_kv).astype(bf16).reshape(2, 2, 8 * own, 2 * LANES)
    query_term = reduce_bit(reduce_bit(query_term, BIT_Y, 0), BIT_X, 0)
    kv_term = reduce_bit(reduce_bit(kv_term, BIT_X, 1), BIT_Y, 0)
    head_sums = jnp.concatenate([query_term.astype(bf16), kv_term.astype(bf16)], axis=1)
    head_term = head_sums.reshape(2, 2, 2, own, PAD_COLS)
    for axis, bit in ((0, BIT_ZH), (1, BIT_ZL), (2, BIT_C)):
        head_term = trade_bit(head_term, bit, axis)
    head_term = head_term.transpose(3, 2, 1, 0, 4).reshape(own, KV_HEADS, PAD_COLS)

    def grad_of(first, each):
        cols = head_term[..., first * LANES : (first + each) * LANES]
        return cut_heads(cols.reshape(own, -1)).astype(f32) * gain_one

    query_grad, key_grad, value_grad = grad_of(0, PAIR), grad_of(PAIR, 1), grad_of(PAIR + 1, 1)

    out_part = dot_tn(mixed, middle_all).astype(bf16).reshape(2, 2, LANES // 2, D)[:, :, :own]
    out_part = reduce_bit(reduce_bit(after(out_part, head_sums), BIT_Y, 1), BIT_X, 0)
    output_grad = across(out_part.astype(bf16)).astype(f32)

    both_sum = jnp.stack(
        [total(gate_pair, head_sums), total(up_pair, head_sums)], axis=2
    ).astype(bf16)
    both_sum = both_sum.reshape(2, 4 * own, 2, width).reshape(2, 2, 2, own, 2, width)
    for axis, bit in ((0, BIT_X), (1, BIT_ZL), (2, BIT_C)):
        both_sum = trade_bit(both_sum, bit, axis)
    both_sum = both_sum.reshape(2, 2, 2, own, 2, 2, 2, hidden_block)
    both_sum = both_sum.transpose(4, 3, 5, 0, 6, 1, 2, 7).reshape(2, own, -1).astype(f32)
    gate_grad, up_grad = both_sum[0] * gain_two, both_sum[1] * gain_two
    down_grad = total(down_pair, first_term)
    second_grad = jnp.sum(
        gate_weight.astype(f32) * gate_grad + up_weight.astype(f32) * up_grad, axis=-1
    ) / gain_two[:, 0]

    first_grad = (
        jnp.sum(query_weight.astype(f32) * query_grad, axis=-1)
        + jnp.sum(key_weight.astype(f32) * key_grad, axis=-1)
        + jnp.sum(value_weight.astype(f32) * value_grad, axis=-1)
    ) / gain_one[:, 0]
    return (
        outputs,
        inputs_grad,
        first_grad,
        query_grad,
        key_grad,
        value_grad,
        output_grad,
        second_grad,
        gate_grad,
        up_grad,
        down_grad,
    )


def solution(mesh):
    placed = (
        P(("dp", "seq"), None),
        P(("dp", "seq"), None),
        P(("dp", "seq")),
        P(("dp", "seq")),
        P(("dp", "seq")),
        P(("dp", "seq"), None),
        P(("dp", "seq"), None),
        P(("dp", "seq"), None),
        P(("dp", "seq"), None),
        P(("dp", "seq")),
        P(("dp", "seq"), None),
        P(("dp", "seq"), None),
        P(("dp", "seq"), None),
    )
    shape = dict(mesh.shape)
    tensor_parallel = shape["dp"] == 4 and shape["seq"] == KV_HEADS
    return jax.shard_map(
        body_fast if tensor_parallel else body,
        mesh=mesh,
        in_specs=placed,
        out_specs=(
            P(("dp", "seq"), None),
            P(("dp", "seq"), None),
            P(("dp", "seq")),
            P(("dp", "seq"), None),
            P(("dp", "seq"), None),
            P(("dp", "seq"), None),
            P(("dp", "seq"), None),
            P(("dp", "seq")),
            P(("dp", "seq"), None),
            P(("dp", "seq"), None),
            P(("dp", "seq"), None),
        ),
        check_vma=False,
    )
```

```python
import math

import jax
import jax.numpy as jnp
from jax import lax
from jax.experimental import pallas as pl
from jax.experimental.pallas import tpu as pltpu
from jax.sharding import Mesh, PartitionSpec as P

D = 1536
HEADS = 16
KV_HEADS = 8
HEAD = 96


norm_epsilon = 1e-05
rotary_base = 100000.0


def normalize(values_in, gain):
    return (
        values_in
        * lax.rsqrt(jnp.mean(values_in * values_in, axis=-1, keepdims=True) + norm_epsilon)
        * gain
    )


def swish_product(gate, upward):
    return jax.nn.silu(gate) * upward


def rotate(matrix, positions, heads_count, direction):
    halfway = HEAD // 2
    inverse_freq = rotary_base ** (-jnp.arange(halfway, dtype=jnp.float32) * 2.0 / HEAD)
    angles = positions.astype(jnp.float32)[:, None] * inverse_freq[None, :]
    cosine = jnp.cos(angles)[:, None, :]
    sine_table = direction * jnp.sin(angles)[:, None, :]
    shaped = matrix.reshape(matrix.shape[0], heads_count, HEAD)
    first_half = shaped[..., :halfway]
    second_half = shaped[..., halfway:]
    turned = jnp.concatenate(
        [
            first_half * cosine - second_half * sine_table,
            second_half * cosine + first_half * sine_table,
        ],
        axis=-1,
    )
    return turned.reshape(matrix.shape)


def times_transposed(left, right):
    return lax.dot_general(
        left, right, (((1,), (1,)), ((), ())), preferred_element_type=jnp.float32
    )


def transposed_times(left, right):
    return lax.dot_general(
        left, right, (((0,), (0,)), ((), ())), preferred_element_type=jnp.float32
    )


def matrix_product(left, right):
    return jnp.dot(left, right, preferred_element_type=jnp.float32)


def block_rows(total_rows):
    size_rows = min(total_rows, 1024)
    while total_rows % size_rows:
        size_rows -= 1
    return size_rows


def fold_local(block_step, initial, arrays):
    total_rows = arrays[0].shape[0]
    size_rows = block_rows(total_rows)

    def one_turn(turn_index, state_in):
        begin_row = turn_index * size_rows
        pieces = tuple(
            (lax.dynamic_slice_in_dim(member, begin_row, size_rows, 0) for member in arrays)
        )
        return block_step(state_in, pieces, begin_row)

    return lax.fori_loop(0, total_rows // size_rows, one_turn, initial)


def piece_fold(block_step, state_in, pieces):
    return fold_local(block_step, state_in, pieces)


def keep_state(state_now):
    return state_now


def body(
    inputs,
    cotangent,
    doc_ids,
    positions,
    gain_first,
    query_weight,
    key_weight,
    value_weight,
    output_weight,
    gain_second,
    gate_weight,
    up_weight,
    down_weight,
):
    f32 = jnp.float32
    bf16 = jnp.bfloat16
    attend_set = (
        lax.all_gather(gain_first, ("dp", "seq"), axis=0, tiled=True),
        lax.all_gather(query_weight, ("dp", "seq"), axis=0, tiled=True),
        lax.all_gather(key_weight, ("dp", "seq"), axis=0, tiled=True),
        lax.all_gather(value_weight, ("dp", "seq"), axis=0, tiled=True),
        lax.all_gather(output_weight, ("dp", "seq"), axis=0, tiled=True),
    )
    feed_set = (
        lax.all_gather(gain_second, ("dp", "seq"), axis=0, tiled=True),
        lax.all_gather(gate_weight, ("dp", "seq"), axis=0, tiled=True),
        lax.all_gather(up_weight, ("dp", "seq"), axis=0, tiled=True),
        lax.all_gather(down_weight, ("dp", "seq"), axis=0, tiled=True),
    )
    gain_one, w_query, w_key, w_value, w_output = attend_set
    gain_two, w_gate, w_up, w_down = feed_set
    row_count = inputs.shape[0]
    group_size = HEADS // KV_HEADS
    kv_width = KV_HEADS * HEAD
    score_scale = 1.0 / math.sqrt(HEAD)
    query_rows = lax.axis_index("seq") * row_count + jnp.arange(row_count, dtype=jnp.int32)
    x_float = inputs.astype(f32)
    gain_one_float = gain_one.astype(f32)
    normed = normalize(x_float, gain_one_float).astype(bf16)
    query_rot = rotate(matrix_product(normed, w_query), positions, HEADS, 1.0).astype(bf16)
    key_rot = rotate(matrix_product(normed, w_key), positions, KV_HEADS, 1.0).astype(bf16)
    value_low = matrix_product(normed, w_value).astype(bf16)
    query_four = query_rot.reshape(row_count, KV_HEADS, group_size, HEAD)

    def mask_for(docs_part, first_key, piece_rows):
        key_rows = first_key + jnp.arange(piece_rows, dtype=jnp.int32)
        return (key_rows[None, :] <= query_rows[:, None]) & (docs_part[None, :] == doc_ids[:, None])

    def forward_step(state_in, pieces, first_key):
        keys_part, values_part, docs_part = pieces
        piece_rows = keys_part.shape[0]
        allowed = mask_for(docs_part, first_key, piece_rows)

        def forward_compute(state_now):
            accumulated, running, totals = state_now
            logits = (
                jnp.einsum(
                    "qgrd,kgd->grqk",
                    query_four,
                    keys_part.reshape(piece_rows, KV_HEADS, HEAD),
                    preferred_element_type=f32,
                )
                * score_scale
            )
            logits = jnp.where(allowed, logits, -1e30)
            new_max = jnp.maximum(running, jnp.max(logits, axis=-1))
            weights_block = jnp.where(allowed, jnp.exp(logits - new_max[..., None]), 0.0)
            factor = jnp.exp(running - new_max)
            totals = totals * factor + jnp.sum(weights_block, axis=-1)
            update = jnp.einsum(
                "grqk,kgd->qgrd",
                weights_block.astype(bf16),
                values_part.reshape(piece_rows, KV_HEADS, HEAD),
                preferred_element_type=f32,
            )
            accumulated = accumulated * jnp.transpose(factor, (2, 0, 1))[..., None] + update
            return (accumulated, new_max, totals)

        return lax.cond(jnp.any(allowed), forward_compute, keep_state, state_in)

    forward_init = (
        jnp.zeros((row_count, KV_HEADS, group_size, HEAD), f32),
        jnp.full((KV_HEADS, group_size, row_count), -1e30, f32),
        jnp.zeros((KV_HEADS, group_size, row_count), f32),
    )
    forward_state = piece_fold(
        forward_step,
        forward_init,
        (
            lax.all_gather(key_rot, "seq", axis=0, tiled=True),
            lax.all_gather(value_low, "seq", axis=0, tiled=True),
            lax.all_gather(doc_ids, "seq", axis=0, tiled=True),
        ),
    )
    accumulated, running, totals = forward_state
    attend_float = accumulated / jnp.transpose(totals, (2, 0, 1))[..., None]
    log_totals = running + jnp.log(totals)
    mixed = attend_float.reshape(row_count, D).astype(bf16)
    middle = x_float + matrix_product(mixed, w_output)
    gain_two_float = gain_two.astype(f32)
    normed_two = normalize(middle, gain_two_float).astype(bf16)
    gate = matrix_product(normed_two, w_gate)
    upward = matrix_product(normed_two, w_up)
    hidden = swish_product(gate, upward).astype(bf16)
    outputs = (middle + matrix_product(hidden, w_down)).astype(bf16)
    feed_back = (
        lax.all_gather(gain_second, ("dp", "seq"), axis=0, tiled=True),
        lax.all_gather(gate_weight, ("dp", "seq"), axis=0, tiled=True),
        lax.all_gather(up_weight, ("dp", "seq"), axis=0, tiled=True),
        lax.all_gather(down_weight, ("dp", "seq"), axis=0, tiled=True),
    )
    attend_back = (
        lax.all_gather(gain_first, ("dp", "seq"), axis=0, tiled=True),
        lax.all_gather(query_weight, ("dp", "seq"), axis=0, tiled=True),
        lax.all_gather(key_weight, ("dp", "seq"), axis=0, tiled=True),
        lax.all_gather(value_weight, ("dp", "seq"), axis=0, tiled=True),
        lax.all_gather(output_weight, ("dp", "seq"), axis=0, tiled=True),
    )
    unused_gain_two, back_gate, back_up, back_down = feed_back
    unused_gain_one, back_query, back_key, back_value, back_output = attend_back
    cot_float = cotangent.astype(f32)
    cot_low = cot_float.astype(bf16)
    down_term = transposed_times(hidden, cot_low)
    grad_hidden = times_transposed(cot_low, back_down)
    unused_swish, swish_back = jax.vjp(swish_product, gate, upward)
    grad_gate, grad_up = swish_back(grad_hidden)
    grad_gate_low = grad_gate.astype(bf16)
    grad_up_low = grad_up.astype(bf16)
    gate_term = transposed_times(normed_two, grad_gate_low)
    up_term = transposed_times(normed_two, grad_up_low)
    grad_normed_two = times_transposed(grad_gate_low, back_gate) + times_transposed(
        grad_up_low, back_up
    )
    unused_norm_two, norm_two_back = jax.vjp(normalize, middle, gain_two_float)
    grad_middle_part, gain_two_term = norm_two_back(grad_normed_two)
    second_grad, gate_grad, up_grad, down_grad = (
        lax.psum_scatter(gain_two_term, ("dp", "seq"), scatter_dimension=0, tiled=True),
        lax.psum_scatter(gate_term, ("dp", "seq"), scatter_dimension=0, tiled=True),
        lax.psum_scatter(up_term, ("dp", "seq"), scatter_dimension=0, tiled=True),
        lax.psum_scatter(down_term, ("dp", "seq"), scatter_dimension=0, tiled=True),
    )
    grad_middle = cot_float + grad_middle_part
    middle_low = grad_middle.astype(bf16)
    output_term = transposed_times(mixed, middle_low)
    grad_mixed = times_transposed(middle_low, back_output).astype(bf16)
    dout_four = grad_mixed.reshape(row_count, KV_HEADS, group_size, HEAD)
    delta_rows = jnp.einsum("qgrd,qgrd->grq", dout_four.astype(f32), attend_float)

    def query_grad_block(allowed, keys_three, values_three):
        logits = (
            jnp.einsum("qgrd,kgd->grqk", query_four, keys_three, preferred_element_type=f32)
            * score_scale
        )
        logits = jnp.where(allowed, logits, -1e30)
        weights_block = jnp.where(allowed, jnp.exp(logits - log_totals[..., None]), 0.0)
        grad_weights = jnp.einsum(
            "qgrd,kgd->grqk", dout_four, values_three, preferred_element_type=f32
        )
        grad_logits = (weights_block * (grad_weights - delta_rows[..., None]) * score_scale).astype(
            bf16
        )
        return (weights_block, grad_logits)

    def query_step(state_in, pieces, first_key):
        keys_part, values_part, docs_part = pieces
        piece_rows = keys_part.shape[0]
        allowed = mask_for(docs_part, first_key, piece_rows)

        def query_compute(grad_query):
            keys_three = keys_part.reshape(piece_rows, KV_HEADS, HEAD)
            values_three = values_part.reshape(piece_rows, KV_HEADS, HEAD)
            unused_weights, grad_logits = query_grad_block(allowed, keys_three, values_three)
            return grad_query + jnp.einsum(
                "grqk,kgd->qgrd", grad_logits, keys_three, preferred_element_type=f32
            )

        return lax.cond(jnp.any(allowed), query_compute, keep_state, state_in)

    grad_query_rot = piece_fold(
        query_step,
        jnp.zeros((row_count, KV_HEADS, group_size, HEAD), f32),
        (
            lax.all_gather(key_rot, "seq", axis=0, tiled=True),
            lax.all_gather(value_low, "seq", axis=0, tiled=True),
            lax.all_gather(doc_ids, "seq", axis=0, tiled=True),
        ),
    )
    lse_rows = jnp.transpose(log_totals, (2, 0, 1)).reshape(row_count, HEADS)
    delta_flat = jnp.transpose(delta_rows, (2, 0, 1)).reshape(row_count, HEADS)
    lse_all, delta_all = (
        lax.all_gather(lse_rows, "seq", axis=0, tiled=True),
        lax.all_gather(delta_flat, "seq", axis=0, tiled=True),
    )
    keys_mine = key_rot.reshape(row_count, KV_HEADS, HEAD)
    values_mine = value_low.reshape(row_count, KV_HEADS, HEAD)

    def key_step(state_in, pieces, first_query):
        queries_part, dout_part, docs_part = pieces
        piece_rows = queries_part.shape[0]
        other_rows = first_query + jnp.arange(piece_rows, dtype=jnp.int32)
        allowed = (query_rows[None, :] <= other_rows[:, None]) & (
            doc_ids[None, :] == docs_part[:, None]
        )

        def key_compute(state_now):
            grad_keys, grad_values = state_now
            lse_part = lax.dynamic_slice_in_dim(lse_all, first_query, piece_rows, 0)
            delta_part = lax.dynamic_slice_in_dim(delta_all, first_query, piece_rows, 0)
            lse_three = jnp.transpose(lse_part.reshape(piece_rows, KV_HEADS, group_size), (1, 2, 0))
            delta_three = jnp.transpose(
                delta_part.reshape(piece_rows, KV_HEADS, group_size), (1, 2, 0)
            )
            queries_four = queries_part.reshape(piece_rows, KV_HEADS, group_size, HEAD)
            douts_four = dout_part.reshape(piece_rows, KV_HEADS, group_size, HEAD)
            logits = (
                jnp.einsum("qgrd,kgd->grqk", queries_four, keys_mine, preferred_element_type=f32)
                * score_scale
            )
            logits = jnp.where(allowed, logits, -1e30)
            weights_block = jnp.where(allowed, jnp.exp(logits - lse_three[..., None]), 0.0)
            grad_weights = jnp.einsum(
                "qgrd,kgd->grqk", douts_four, values_mine, preferred_element_type=f32
            )
            grad_logits = (
                weights_block * (grad_weights - delta_three[..., None]) * score_scale
            ).astype(bf16)
            grad_keys = grad_keys + jnp.einsum(
                "grqk,qgrd->kgd", grad_logits, queries_four, preferred_element_type=f32
            )
            grad_values = grad_values + jnp.einsum(
                "grqk,qgrd->kgd", weights_block.astype(bf16), douts_four, preferred_element_type=f32
            )
            return (grad_keys, grad_values)

        return lax.cond(jnp.any(allowed), key_compute, keep_state, state_in)

    key_init = (
        jnp.zeros((row_count, KV_HEADS, HEAD), f32),
        jnp.zeros((row_count, KV_HEADS, HEAD), f32),
    )
    grad_keys_three, grad_values_three = piece_fold(
        key_step,
        key_init,
        (
            lax.all_gather(query_rot, "seq", axis=0, tiled=True),
            lax.all_gather(grad_mixed, "seq", axis=0, tiled=True),
            lax.all_gather(doc_ids, "seq", axis=0, tiled=True),
        ),
    )
    grad_keys_mine = grad_keys_three.reshape(row_count, kv_width)
    grad_values_mine = grad_values_three.reshape(row_count, kv_width)
    grad_query_low = rotate(grad_query_rot.reshape(row_count, D), positions, HEADS, -1.0).astype(
        bf16
    )
    grad_key_low = rotate(grad_keys_mine, positions, KV_HEADS, -1.0).astype(bf16)
    grad_value_low = grad_values_mine.astype(bf16)
    query_term = transposed_times(normed, grad_query_low)
    key_term_all = transposed_times(normed, grad_key_low)
    value_term_all = transposed_times(normed, grad_value_low)
    grad_normed = (
        times_transposed(grad_query_low, back_query)
        + times_transposed(grad_key_low, back_key)
        + times_transposed(grad_value_low, back_value)
    )
    unused_norm_one, norm_one_back = jax.vjp(normalize, x_float, gain_one_float)
    grad_input_part, gain_one_term = norm_one_back(grad_normed)
    inputs_grad = (grad_middle + grad_input_part).astype(bf16)
    first_grad, query_grad, key_grad, value_grad, output_grad = (
        lax.psum_scatter(gain_one_term, ("dp", "seq"), scatter_dimension=0, tiled=True),
        lax.psum_scatter(query_term, ("dp", "seq"), scatter_dimension=0, tiled=True),
        lax.psum_scatter(key_term_all, ("dp", "seq"), scatter_dimension=0, tiled=True),
        lax.psum_scatter(value_term_all, ("dp", "seq"), scatter_dimension=0, tiled=True),
        lax.psum_scatter(output_term, ("dp", "seq"), scatter_dimension=0, tiled=True),
    )
    return (
        outputs,
        inputs_grad,
        first_grad,
        query_grad,
        key_grad,
        value_grad,
        output_grad,
        second_grad,
        gate_grad,
        up_grad,
        down_grad,
    )

AXES = ("y", "x", "zh", "zl", "c")
SEQUENCE = ("zh", "zl", "c")
PAIR = 2
LANES = 128
QUERY_COLS = PAIR * LANES
PAD_COLS = (PAIR + 2) * LANES
BLOCK = 256
f32 = jnp.float32
bf16 = jnp.bfloat16


def swap(value, axis):
    return lax.ppermute(value, axis, [(0, 1), (1, 0)])


def my_bit(axis):
    return lax.axis_index(axis)


def pick(value, index, axis):
    return lax.dynamic_index_in_dim(value, index, axis, keepdims=False)


def together(*values):
    return lax.optimization_barrier(values)


def paired(mine, other, bit, axis):
    low_first = my_bit(bit) == 0
    return jnp.stack(
        [jnp.where(low_first, mine, other), jnp.where(low_first, other, mine)], axis
    )


def gather_bit(value, bit, axis):
    return paired(value, swap(value, bit), bit, axis)


def halves(value, bit, axis):
    mine = my_bit(bit)
    return pick(value, mine, axis), swap(pick(value, 1 - mine, axis).astype(bf16), bit)


def total(pair):
    return pair[0].astype(f32) + pair[1].astype(f32)


def reduce_bit(value, bit, axis):
    return total(halves(value, bit, axis))


def across(value):
    pairs = []
    for i in range(32):
        y, x, zh, zl, c = (i >> 4) & 1, (i >> 3) & 1, (i >> 2) & 1, (i >> 1) & 1, i & 1
        pairs.append((i, c * 16 + zl * 8 + zh * 4 + x * 2 + y))
    return lax.ppermute(value, AXES, pairs)


def gather_rows(value):
    return lax.all_gather(value, SEQUENCE, axis=0, tiled=True)


def scatter_rows(value):
    return lax.psum_scatter(value, SEQUENCE, scatter_dimension=0, tiled=True)


def exchange(parts):
    return lax.all_to_all(parts, SEQUENCE, 0, 0, tiled=True)


def gather_yx(value):
    rows, cols = value.shape
    low, high = value[:, : cols // 2], value[:, cols // 2 :]
    low = gather_bit(gather_bit(low, "y", 0), "x", 1)
    high = gather_bit(gather_bit(high, "x", 0), "y", 0)
    return low.reshape(4 * rows, -1), high.reshape(4 * rows, -1)


def reduce_one(low, high):
    low = low.reshape(2, 2, -1, low.shape[-1])
    high = high.reshape(2, 2, -1, high.shape[-1])
    return (*halves(low, "y", 0), *halves(high, "x", 1))


def reduce_two(one):
    return (*halves(total(one[:2]), "x", 0), *halves(total(one[2:]), "y", 0))


def reduced(two):
    return jnp.concatenate([total(two[:2]), total(two[2:])], axis=-1)


def dot_nn(left, right):
    return jnp.dot(left, right, preferred_element_type=f32)


def dot_nt(left, right):
    return lax.dot_general(left, right, (((1,), (1,)), ((), ())), preferred_element_type=f32)


def dot_tn(left, right):
    return lax.dot_general(left, right, (((0,), (0,)), ((), ())), preferred_element_type=f32)


def whole(*shape):
    return pl.BlockSpec(shape, lambda i: (0,) * len(shape), pipeline_mode=pl.Buffered(1))


def rows_of(cols):
    return pl.BlockSpec((BLOCK, cols), lambda i: (i, 0))


def call(kernel, steps, in_specs, outs, scratch=(), vmem=60, flops=0):
    return pl.pallas_call(
        kernel,
        grid=(steps,),
        in_specs=in_specs,
        out_specs=[spec for spec, shape, kind in outs],
        out_shape=[jax.ShapeDtypeStruct(shape, kind) for spec, shape, kind in outs],
        scratch_shapes=list(scratch),
        compiler_params=pltpu.CompilerParams(vmem_limit_bytes=vmem * 1024 * 1024),
        cost_estimate=pl.CostEstimate(flops=flops, bytes_accessed=flops // 500, transcendentals=0),
        name=kernel.__name__,
    )


def turn(matrix, cosine, sine):
    return matrix * cosine + pltpu.roll(matrix, LANES // 2, 1) * sine


def head(h):
    return slice(h * LANES, (h + 1) * LANES)


SCALE = 1.0 / math.sqrt(HEAD)
HALF = HEAD // 2


def halves_of_heads(group, each):
    for h in range(each):
        for k in range(2):
            at = ((group * each + h) * 2 + k) * HALF
            to = h * LANES + k * (LANES // 2)
            yield slice(at, at + HALF), slice(to, to + HALF)


GROUPS = [((s & 1) << 2) | (s & 2) | (s >> 2) for s in range(8)]


def pack_heads(gain_ref, q_ref, k_ref, v_ref, out_ref):
    gain = gain_ref[...].astype(f32)
    out_ref[...] = jnp.zeros_like(out_ref)
    for ref, first, each in ((q_ref, 0, PAIR), (k_ref, PAIR, 1), (v_ref, PAIR + 1, 1)):
        scaled = ref[...].astype(f32) * gain
        for s, group in enumerate(GROUPS):
            for at, to in halves_of_heads(group, each):
                to = slice(first * LANES + to.start, first * LANES + to.stop)
                out_ref[s, :, to] = scaled[:, at].astype(bf16)


def unpack_heads(gain_ref, q_ref, k_ref, v_ref, in_ref, dq_ref, dk_ref, dv_ref, dgain_ref):
    gain = gain_ref[...].astype(f32)
    for ref, first, each in ((dq_ref, 0, PAIR), (dk_ref, PAIR, 1), (dv_ref, PAIR + 1, 1)):
        for s, group in enumerate(GROUPS):
            for at, to in halves_of_heads(group, each):
                to = slice(first * LANES + to.start, first * LANES + to.stop)
                ref[:, at] = in_ref[s, :, to].astype(f32) * gain
    sums = 0.0
    for ref, grad_ref in ((q_ref, dq_ref), (k_ref, dk_ref), (v_ref, dv_ref)):
        sums = sums + jnp.sum(ref[...].astype(f32) * grad_ref[...], axis=-1, keepdims=True)
    dgain_ref[...] = sums / gain


def feed_blocks():
    for t in range(8):
        for b in range(4):
            yield t, b, b * 8 + t


def pack_feed(gain_ref, g_ref, u_ref, out_ref):
    gain = gain_ref[...].astype(f32)
    for t, b, i in feed_blocks():
        out_ref[t, :, head(b)] = (g_ref[:, head(i)].astype(f32) * gain).astype(bf16)
        out_ref[t, :, head(4 + b)] = (u_ref[:, head(i)].astype(f32) * gain).astype(bf16)


def unpack_feed(gain_ref, g_ref, u_ref, in_ref, dg_ref, du_ref, dgain_ref):
    gain = gain_ref[...].astype(f32)
    sums = jnp.zeros((gain.shape[0], LANES), f32)
    for t, b, i in feed_blocks():
        gate = in_ref[t, :, head(b)].astype(f32) * gain
        up = in_ref[t, :, head(4 + b)].astype(f32) * gain
        dg_ref[:, head(i)] = gate
        du_ref[:, head(i)] = up
        sums = sums + g_ref[:, head(i)].astype(f32) * gate + u_ref[:, head(i)].astype(f32) * up
    dgain_ref[...] = jnp.sum(sums, axis=-1, keepdims=True) / gain


def project(
    x_ref, wq_ref, wkv_ref, freq_ref, hn_ref, q_ref, k_ref, v_ref, cos_ref, sin_ref, first_ref
):
    x = x_ref[:, :D].astype(f32)
    scale = lax.rsqrt(jnp.mean(x * x, axis=-1, keepdims=True) + norm_epsilon)
    normed = (x * scale).astype(bf16)
    hn_ref[...] = normed
    extra = x_ref[:, D:].astype(f32)
    place = extra[:, 0:1] * 128.0 + extra[:, 1:2]
    at = pl.program_id(0) * BLOCK + lax.broadcasted_iota(jnp.int32, place.shape, 0)
    first_ref[...] = at.astype(f32) - place
    angles = place * freq_ref[...]
    lane = lax.broadcasted_iota(jnp.int32, angles.shape, 1)
    cosine = jnp.cos(angles)
    sine = jnp.sin(angles)
    sine = jnp.where(lane < LANES // 2, -sine, sine)
    cos_ref[...] = cosine
    sin_ref[...] = sine
    full = dot_nn(normed, wq_ref[...])
    for h in range(PAIR):
        q_ref[:, head(h)] = turn(full[:, head(h)], cosine, sine).astype(bf16)
    full = dot_nn(normed, wkv_ref[...])
    k_ref[...] = turn(full[:, :LANES], cosine, sine).astype(bf16)
    v_ref[...] = full[:, LANES:].astype(bf16)


def allowed_pairs(first_ref, first, keys):
    shape = (BLOCK, keys)
    query_at = first + lax.broadcasted_iota(jnp.int32, shape, 0)
    key_at = lax.broadcasted_iota(jnp.int32, shape, 1)
    return (key_at <= query_at) & (key_at.astype(f32) >= first_ref[...])


def attend(q_ref, k_ref, v_ref, first_ref, w_ref, a_ref, lse_ref, o_ref):
    blocks = k_ref.shape[0] // BLOCK

    def run(b):
        keys = (b + 1) * BLOCK
        allowed = allowed_pairs(first_ref, b * BLOCK, keys)
        for h in range(PAIR):
            cols = slice(h * LANES, (h + 1) * LANES)
            logits = dot_nt(q_ref[:, cols], k_ref[:keys, :]) * SCALE
            logits = jnp.where(allowed, logits, -1e30)
            top = jnp.max(logits, axis=-1, keepdims=True)
            weights = jnp.exp(logits - top)
            total = jnp.sum(weights, axis=-1, keepdims=True)
            mixed = dot_nn(weights.astype(bf16), v_ref[:keys, :]) / total
            a_ref[:, cols] = mixed.astype(bf16)
            lse_ref[:, h : h + 1] = top + jnp.log(total)

    for b in range(blocks):
        pl.when(pl.program_id(0) == b)(lambda b=b: run(b))
    o_ref[...] = dot_nn(a_ref[...], w_ref[...]).astype(bf16)


def attend_back(
    mb_ref, w_ref, q_ref, k_ref, v_ref, a_ref, lse_ref, first_ref, cos_ref, sin_ref,
    dq_ref, dkv_ref, dk_acc, dv_acc, dq_acc
):
    step = pl.program_id(0)
    blocks = k_ref.shape[0] // BLOCK

    @pl.when(step == 0)
    def _():
        dk_acc[...] = jnp.zeros_like(dk_acc)
        dv_acc[...] = jnp.zeros_like(dv_acc)

    grad_mixed = dot_nt(mb_ref[...], w_ref[...]).astype(bf16)

    def run(b):
        keys = (b + 1) * BLOCK
        allowed = allowed_pairs(first_ref, b * BLOCK, keys)
        for h in range(PAIR):
            cols = slice(h * LANES, (h + 1) * LANES)
            query = q_ref[:, cols]
            grad = grad_mixed[:, cols]
            delta = jnp.sum(
                grad.astype(f32) * a_ref[:, cols].astype(f32), axis=-1, keepdims=True
            )
            logits = dot_nt(query, k_ref[:keys, :]) * SCALE
            logits = jnp.where(allowed, logits, -1e30)
            weights = jnp.exp(logits - lse_ref[:, h : h + 1])
            grad_weights = dot_nt(grad, v_ref[:keys, :])
            grad_logits = (weights * (grad_weights - delta) * SCALE).astype(bf16)
            dq_acc[:, cols] = dot_nn(grad_logits, k_ref[:keys, :])
            dk_acc[:keys, :] += dot_tn(grad_logits, query)
            dv_acc[:keys, :] += dot_tn(weights.astype(bf16), grad)

    for b in range(blocks):
        pl.when(step == b)(lambda b=b: run(b))

    rows = pl.ds(pl.multiple_of(step * BLOCK, BLOCK), BLOCK)
    for h in range(PAIR):
        cols = slice(h * LANES, (h + 1) * LANES)
        dq_ref[:, cols] = turn(dq_acc[:, cols], cos_ref[rows, :], -sin_ref[rows, :]).astype(bf16)

    @pl.when(step == blocks - 1)
    def _():
        dkv_ref[:, :LANES] = turn(dk_acc[...], cos_ref[...], -sin_ref[...]).astype(bf16)
        dkv_ref[:, LANES:] = dv_acc[...].astype(bf16)


def feed(
    hn_ref, cb_ref, wg_ref, wu_ref, low_ref, high_ref, f_ref, dg_ref, du_ref, o_ref, e_ref
):
    middle = D // 2
    gate = dot_nn(hn_ref[...], wg_ref[...])
    up = dot_nn(hn_ref[...], wu_ref[...])
    sig = 1.0 / (1.0 + jnp.exp(-gate))
    swish = gate * sig
    inner = (swish * up).astype(bf16)
    f_ref[...] = inner
    o_ref[:, :middle] = dot_nn(inner, low_ref[...]).astype(bf16)
    o_ref[:, middle:] = dot_nn(inner, high_ref[...]).astype(bf16)
    grad = dot_nt(cb_ref[:, :middle], low_ref[...]) + dot_nt(cb_ref[:, middle:], high_ref[...])
    dg_ref[...] = (grad * up * sig * (1.0 + gate * (1.0 - sig))).astype(bf16)
    du_ref[...] = (grad * swish).astype(bf16)
    back = dot_nt(dg_ref[...], wg_ref[...]) + dot_nt(du_ref[...], wu_ref[...])
    e_ref[...] = back.astype(bf16)


def inverse_norm(values):
    return lax.rsqrt(jnp.mean(values * values, axis=-1, keepdims=True) + norm_epsilon)


def norm_back(values, inverse, grad):
    return inverse * grad - values * inverse**3 * jnp.mean(grad * values, axis=-1, keepdims=True)


def body_fast(
    inputs,
    cotangent,
    doc_ids,
    positions,
    gain_first,
    query_weight,
    key_weight,
    value_weight,
    output_weight,
    gain_second,
    gate_weight,
    up_weight,
    down_weight,
):
    rows = inputs.shape[0]
    own = query_weight.shape[0]
    hidden_block = down_weight.shape[0]
    width = 4 * hidden_block
    total_rows = 8 * rows
    steps = total_rows // BLOCK
    gain_one = gain_first.reshape(own, 1)
    gain_two = gain_second.reshape(own, 1)

    marks = jnp.stack([positions // 128, positions % 128], axis=1).astype(bf16)
    marks = jnp.pad(marks, ((0, 0), (0, LANES - 2)))
    marked = jnp.concatenate([inputs, marks], axis=1)

    heads_in = [whole(own, 1), whole(own, D), whole(own, D // 2), whole(own, D // 2)]
    feed_in = [whole(own, 1), whole(own, 8 * width), whole(own, 8 * width)]
    (parts,) = call(
        pack_heads, 1, heads_in, [(whole(8, own, PAD_COLS), (8, own, PAD_COLS), bf16)]
    )(gain_one, query_weight, key_weight, value_weight)
    (both,) = call(
        pack_feed, 1, feed_in, [(whole(8, own, 2 * width), (8, own, 2 * width), bf16)]
    )(gain_two, gate_weight, up_weight)
    rows_all = gather_rows(marked)
    w_out = gather_bit(gather_bit(output_weight, "c", 0), "zl", 0)
    parts, both, w_out, cotangent = together(exchange(parts), both, w_out, cotangent)
    cot_all = gather_rows(cotangent)
    parts = parts.reshape(8 * own, PAD_COLS)
    w_query, w_kv = parts[:, :QUERY_COLS], parts[:, QUERY_COLS:]
    w_query, w_kv = together(gather_bit(w_query, "y", 0), gather_bit(w_kv, "x", 0))
    w_query = gather_bit(w_query, "x", 1).reshape(D, QUERY_COLS)
    w_kv = gather_bit(w_kv, "y", 0).reshape(D, 2 * LANES)
    w_out = across(w_out)
    rows_all, w_query, w_kv, w_out, both = together(rows_all, w_query, w_kv, w_out, both)
    w_out = jnp.pad(w_out, ((0, 0), (0, 0), (0, LANES // 2 - own), (0, 0)))
    w_out = w_out.reshape(QUERY_COLS, D)

    lane = jnp.arange(LANES) % (LANES // 2)
    freq = rotary_base ** (-lane.astype(f32) * 2.0 / HEAD)
    freq = jnp.where(lane < HALF, freq, 0.0).reshape(1, LANES)

    def rows_out(cols, kind):
        return (rows_of(cols), (total_rows, cols), kind)

    normed, query, key, value, cosine, sine, row_first = call(
        project,
        steps,
        [rows_of(D + LANES), whole(D, QUERY_COLS), whole(D, 2 * LANES), whole(1, LANES)],
        [
            rows_out(D, bf16),
            rows_out(QUERY_COLS, bf16),
            rows_out(LANES, bf16),
            rows_out(LANES, bf16),
            rows_out(LANES, f32),
            rows_out(LANES, f32),
            rows_out(1, f32),
        ],
        flops=3 << 30,
    )(rows_all, w_query, w_kv, freq)
    mixed, lse, term = call(
        attend,
        steps,
        [
            rows_of(QUERY_COLS),
            whole(total_rows, LANES),
            whole(total_rows, LANES),
            rows_of(1),
            whole(QUERY_COLS, D),
        ],
        [rows_out(QUERY_COLS, bf16), rows_out(PAIR, f32), rows_out(D, bf16)],
        flops=6 << 30,
    )(query, key, value, row_first, w_out)
    term, both, cot_all, down_weight = together(term, exchange(both), cot_all, down_weight)
    attended = scatter_rows(term)
    both = both.reshape(8 * own, 2 * width)
    attended, feed_low, feed_high, down_weight = together(
        attended,
        gather_bit(both[:, :width], "y", 0),
        gather_bit(both[:, width:], "x", 0),
        down_weight,
    )
    x_float = inputs.astype(f32)
    middle = x_float + attended.astype(f32)

    inverse_two = inverse_norm(middle)
    normed_two = gather_rows((middle * inverse_two).astype(bf16))
    w_gate = gather_bit(feed_low, "x", 1).reshape(D, width)
    w_up = gather_bit(feed_high, "y", 0).reshape(D, width)
    w_down = gather_yx(down_weight)
    normed_two, w_gate, w_up, *w_down = together(normed_two, w_gate, w_up, *w_down)
    inner, grad_gate, grad_up, out_term, back_term = call(
        feed,
        steps,
        [
            rows_of(D),
            rows_of(D),
            whole(D, width),
            whole(D, width),
            whole(width, D // 2),
            whole(width, D // 2),
        ],
        [
            rows_out(width, bf16),
            rows_out(width, bf16),
            rows_out(width, bf16),
            rows_out(D, bf16),
            rows_out(D, bf16),
        ],
    )(normed_two, cot_all, w_gate, w_up, *w_down)
    back_two = scatter_rows(back_term)
    inner, normed_two, out_term, back_term = together(inner, normed_two, out_term, back_term)
    feed_one = reduce_one(
        dot_tn(normed_two, grad_gate).astype(bf16), dot_tn(normed_two, grad_up).astype(bf16)
    )
    down_one = reduce_one(
        dot_tn(inner, cot_all[:, : D // 2]).astype(bf16),
        dot_tn(inner, cot_all[:, D // 2 :]).astype(bf16),
    )
    back_two, *rest = together(back_two, *feed_one, *down_one)
    feed_one, down_one = rest[:4], rest[4:]
    cot_float = cotangent.astype(f32)
    grad_middle = cot_float + norm_back(middle, inverse_two, back_two.astype(f32))
    middle_all = gather_rows(grad_middle.astype(bf16))
    feed_two, down_two = reduce_two(feed_one), reduce_two(down_one)
    feed_two = together(*feed_two)
    both_sum = exchange(reduced(feed_two).astype(bf16).reshape(8, own, 2 * width))
    middle_all, out_term, both_sum, *down_two = together(
        middle_all, out_term, both_sum, *down_two
    )
    outputs = scatter_rows(out_term)

    grad_query, grad_kv = call(
        attend_back,
        steps,
        [
            rows_of(D),
            whole(QUERY_COLS, D),
            rows_of(QUERY_COLS),
            whole(total_rows, LANES),
            whole(total_rows, LANES),
            rows_of(QUERY_COLS),
            rows_of(PAIR),
            rows_of(1),
            whole(total_rows, LANES),
            whole(total_rows, LANES),
        ],
        [
            rows_out(QUERY_COLS, bf16),
            (whole(total_rows, 2 * LANES), (total_rows, 2 * LANES), bf16),
        ],
        scratch=[
            pltpu.VMEM((total_rows, LANES), f32),
            pltpu.VMEM((total_rows, LANES), f32),
            pltpu.VMEM((BLOCK, QUERY_COLS), f32),
        ],
        flops=6 << 30,
    )(middle_all, w_out, query, key, value, mixed, lse, row_first, cosine, sine)
    first_term = (dot_nt(grad_query, w_query) + dot_nt(grad_kv, w_kv)).astype(bf16)
    head_one = reduce_one(
        dot_tn(normed, grad_query).astype(bf16), dot_tn(normed, grad_kv).astype(bf16)
    )
    head_two = reduce_two(together(*head_one))
    first_term, outputs, mixed, *rest = together(first_term, outputs, mixed, *head_two, *down_two)
    head_two, down_two = rest[:4], rest[4:]
    first_sum = scatter_rows(first_term).astype(f32)
    head_term = exchange(reduced(head_two).astype(bf16).reshape(8, own, PAD_COLS))
    out_part = dot_tn(mixed, middle_all).astype(bf16).reshape(2, 2, LANES // 2, D)[:, :, :own]
    head_term, *out_pair = together(head_term, *halves(out_part, "y", 1))
    out_pair = halves(total(out_pair), "x", 0)
    output_grad = across(total(out_pair).astype(bf16)).astype(f32)
    down_grad = reduced(down_two)
    outputs = (middle + outputs.astype(f32)).astype(bf16)
    inputs_grad = (grad_middle + norm_back(x_float, inverse_norm(x_float), first_sum)).astype(bf16)

    wide = (whole(own, 8 * width), (own, 8 * width), f32)
    column = (whole(own, 1), (own, 1), f32)
    gate_grad, up_grad, second_grad = call(
        unpack_feed,
        1,
        [*feed_in, whole(8, own, 2 * width)],
        [wide, wide, column],
    )(gain_two, gate_weight, up_weight, both_sum)
    query_grad, key_grad, value_grad, first_grad = call(
        unpack_heads,
        1,
        [*heads_in, whole(8, own, PAD_COLS)],
        [
            (whole(own, D), (own, D), f32),
            (whole(own, D // 2), (own, D // 2), f32),
            (whole(own, D // 2), (own, D // 2), f32),
            column,
        ],
    )(gain_one, query_weight, key_weight, value_weight, head_term)
    return (
        outputs,
        inputs_grad,
        first_grad.reshape(own),
        query_grad,
        key_grad,
        value_grad,
        output_grad,
        second_grad.reshape(own),
        gate_grad,
        up_grad,
        down_grad,
    )


def solution(mesh):
    shape = dict(mesh.shape)
    step, axes = body, ("dp", "seq")
    if shape["dp"] == 4 and shape["seq"] == KV_HEADS:
        step, axes = body_fast, AXES
        mesh = Mesh(mesh.devices.reshape(2, 2, 2, 2, 2), AXES)
    wide, line = P(axes, None), P(axes)
    return jax.shard_map(
        step,
        mesh=mesh,
        in_specs=(wide, wide, line, line, line, wide, wide, wide, wide, line, wide, wide, wide),
        out_specs=(wide, wide, line, wide, wide, wide, wide, line, wide, wide, wide),
        check_vma=False,
    )
```

```python
import math

import jax
import jax.numpy as jnp
from jax import lax
from jax.experimental import pallas as pl
from jax.experimental.pallas import tpu as pltpu
from jax.sharding import Mesh, PartitionSpec as P

D = 1536
HEADS = 16
KV_HEADS = 8
HEAD = 96


norm_epsilon = 1e-05
rotary_base = 100000.0


def normalize(values_in, gain):
    return (
        values_in
        * lax.rsqrt(jnp.mean(values_in * values_in, axis=-1, keepdims=True) + norm_epsilon)
        * gain
    )


def swish_product(gate, upward):
    return jax.nn.silu(gate) * upward


def rotate(matrix, positions, heads_count, direction):
    halfway = HEAD // 2
    inverse_freq = rotary_base ** (-jnp.arange(halfway, dtype=jnp.float32) * 2.0 / HEAD)
    angles = positions.astype(jnp.float32)[:, None] * inverse_freq[None, :]
    cosine = jnp.cos(angles)[:, None, :]
    sine_table = direction * jnp.sin(angles)[:, None, :]
    shaped = matrix.reshape(matrix.shape[0], heads_count, HEAD)
    first_half = shaped[..., :halfway]
    second_half = shaped[..., halfway:]
    turned = jnp.concatenate(
        [
            first_half * cosine - second_half * sine_table,
            second_half * cosine + first_half * sine_table,
        ],
        axis=-1,
    )
    return turned.reshape(matrix.shape)


def times_transposed(left, right):
    return lax.dot_general(
        left, right, (((1,), (1,)), ((), ())), preferred_element_type=jnp.float32
    )


def transposed_times(left, right):
    return lax.dot_general(
        left, right, (((0,), (0,)), ((), ())), preferred_element_type=jnp.float32
    )


def matrix_product(left, right):
    return jnp.dot(left, right, preferred_element_type=jnp.float32)


def block_rows(total_rows):
    size_rows = min(total_rows, 1024)
    while total_rows % size_rows:
        size_rows -= 1
    return size_rows


def fold_local(block_step, initial, arrays):
    total_rows = arrays[0].shape[0]
    size_rows = block_rows(total_rows)

    def one_turn(turn_index, state_in):
        begin_row = turn_index * size_rows
        pieces = tuple(
            (lax.dynamic_slice_in_dim(member, begin_row, size_rows, 0) for member in arrays)
        )
        return block_step(state_in, pieces, begin_row)

    return lax.fori_loop(0, total_rows // size_rows, one_turn, initial)


def piece_fold(block_step, state_in, pieces):
    return fold_local(block_step, state_in, pieces)


def keep_state(state_now):
    return state_now


def body(
    inputs,
    cotangent,
    doc_ids,
    positions,
    gain_first,
    query_weight,
    key_weight,
    value_weight,
    output_weight,
    gain_second,
    gate_weight,
    up_weight,
    down_weight,
):
    f32 = jnp.float32
    bf16 = jnp.bfloat16
    attend_set = (
        lax.all_gather(gain_first, ("dp", "seq"), axis=0, tiled=True),
        lax.all_gather(query_weight, ("dp", "seq"), axis=0, tiled=True),
        lax.all_gather(key_weight, ("dp", "seq"), axis=0, tiled=True),
        lax.all_gather(value_weight, ("dp", "seq"), axis=0, tiled=True),
        lax.all_gather(output_weight, ("dp", "seq"), axis=0, tiled=True),
    )
    feed_set = (
        lax.all_gather(gain_second, ("dp", "seq"), axis=0, tiled=True),
        lax.all_gather(gate_weight, ("dp", "seq"), axis=0, tiled=True),
        lax.all_gather(up_weight, ("dp", "seq"), axis=0, tiled=True),
        lax.all_gather(down_weight, ("dp", "seq"), axis=0, tiled=True),
    )
    gain_one, w_query, w_key, w_value, w_output = attend_set
    gain_two, w_gate, w_up, w_down = feed_set
    row_count = inputs.shape[0]
    group_size = HEADS // KV_HEADS
    kv_width = KV_HEADS * HEAD
    score_scale = 1.0 / math.sqrt(HEAD)
    query_rows = lax.axis_index("seq") * row_count + jnp.arange(row_count, dtype=jnp.int32)
    x_float = inputs.astype(f32)
    gain_one_float = gain_one.astype(f32)
    normed = normalize(x_float, gain_one_float).astype(bf16)
    query_rot = rotate(matrix_product(normed, w_query), positions, HEADS, 1.0).astype(bf16)
    key_rot = rotate(matrix_product(normed, w_key), positions, KV_HEADS, 1.0).astype(bf16)
    value_low = matrix_product(normed, w_value).astype(bf16)
    query_four = query_rot.reshape(row_count, KV_HEADS, group_size, HEAD)

    def mask_for(docs_part, first_key, piece_rows):
        key_rows = first_key + jnp.arange(piece_rows, dtype=jnp.int32)
        return (key_rows[None, :] <= query_rows[:, None]) & (docs_part[None, :] == doc_ids[:, None])

    def forward_step(state_in, pieces, first_key):
        keys_part, values_part, docs_part = pieces
        piece_rows = keys_part.shape[0]
        allowed = mask_for(docs_part, first_key, piece_rows)

        def forward_compute(state_now):
            accumulated, running, totals = state_now
            logits = (
                jnp.einsum(
                    "qgrd,kgd->grqk",
                    query_four,
                    keys_part.reshape(piece_rows, KV_HEADS, HEAD),
                    preferred_element_type=f32,
                )
                * score_scale
            )
            logits = jnp.where(allowed, logits, -1e30)
            new_max = jnp.maximum(running, jnp.max(logits, axis=-1))
            weights_block = jnp.where(allowed, jnp.exp(logits - new_max[..., None]), 0.0)
            factor = jnp.exp(running - new_max)
            totals = totals * factor + jnp.sum(weights_block, axis=-1)
            update = jnp.einsum(
                "grqk,kgd->qgrd",
                weights_block.astype(bf16),
                values_part.reshape(piece_rows, KV_HEADS, HEAD),
                preferred_element_type=f32,
            )
            accumulated = accumulated * jnp.transpose(factor, (2, 0, 1))[..., None] + update
            return (accumulated, new_max, totals)

        return lax.cond(jnp.any(allowed), forward_compute, keep_state, state_in)

    forward_init = (
        jnp.zeros((row_count, KV_HEADS, group_size, HEAD), f32),
        jnp.full((KV_HEADS, group_size, row_count), -1e30, f32),
        jnp.zeros((KV_HEADS, group_size, row_count), f32),
    )
    forward_state = piece_fold(
        forward_step,
        forward_init,
        (
            lax.all_gather(key_rot, "seq", axis=0, tiled=True),
            lax.all_gather(value_low, "seq", axis=0, tiled=True),
            lax.all_gather(doc_ids, "seq", axis=0, tiled=True),
        ),
    )
    accumulated, running, totals = forward_state
    attend_float = accumulated / jnp.transpose(totals, (2, 0, 1))[..., None]
    log_totals = running + jnp.log(totals)
    mixed = attend_float.reshape(row_count, D).astype(bf16)
    middle = x_float + matrix_product(mixed, w_output)
    gain_two_float = gain_two.astype(f32)
    normed_two = normalize(middle, gain_two_float).astype(bf16)
    gate = matrix_product(normed_two, w_gate)
    upward = matrix_product(normed_two, w_up)
    hidden = swish_product(gate, upward).astype(bf16)
    outputs = (middle + matrix_product(hidden, w_down)).astype(bf16)
    feed_back = (
        lax.all_gather(gain_second, ("dp", "seq"), axis=0, tiled=True),
        lax.all_gather(gate_weight, ("dp", "seq"), axis=0, tiled=True),
        lax.all_gather(up_weight, ("dp", "seq"), axis=0, tiled=True),
        lax.all_gather(down_weight, ("dp", "seq"), axis=0, tiled=True),
    )
    attend_back = (
        lax.all_gather(gain_first, ("dp", "seq"), axis=0, tiled=True),
        lax.all_gather(query_weight, ("dp", "seq"), axis=0, tiled=True),
        lax.all_gather(key_weight, ("dp", "seq"), axis=0, tiled=True),
        lax.all_gather(value_weight, ("dp", "seq"), axis=0, tiled=True),
        lax.all_gather(output_weight, ("dp", "seq"), axis=0, tiled=True),
    )
    unused_gain_two, back_gate, back_up, back_down = feed_back
    unused_gain_one, back_query, back_key, back_value, back_output = attend_back
    cot_float = cotangent.astype(f32)
    cot_low = cot_float.astype(bf16)
    down_term = transposed_times(hidden, cot_low)
    grad_hidden = times_transposed(cot_low, back_down)
    unused_swish, swish_back = jax.vjp(swish_product, gate, upward)
    grad_gate, grad_up = swish_back(grad_hidden)
    grad_gate_low = grad_gate.astype(bf16)
    grad_up_low = grad_up.astype(bf16)
    gate_term = transposed_times(normed_two, grad_gate_low)
    up_term = transposed_times(normed_two, grad_up_low)
    grad_normed_two = times_transposed(grad_gate_low, back_gate) + times_transposed(
        grad_up_low, back_up
    )
    unused_norm_two, norm_two_back = jax.vjp(normalize, middle, gain_two_float)
    grad_middle_part, gain_two_term = norm_two_back(grad_normed_two)
    second_grad, gate_grad, up_grad, down_grad = (
        lax.psum_scatter(gain_two_term, ("dp", "seq"), scatter_dimension=0, tiled=True),
        lax.psum_scatter(gate_term, ("dp", "seq"), scatter_dimension=0, tiled=True),
        lax.psum_scatter(up_term, ("dp", "seq"), scatter_dimension=0, tiled=True),
        lax.psum_scatter(down_term, ("dp", "seq"), scatter_dimension=0, tiled=True),
    )
    grad_middle = cot_float + grad_middle_part
    middle_low = grad_middle.astype(bf16)
    output_term = transposed_times(mixed, middle_low)
    grad_mixed = times_transposed(middle_low, back_output).astype(bf16)
    dout_four = grad_mixed.reshape(row_count, KV_HEADS, group_size, HEAD)
    delta_rows = jnp.einsum("qgrd,qgrd->grq", dout_four.astype(f32), attend_float)

    def query_grad_block(allowed, keys_three, values_three):
        logits = (
            jnp.einsum("qgrd,kgd->grqk", query_four, keys_three, preferred_element_type=f32)
            * score_scale
        )
        logits = jnp.where(allowed, logits, -1e30)
        weights_block = jnp.where(allowed, jnp.exp(logits - log_totals[..., None]), 0.0)
        grad_weights = jnp.einsum(
            "qgrd,kgd->grqk", dout_four, values_three, preferred_element_type=f32
        )
        grad_logits = (weights_block * (grad_weights - delta_rows[..., None]) * score_scale).astype(
            bf16
        )
        return (weights_block, grad_logits)

    def query_step(state_in, pieces, first_key):
        keys_part, values_part, docs_part = pieces
        piece_rows = keys_part.shape[0]
        allowed = mask_for(docs_part, first_key, piece_rows)

        def query_compute(grad_query):
            keys_three = keys_part.reshape(piece_rows, KV_HEADS, HEAD)
            values_three = values_part.reshape(piece_rows, KV_HEADS, HEAD)
            unused_weights, grad_logits = query_grad_block(allowed, keys_three, values_three)
            return grad_query + jnp.einsum(
                "grqk,kgd->qgrd", grad_logits, keys_three, preferred_element_type=f32
            )

        return lax.cond(jnp.any(allowed), query_compute, keep_state, state_in)

    grad_query_rot = piece_fold(
        query_step,
        jnp.zeros((row_count, KV_HEADS, group_size, HEAD), f32),
        (
            lax.all_gather(key_rot, "seq", axis=0, tiled=True),
            lax.all_gather(value_low, "seq", axis=0, tiled=True),
            lax.all_gather(doc_ids, "seq", axis=0, tiled=True),
        ),
    )
    lse_rows = jnp.transpose(log_totals, (2, 0, 1)).reshape(row_count, HEADS)
    delta_flat = jnp.transpose(delta_rows, (2, 0, 1)).reshape(row_count, HEADS)
    lse_all, delta_all = (
        lax.all_gather(lse_rows, "seq", axis=0, tiled=True),
        lax.all_gather(delta_flat, "seq", axis=0, tiled=True),
    )
    keys_mine = key_rot.reshape(row_count, KV_HEADS, HEAD)
    values_mine = value_low.reshape(row_count, KV_HEADS, HEAD)

    def key_step(state_in, pieces, first_query):
        queries_part, dout_part, docs_part = pieces
        piece_rows = queries_part.shape[0]
        other_rows = first_query + jnp.arange(piece_rows, dtype=jnp.int32)
        allowed = (query_rows[None, :] <= other_rows[:, None]) & (
            doc_ids[None, :] == docs_part[:, None]
        )

        def key_compute(state_now):
            grad_keys, grad_values = state_now
            lse_part = lax.dynamic_slice_in_dim(lse_all, first_query, piece_rows, 0)
            delta_part = lax.dynamic_slice_in_dim(delta_all, first_query, piece_rows, 0)
            lse_three = jnp.transpose(lse_part.reshape(piece_rows, KV_HEADS, group_size), (1, 2, 0))
            delta_three = jnp.transpose(
                delta_part.reshape(piece_rows, KV_HEADS, group_size), (1, 2, 0)
            )
            queries_four = queries_part.reshape(piece_rows, KV_HEADS, group_size, HEAD)
            douts_four = dout_part.reshape(piece_rows, KV_HEADS, group_size, HEAD)
            logits = (
                jnp.einsum("qgrd,kgd->grqk", queries_four, keys_mine, preferred_element_type=f32)
                * score_scale
            )
            logits = jnp.where(allowed, logits, -1e30)
            weights_block = jnp.where(allowed, jnp.exp(logits - lse_three[..., None]), 0.0)
            grad_weights = jnp.einsum(
                "qgrd,kgd->grqk", douts_four, values_mine, preferred_element_type=f32
            )
            grad_logits = (
                weights_block * (grad_weights - delta_three[..., None]) * score_scale
            ).astype(bf16)
            grad_keys = grad_keys + jnp.einsum(
                "grqk,qgrd->kgd", grad_logits, queries_four, preferred_element_type=f32
            )
            grad_values = grad_values + jnp.einsum(
                "grqk,qgrd->kgd", weights_block.astype(bf16), douts_four, preferred_element_type=f32
            )
            return (grad_keys, grad_values)

        return lax.cond(jnp.any(allowed), key_compute, keep_state, state_in)

    key_init = (
        jnp.zeros((row_count, KV_HEADS, HEAD), f32),
        jnp.zeros((row_count, KV_HEADS, HEAD), f32),
    )
    grad_keys_three, grad_values_three = piece_fold(
        key_step,
        key_init,
        (
            lax.all_gather(query_rot, "seq", axis=0, tiled=True),
            lax.all_gather(grad_mixed, "seq", axis=0, tiled=True),
            lax.all_gather(doc_ids, "seq", axis=0, tiled=True),
        ),
    )
    grad_keys_mine = grad_keys_three.reshape(row_count, kv_width)
    grad_values_mine = grad_values_three.reshape(row_count, kv_width)
    grad_query_low = rotate(grad_query_rot.reshape(row_count, D), positions, HEADS, -1.0).astype(
        bf16
    )
    grad_key_low = rotate(grad_keys_mine, positions, KV_HEADS, -1.0).astype(bf16)
    grad_value_low = grad_values_mine.astype(bf16)
    query_term = transposed_times(normed, grad_query_low)
    key_term_all = transposed_times(normed, grad_key_low)
    value_term_all = transposed_times(normed, grad_value_low)
    grad_normed = (
        times_transposed(grad_query_low, back_query)
        + times_transposed(grad_key_low, back_key)
        + times_transposed(grad_value_low, back_value)
    )
    unused_norm_one, norm_one_back = jax.vjp(normalize, x_float, gain_one_float)
    grad_input_part, gain_one_term = norm_one_back(grad_normed)
    inputs_grad = (grad_middle + grad_input_part).astype(bf16)
    first_grad, query_grad, key_grad, value_grad, output_grad = (
        lax.psum_scatter(gain_one_term, ("dp", "seq"), scatter_dimension=0, tiled=True),
        lax.psum_scatter(query_term, ("dp", "seq"), scatter_dimension=0, tiled=True),
        lax.psum_scatter(key_term_all, ("dp", "seq"), scatter_dimension=0, tiled=True),
        lax.psum_scatter(value_term_all, ("dp", "seq"), scatter_dimension=0, tiled=True),
        lax.psum_scatter(output_term, ("dp", "seq"), scatter_dimension=0, tiled=True),
    )
    return (
        outputs,
        inputs_grad,
        first_grad,
        query_grad,
        key_grad,
        value_grad,
        output_grad,
        second_grad,
        gate_grad,
        up_grad,
        down_grad,
    )

AXES = ("y", "x", "zh", "zl", "c")
SEQUENCE = ("zh", "zl", "c")
PAIR = 2
LANES = 128
QUERY_COLS = PAIR * LANES
PAD_COLS = (PAIR + 2) * LANES
BLOCK = 256
MAIN = 3 * D // 4
REST = D - MAIN
f32 = jnp.float32
bf16 = jnp.bfloat16


def swap(value, axis):
    return lax.ppermute(value, axis, [(0, 1), (1, 0)])


def my_bit(axis):
    return lax.axis_index(axis)


def pick(value, index, axis):
    return lax.dynamic_index_in_dim(value, index, axis, keepdims=False)


def together(*values):
    return lax.optimization_barrier(values)


def paired(mine, other, bit, axis):
    low_first = my_bit(bit) == 0
    return jnp.stack(
        [jnp.where(low_first, mine, other), jnp.where(low_first, other, mine)], axis
    )


def gather_bit(value, bit, axis):
    return paired(value, swap(value, bit), bit, axis)


def halves(value, bit, axis):
    mine = my_bit(bit)
    return pick(value, mine, axis), swap(pick(value, 1 - mine, axis).astype(bf16), bit)


def total(pair):
    return pair[0].astype(f32) + pair[1].astype(f32)


def reduce_bit(value, bit, axis):
    return total(halves(value, bit, axis))


def across(value):
    pairs = []
    for i in range(32):
        y, x, zh, zl, c = (i >> 4) & 1, (i >> 3) & 1, (i >> 2) & 1, (i >> 1) & 1, i & 1
        pairs.append((i, c * 16 + zl * 8 + zh * 4 + x * 2 + y))
    return lax.ppermute(value, AXES, pairs)


def gather_rows(value):
    return lax.all_gather(value, SEQUENCE, axis=0, tiled=True)


def scatter_rows(value):
    return lax.psum_scatter(value, SEQUENCE, scatter_dimension=0, tiled=True)


def gather_line(value):
    value = gather_bit(gather_bit(gather_bit(value, "zh", 0), "zl", 1), "c", 2)
    return value.reshape(-1, value.shape[-1])


def scatter_line(value):
    value = value.reshape(2, 2, 2, value.shape[0] // 8, -1)
    return reduce_bit(reduce_bit(reduce_bit(value, "c", 2), "zl", 1), "zh", 0)


def gather_split(value):
    return gather_rows(value[:, :MAIN]), gather_line(value[:, MAIN:])


def scatter_split(main, rest):
    return scatter_rows(main), scatter_line(rest)


def joined(main, rest):
    return jnp.concatenate([main.astype(f32), rest], axis=-1)


def exchange(parts):
    return lax.all_to_all(parts, SEQUENCE, 0, 0, tiled=True)


def gather_yx(value):
    rows, cols = value.shape
    low, high = value[:, : cols // 2], value[:, cols // 2 :]
    low = gather_bit(gather_bit(low, "y", 0), "x", 1)
    high = gather_bit(gather_bit(high, "x", 0), "y", 0)
    return low.reshape(4 * rows, -1), high.reshape(4 * rows, -1)


def reduce_one(low, high):
    low = low.reshape(2, 2, -1, low.shape[-1])
    high = high.reshape(2, 2, -1, high.shape[-1])
    return (*halves(low, "y", 0), *halves(high, "x", 1))


def reduce_two(one):
    return (*halves(total(one[:2]), "x", 0), *halves(total(one[2:]), "y", 0))


def reduced(two):
    return jnp.concatenate([total(two[:2]), total(two[2:])], axis=-1)


def dot_nn(left, right):
    return jnp.dot(left, right, preferred_element_type=f32)


def dot_nt(left, right):
    return lax.dot_general(left, right, (((1,), (1,)), ((), ())), preferred_element_type=f32)


def dot_tn(left, right):
    return lax.dot_general(left, right, (((0,), (0,)), ((), ())), preferred_element_type=f32)


def whole(*shape):
    return pl.BlockSpec(shape, lambda i: (0,) * len(shape), pipeline_mode=pl.Buffered(1))


def rows_of(cols):
    return pl.BlockSpec((BLOCK, cols), lambda i: (i, 0))


def call(kernel, steps, in_specs, outs, scratch=(), vmem=60, flops=0):
    return pl.pallas_call(
        kernel,
        grid=(steps,),
        in_specs=in_specs,
        out_specs=[spec for spec, shape, kind in outs],
        out_shape=[jax.ShapeDtypeStruct(shape, kind) for spec, shape, kind in outs],
        scratch_shapes=list(scratch),
        compiler_params=pltpu.CompilerParams(vmem_limit_bytes=vmem * 1024 * 1024),
        cost_estimate=pl.CostEstimate(flops=flops, bytes_accessed=flops // 500, transcendentals=0),
        name=kernel.__name__,
    )


def turn(matrix, cosine, sine):
    return matrix * cosine + pltpu.roll(matrix, LANES // 2, 1) * sine


def head(h):
    return slice(h * LANES, (h + 1) * LANES)


SCALE = 1.0 / math.sqrt(HEAD)
HALF = HEAD // 2


def halves_of_heads(group, each):
    for h in range(each):
        for k in range(2):
            at = ((group * each + h) * 2 + k) * HALF
            to = h * LANES + k * (LANES // 2)
            yield slice(at, at + HALF), slice(to, to + HALF)


GROUPS = [((s & 1) << 2) | (s & 2) | (s >> 2) for s in range(8)]


def pack_heads(gain_ref, q_ref, k_ref, v_ref, out_ref):
    gain = gain_ref[...].astype(f32)
    out_ref[...] = jnp.zeros_like(out_ref)
    for ref, first, each in ((q_ref, 0, PAIR), (k_ref, PAIR, 1), (v_ref, PAIR + 1, 1)):
        scaled = ref[...].astype(f32) * gain
        for s, group in enumerate(GROUPS):
            for at, to in halves_of_heads(group, each):
                to = slice(first * LANES + to.start, first * LANES + to.stop)
                out_ref[s, :, to] = scaled[:, at].astype(bf16)


def unpack_heads(gain_ref, q_ref, k_ref, v_ref, in_ref, dq_ref, dk_ref, dv_ref, dgain_ref):
    gain = gain_ref[...].astype(f32)
    for ref, first, each in ((dq_ref, 0, PAIR), (dk_ref, PAIR, 1), (dv_ref, PAIR + 1, 1)):
        for s, group in enumerate(GROUPS):
            for at, to in halves_of_heads(group, each):
                to = slice(first * LANES + to.start, first * LANES + to.stop)
                ref[:, at] = in_ref[s, :, to].astype(f32) * gain
    sums = 0.0
    for ref, grad_ref in ((q_ref, dq_ref), (k_ref, dk_ref), (v_ref, dv_ref)):
        sums = sums + jnp.sum(ref[...].astype(f32) * grad_ref[...], axis=-1, keepdims=True)
    dgain_ref[...] = sums / gain


def feed_blocks():
    for t in range(8):
        for b in range(4):
            yield t, b, b * 8 + t


def pack_feed(gain_ref, g_ref, u_ref, out_ref):
    gain = gain_ref[...].astype(f32)
    for t, b, i in feed_blocks():
        out_ref[t, :, head(b)] = (g_ref[:, head(i)].astype(f32) * gain).astype(bf16)
        out_ref[t, :, head(4 + b)] = (u_ref[:, head(i)].astype(f32) * gain).astype(bf16)


def unpack_feed(gain_ref, g_ref, u_ref, in_ref, dg_ref, du_ref, dgain_ref):
    gain = gain_ref[...].astype(f32)
    sums = jnp.zeros((gain.shape[0], LANES), f32)
    for t, b, i in feed_blocks():
        gate = in_ref[t, :, head(b)].astype(f32) * gain
        up = in_ref[t, :, head(4 + b)].astype(f32) * gain
        dg_ref[:, head(i)] = gate
        du_ref[:, head(i)] = up
        sums = sums + g_ref[:, head(i)].astype(f32) * gate + u_ref[:, head(i)].astype(f32) * up
    dgain_ref[...] = jnp.sum(sums, axis=-1, keepdims=True) / gain


def project(
    x_ref, wq_ref, wkv_ref, freq_ref, hn_ref, q_ref, k_ref, v_ref, cos_ref, sin_ref, first_ref
):
    x = x_ref[:, :D].astype(f32)
    scale = lax.rsqrt(jnp.mean(x * x, axis=-1, keepdims=True) + norm_epsilon)
    normed = (x * scale).astype(bf16)
    hn_ref[...] = normed
    extra = x_ref[:, D:].astype(f32)
    place = extra[:, 0:1] * 128.0 + extra[:, 1:2]
    at = pl.program_id(0) * BLOCK + lax.broadcasted_iota(jnp.int32, place.shape, 0)
    first_ref[...] = at.astype(f32) - place
    angles = place * freq_ref[...]
    lane = lax.broadcasted_iota(jnp.int32, angles.shape, 1)
    cosine = jnp.cos(angles)
    sine = jnp.sin(angles)
    sine = jnp.where(lane < LANES // 2, -sine, sine)
    cos_ref[...] = cosine
    sin_ref[...] = sine
    full = dot_nn(normed, wq_ref[...])
    for h in range(PAIR):
        q_ref[:, head(h)] = turn(full[:, head(h)], cosine, sine).astype(bf16)
    full = dot_nn(normed, wkv_ref[...])
    k_ref[...] = turn(full[:, :LANES], cosine, sine).astype(bf16)
    v_ref[...] = full[:, LANES:].astype(bf16)


def allowed_pairs(first_ref, first, keys):
    shape = (BLOCK, keys)
    query_at = first + lax.broadcasted_iota(jnp.int32, shape, 0)
    key_at = lax.broadcasted_iota(jnp.int32, shape, 1)
    return (key_at <= query_at) & (key_at.astype(f32) >= first_ref[...])


def attend(q_ref, k_ref, v_ref, first_ref, w_ref, a_ref, lse_ref, o_ref):
    blocks = k_ref.shape[0] // BLOCK

    def run(b):
        keys = (b + 1) * BLOCK
        allowed = allowed_pairs(first_ref, b * BLOCK, keys)
        for h in range(PAIR):
            cols = slice(h * LANES, (h + 1) * LANES)
            logits = dot_nt(q_ref[:, cols], k_ref[:keys, :]) * SCALE
            logits = jnp.where(allowed, logits, -1e30)
            top = jnp.max(logits, axis=-1, keepdims=True)
            weights = jnp.exp(logits - top)
            total = jnp.sum(weights, axis=-1, keepdims=True)
            mixed = dot_nn(weights.astype(bf16), v_ref[:keys, :]) / total
            a_ref[:, cols] = mixed.astype(bf16)
            lse_ref[:, h : h + 1] = top + jnp.log(total)

    for b in range(blocks):
        pl.when(pl.program_id(0) == b)(lambda b=b: run(b))
    o_ref[...] = dot_nn(a_ref[...], w_ref[...]).astype(bf16)


def attend_back(
    main_ref, rest_ref, w_ref, q_ref, k_ref, v_ref, a_ref, lse_ref, first_ref, cos_ref, sin_ref,
    dq_ref, dkv_ref, dk_acc, dv_acc, dq_acc
):
    step = pl.program_id(0)
    blocks = k_ref.shape[0] // BLOCK

    @pl.when(step == 0)
    def _():
        dk_acc[...] = jnp.zeros_like(dk_acc)
        dv_acc[...] = jnp.zeros_like(dv_acc)

    grad_mixed = dot_nt(main_ref[...], w_ref[:, :MAIN]) + dot_nt(rest_ref[...], w_ref[:, MAIN:])
    grad_mixed = grad_mixed.astype(bf16)

    def run(b):
        keys = (b + 1) * BLOCK
        allowed = allowed_pairs(first_ref, b * BLOCK, keys)
        for h in range(PAIR):
            cols = slice(h * LANES, (h + 1) * LANES)
            query = q_ref[:, cols]
            grad = grad_mixed[:, cols]
            delta = jnp.sum(
                grad.astype(f32) * a_ref[:, cols].astype(f32), axis=-1, keepdims=True
            )
            logits = dot_nt(query, k_ref[:keys, :]) * SCALE
            logits = jnp.where(allowed, logits, -1e30)
            weights = jnp.exp(logits - lse_ref[:, h : h + 1])
            grad_weights = dot_nt(grad, v_ref[:keys, :])
            grad_logits = (weights * (grad_weights - delta) * SCALE).astype(bf16)
            dq_acc[:, cols] = dot_nn(grad_logits, k_ref[:keys, :])
            dk_acc[:keys, :] += dot_tn(grad_logits, query)
            dv_acc[:keys, :] += dot_tn(weights.astype(bf16), grad)

    for b in range(blocks):
        pl.when(step == b)(lambda b=b: run(b))

    rows = pl.ds(pl.multiple_of(step * BLOCK, BLOCK), BLOCK)
    for h in range(PAIR):
        cols = slice(h * LANES, (h + 1) * LANES)
        dq_ref[:, cols] = turn(dq_acc[:, cols], cos_ref[rows, :], -sin_ref[rows, :]).astype(bf16)

    @pl.when(step == blocks - 1)
    def _():
        dkv_ref[:, :LANES] = turn(dk_acc[...], cos_ref[...], -sin_ref[...]).astype(bf16)
        dkv_ref[:, LANES:] = dv_acc[...].astype(bf16)


def feed(
    main_ref, rest_ref, c_main_ref, c_rest_ref, wg_ref, wu_ref, low_ref, high_ref,
    hn_ref, f_ref, dg_ref, du_ref, o_main_ref, o_rest_ref, e_ref
):
    middle = D // 2
    hn_ref[:, :MAIN] = main_ref[...]
    hn_ref[:, MAIN:] = rest_ref[...]
    gate = dot_nn(hn_ref[...], wg_ref[...])
    up = dot_nn(hn_ref[...], wu_ref[...])
    sig = 1.0 / (1.0 + jnp.exp(-gate))
    swish = gate * sig
    inner = (swish * up).astype(bf16)
    f_ref[...] = inner
    o_main_ref[:, :middle] = dot_nn(inner, low_ref[...]).astype(bf16)
    high = dot_nn(inner, high_ref[...]).astype(bf16)
    o_main_ref[:, middle:] = high[:, : MAIN - middle]
    o_rest_ref[...] = high[:, MAIN - middle :]
    grad = dot_nt(c_main_ref[:, :middle], low_ref[...])
    grad = grad + dot_nt(c_main_ref[:, middle:], high_ref[:, : MAIN - middle])
    grad = grad + dot_nt(c_rest_ref[...], high_ref[:, MAIN - middle :])
    dg_ref[...] = (grad * up * sig * (1.0 + gate * (1.0 - sig))).astype(bf16)
    du_ref[...] = (grad * swish).astype(bf16)
    back = dot_nt(dg_ref[...], wg_ref[...]) + dot_nt(du_ref[...], wu_ref[...])
    e_ref[...] = back.astype(bf16)


def inverse_norm(values):
    return lax.rsqrt(jnp.mean(values * values, axis=-1, keepdims=True) + norm_epsilon)


def norm_back(values, inverse, grad):
    return inverse * grad - values * inverse**3 * jnp.mean(grad * values, axis=-1, keepdims=True)


def body_fast(
    inputs,
    cotangent,
    doc_ids,
    positions,
    gain_first,
    query_weight,
    key_weight,
    value_weight,
    output_weight,
    gain_second,
    gate_weight,
    up_weight,
    down_weight,
):
    rows = inputs.shape[0]
    own = query_weight.shape[0]
    hidden_block = down_weight.shape[0]
    width = 4 * hidden_block
    total_rows = 8 * rows
    steps = total_rows // BLOCK
    gain_one = gain_first.reshape(own, 1)
    gain_two = gain_second.reshape(own, 1)

    marks = jnp.stack([positions // 128, positions % 128], axis=1).astype(bf16)
    marks = jnp.pad(marks, ((0, 0), (0, LANES - 2)))
    marked = jnp.concatenate([inputs, marks], axis=1)

    heads_in = [whole(own, 1), whole(own, D), whole(own, D // 2), whole(own, D // 2)]
    feed_in = [whole(own, 1), whole(own, 8 * width), whole(own, 8 * width)]
    (parts,) = call(
        pack_heads, 1, heads_in, [(whole(8, own, PAD_COLS), (8, own, PAD_COLS), bf16)]
    )(gain_one, query_weight, key_weight, value_weight)
    (both,) = call(
        pack_feed, 1, feed_in, [(whole(8, own, 2 * width), (8, own, 2 * width), bf16)]
    )(gain_two, gate_weight, up_weight)
    rows_all = gather_rows(marked)
    w_out = gather_bit(gather_bit(output_weight, "c", 0), "zl", 0)
    parts, both, w_out, cotangent = together(exchange(parts), both, w_out, cotangent)
    cot_main, cot_rest = gather_rows(cotangent[:, :MAIN]), cotangent[:, MAIN:]
    parts = parts.reshape(8 * own, PAD_COLS)
    w_query, w_kv = parts[:, :QUERY_COLS], parts[:, QUERY_COLS:]
    w_query, w_kv = together(gather_bit(w_query, "y", 0), gather_bit(w_kv, "x", 0))
    w_query = gather_bit(w_query, "x", 1).reshape(D, QUERY_COLS)
    w_kv = gather_bit(w_kv, "y", 0).reshape(D, 2 * LANES)
    w_out = across(w_out)
    rows_all, w_query, w_kv, w_out, both, cot_rest = together(
        rows_all, w_query, w_kv, w_out, both, cot_rest
    )
    w_out = jnp.pad(w_out, ((0, 0), (0, 0), (0, LANES // 2 - own), (0, 0)))
    w_out = w_out.reshape(QUERY_COLS, D)

    lane = jnp.arange(LANES) % (LANES // 2)
    freq = rotary_base ** (-lane.astype(f32) * 2.0 / HEAD)
    freq = jnp.where(lane < HALF, freq, 0.0).reshape(1, LANES)

    def rows_out(cols, kind):
        return (rows_of(cols), (total_rows, cols), kind)

    normed, query, key, value, cosine, sine, row_first = call(
        project,
        steps,
        [rows_of(D + LANES), whole(D, QUERY_COLS), whole(D, 2 * LANES), whole(1, LANES)],
        [
            rows_out(D, bf16),
            rows_out(QUERY_COLS, bf16),
            rows_out(LANES, bf16),
            rows_out(LANES, bf16),
            rows_out(LANES, f32),
            rows_out(LANES, f32),
            rows_out(1, f32),
        ],
        flops=3 << 30,
    )(rows_all, w_query, w_kv, freq)
    mixed, lse, term = call(
        attend,
        steps,
        [
            rows_of(QUERY_COLS),
            whole(total_rows, LANES),
            whole(total_rows, LANES),
            rows_of(1),
            whole(QUERY_COLS, D),
        ],
        [
            rows_out(QUERY_COLS, bf16),
            rows_out(PAIR, f32),
            rows_out(D, bf16),
        ],
        flops=6 << 30,
    )(query, key, value, row_first, w_out)
    term, both, cot_main, cot_rest, down_weight = together(
        term, exchange(both), cot_main, gather_bit(gather_bit(cot_rest, "zh", 0), "zl", 1), down_weight
    )
    attended = scatter_rows(term)
    both = both.reshape(8 * own, 2 * width)
    feed_low, feed_high, down_low, down_high = together(
        gather_bit(both[:, :width], "y", 0),
        gather_bit(both[:, width:], "x", 0),
        gather_bit(down_weight[:, : D // 2], "y", 0),
        gather_bit(down_weight[:, D // 2 :], "x", 0),
    )
    w_gate, w_up = gather_bit(feed_low, "x", 1), gather_bit(feed_high, "y", 0)
    attended, w_gate, w_up, down_low, down_high, cot_rest = together(
        attended, w_gate, w_up, down_low, down_high, gather_bit(cot_rest, "c", 2)
    )
    cot_rest = cot_rest.reshape(total_rows, REST)
    w_gate, w_up = w_gate.reshape(D, width), w_up.reshape(D, width)
    x_float = inputs.astype(f32)
    middle = x_float + attended.astype(f32)

    inverse_two = inverse_norm(middle)
    main, rest = gather_split((middle * inverse_two).astype(bf16))
    w_low = gather_bit(down_low, "x", 1).reshape(width, D // 2)
    w_high = gather_bit(down_high, "y", 0).reshape(width, D // 2)
    main, rest, w_low, w_high = together(main, rest, w_low, w_high)
    normed_two, inner, grad_gate, grad_up, *terms = call(
        feed,
        steps,
        [
            rows_of(MAIN),
            rows_of(REST),
            rows_of(MAIN),
            rows_of(REST),
            whole(D, width),
            whole(D, width),
            whole(width, D // 2),
            whole(width, D // 2),
        ],
        [
            rows_out(D, bf16),
            rows_out(width, bf16),
            rows_out(width, bf16),
            rows_out(width, bf16),
            rows_out(MAIN, bf16),
            rows_out(REST, bf16),
            rows_out(D, bf16),
        ],
    )(main, rest, cot_main, cot_rest, w_gate, w_up, w_low, w_high)
    normed_two, inner, *terms = together(normed_two, inner, *terms)
    out_term, back_two = terms[:2], scatter_rows(terms[2])
    feed_one = reduce_one(
        dot_tn(normed_two, grad_gate).astype(bf16), dot_tn(normed_two, grad_up).astype(bf16)
    )
    down_one = reduce_one(
        dot_tn(inner, cot_main[:, : D // 2]).astype(bf16),
        jnp.concatenate(
            [dot_tn(inner, cot_main[:, D // 2 :]), dot_tn(inner, cot_rest)], axis=-1
        ).astype(bf16),
    )
    back_two, *rest = together(back_two, *feed_one, *down_one)
    feed_one, down_one = rest[:4], rest[4:]
    cot_float = cotangent.astype(f32)
    grad_middle = cot_float + norm_back(middle, inverse_two, back_two.astype(f32))
    middle_all = gather_split(grad_middle.astype(bf16))
    feed_two, down_two = reduce_two(feed_one), reduce_two(down_one)
    feed_two = together(*feed_two)
    both_sum = exchange(reduced(feed_two).astype(bf16).reshape(8, own, 2 * width))
    rest = together(both_sum, *middle_all, *out_term, *down_two)
    both_sum, middle_all, out_term, down_two = rest[0], rest[1:3], rest[3:5], rest[5:]
    outputs = scatter_split(*out_term)

    grad_query, grad_kv = call(
        attend_back,
        steps,
        [
            rows_of(MAIN),
            rows_of(REST),
            whole(QUERY_COLS, D),
            rows_of(QUERY_COLS),
            whole(total_rows, LANES),
            whole(total_rows, LANES),
            rows_of(QUERY_COLS),
            rows_of(PAIR),
            rows_of(1),
            whole(total_rows, LANES),
            whole(total_rows, LANES),
        ],
        [
            rows_out(QUERY_COLS, bf16),
            (whole(total_rows, 2 * LANES), (total_rows, 2 * LANES), bf16),
        ],
        scratch=[
            pltpu.VMEM((total_rows, LANES), f32),
            pltpu.VMEM((total_rows, LANES), f32),
            pltpu.VMEM((BLOCK, QUERY_COLS), f32),
        ],
        flops=6 << 30,
    )(*middle_all, w_out, query, key, value, mixed, lse, row_first, cosine, sine)
    first_term = (dot_nt(grad_query, w_query) + dot_nt(grad_kv, w_kv)).astype(bf16)
    head_one = reduce_one(
        dot_tn(normed, grad_query).astype(bf16), dot_tn(normed, grad_kv).astype(bf16)
    )
    head_two = reduce_two(together(*head_one))
    first_term, mixed, out_main, *rest = together(
        first_term, mixed, outputs[0], *head_two, *down_two
    )
    head_two, down_two = rest[:4], rest[4:]
    first_sum = scatter_rows(first_term).astype(f32)
    head_term = exchange(reduced(head_two).astype(bf16).reshape(8, own, PAD_COLS))
    out_part = jnp.concatenate([dot_tn(mixed, part) for part in middle_all], axis=-1)
    out_part = out_part.astype(bf16).reshape(2, 2, LANES // 2, D)[:, :, :own]
    head_term, out_rest, *out_pair = together(
        head_term, outputs[1], *halves(out_part, "y", 1)
    )
    out_pair = halves(total(out_pair), "x", 0)
    output_grad = across(total(out_pair).astype(bf16)).astype(f32)
    down_grad = reduced(down_two)
    outputs = (middle + joined(out_main, out_rest)).astype(bf16)
    inputs_grad = (grad_middle + norm_back(x_float, inverse_norm(x_float), first_sum)).astype(bf16)

    wide = (whole(own, 8 * width), (own, 8 * width), f32)
    column = (whole(own, 1), (own, 1), f32)
    gate_grad, up_grad, second_grad = call(
        unpack_feed,
        1,
        [*feed_in, whole(8, own, 2 * width)],
        [wide, wide, column],
    )(gain_two, gate_weight, up_weight, both_sum)
    query_grad, key_grad, value_grad, first_grad = call(
        unpack_heads,
        1,
        [*heads_in, whole(8, own, PAD_COLS)],
        [
            (whole(own, D), (own, D), f32),
            (whole(own, D // 2), (own, D // 2), f32),
            (whole(own, D // 2), (own, D // 2), f32),
            column,
        ],
    )(gain_one, query_weight, key_weight, value_weight, head_term)
    return (
        outputs,
        inputs_grad,
        first_grad.reshape(own),
        query_grad,
        key_grad,
        value_grad,
        output_grad,
        second_grad.reshape(own),
        gate_grad,
        up_grad,
        down_grad,
    )


def solution(mesh):
    shape = dict(mesh.shape)
    step, axes = body, ("dp", "seq")
    if shape["dp"] == 4 and shape["seq"] == KV_HEADS:
        step, axes = body_fast, AXES
        mesh = Mesh(mesh.devices.reshape(2, 2, 2, 2, 2), AXES)
    wide, line = P(axes, None), P(axes)
    return jax.shard_map(
        step,
        mesh=mesh,
        in_specs=(wide, wide, line, line, line, wide, wide, wide, wide, line, wide, wide, wide),
        out_specs=(wide, wide, line, wide, wide, wide, wide, line, wide, wide, wide),
        check_vma=False,
    )
```

```python
import math

import jax
import jax.numpy as jnp
from jax import lax
from jax.experimental import pallas as pl
from jax.experimental.pallas import tpu as pltpu
from jax.sharding import Mesh, PartitionSpec as P

D = 1536
HEADS = 16
KV_HEADS = 8
HEAD = 96


norm_epsilon = 1e-05
rotary_base = 100000.0


def normalize(values_in, gain):
    return (
        values_in
        * lax.rsqrt(jnp.mean(values_in * values_in, axis=-1, keepdims=True) + norm_epsilon)
        * gain
    )


def swish_product(gate, upward):
    return jax.nn.silu(gate) * upward


def rotate(matrix, positions, heads_count, direction):
    halfway = HEAD // 2
    inverse_freq = rotary_base ** (-jnp.arange(halfway, dtype=jnp.float32) * 2.0 / HEAD)
    angles = positions.astype(jnp.float32)[:, None] * inverse_freq[None, :]
    cosine = jnp.cos(angles)[:, None, :]
    sine_table = direction * jnp.sin(angles)[:, None, :]
    shaped = matrix.reshape(matrix.shape[0], heads_count, HEAD)
    first_half = shaped[..., :halfway]
    second_half = shaped[..., halfway:]
    turned = jnp.concatenate(
        [
            first_half * cosine - second_half * sine_table,
            second_half * cosine + first_half * sine_table,
        ],
        axis=-1,
    )
    return turned.reshape(matrix.shape)


def times_transposed(left, right):
    return lax.dot_general(
        left, right, (((1,), (1,)), ((), ())), preferred_element_type=jnp.float32
    )


def transposed_times(left, right):
    return lax.dot_general(
        left, right, (((0,), (0,)), ((), ())), preferred_element_type=jnp.float32
    )


def matrix_product(left, right):
    return jnp.dot(left, right, preferred_element_type=jnp.float32)


def block_rows(total_rows):
    size_rows = min(total_rows, 1024)
    while total_rows % size_rows:
        size_rows -= 1
    return size_rows


def fold_local(block_step, initial, arrays):
    total_rows = arrays[0].shape[0]
    size_rows = block_rows(total_rows)

    def one_turn(turn_index, state_in):
        begin_row = turn_index * size_rows
        pieces = tuple(
            (lax.dynamic_slice_in_dim(member, begin_row, size_rows, 0) for member in arrays)
        )
        return block_step(state_in, pieces, begin_row)

    return lax.fori_loop(0, total_rows // size_rows, one_turn, initial)


def piece_fold(block_step, state_in, pieces):
    return fold_local(block_step, state_in, pieces)


def keep_state(state_now):
    return state_now


def body(
    inputs,
    cotangent,
    doc_ids,
    positions,
    gain_first,
    query_weight,
    key_weight,
    value_weight,
    output_weight,
    gain_second,
    gate_weight,
    up_weight,
    down_weight,
):
    f32 = jnp.float32
    bf16 = jnp.bfloat16
    attend_set = (
        lax.all_gather(gain_first, ("dp", "seq"), axis=0, tiled=True),
        lax.all_gather(query_weight, ("dp", "seq"), axis=0, tiled=True),
        lax.all_gather(key_weight, ("dp", "seq"), axis=0, tiled=True),
        lax.all_gather(value_weight, ("dp", "seq"), axis=0, tiled=True),
        lax.all_gather(output_weight, ("dp", "seq"), axis=0, tiled=True),
    )
    feed_set = (
        lax.all_gather(gain_second, ("dp", "seq"), axis=0, tiled=True),
        lax.all_gather(gate_weight, ("dp", "seq"), axis=0, tiled=True),
        lax.all_gather(up_weight, ("dp", "seq"), axis=0, tiled=True),
        lax.all_gather(down_weight, ("dp", "seq"), axis=0, tiled=True),
    )
    gain_one, w_query, w_key, w_value, w_output = attend_set
    gain_two, w_gate, w_up, w_down = feed_set
    row_count = inputs.shape[0]
    group_size = HEADS // KV_HEADS
    kv_width = KV_HEADS * HEAD
    score_scale = 1.0 / math.sqrt(HEAD)
    query_rows = lax.axis_index("seq") * row_count + jnp.arange(row_count, dtype=jnp.int32)
    x_float = inputs.astype(f32)
    gain_one_float = gain_one.astype(f32)
    normed = normalize(x_float, gain_one_float).astype(bf16)
    query_rot = rotate(matrix_product(normed, w_query), positions, HEADS, 1.0).astype(bf16)
    key_rot = rotate(matrix_product(normed, w_key), positions, KV_HEADS, 1.0).astype(bf16)
    value_low = matrix_product(normed, w_value).astype(bf16)
    query_four = query_rot.reshape(row_count, KV_HEADS, group_size, HEAD)

    def mask_for(docs_part, first_key, piece_rows):
        key_rows = first_key + jnp.arange(piece_rows, dtype=jnp.int32)
        return (key_rows[None, :] <= query_rows[:, None]) & (docs_part[None, :] == doc_ids[:, None])

    def forward_step(state_in, pieces, first_key):
        keys_part, values_part, docs_part = pieces
        piece_rows = keys_part.shape[0]
        allowed = mask_for(docs_part, first_key, piece_rows)

        def forward_compute(state_now):
            accumulated, running, totals = state_now
            logits = (
                jnp.einsum(
                    "qgrd,kgd->grqk",
                    query_four,
                    keys_part.reshape(piece_rows, KV_HEADS, HEAD),
                    preferred_element_type=f32,
                )
                * score_scale
            )
            logits = jnp.where(allowed, logits, -1e30)
            new_max = jnp.maximum(running, jnp.max(logits, axis=-1))
            weights_block = jnp.where(allowed, jnp.exp(logits - new_max[..., None]), 0.0)
            factor = jnp.exp(running - new_max)
            totals = totals * factor + jnp.sum(weights_block, axis=-1)
            update = jnp.einsum(
                "grqk,kgd->qgrd",
                weights_block.astype(bf16),
                values_part.reshape(piece_rows, KV_HEADS, HEAD),
                preferred_element_type=f32,
            )
            accumulated = accumulated * jnp.transpose(factor, (2, 0, 1))[..., None] + update
            return (accumulated, new_max, totals)

        return lax.cond(jnp.any(allowed), forward_compute, keep_state, state_in)

    forward_init = (
        jnp.zeros((row_count, KV_HEADS, group_size, HEAD), f32),
        jnp.full((KV_HEADS, group_size, row_count), -1e30, f32),
        jnp.zeros((KV_HEADS, group_size, row_count), f32),
    )
    forward_state = piece_fold(
        forward_step,
        forward_init,
        (
            lax.all_gather(key_rot, "seq", axis=0, tiled=True),
            lax.all_gather(value_low, "seq", axis=0, tiled=True),
            lax.all_gather(doc_ids, "seq", axis=0, tiled=True),
        ),
    )
    accumulated, running, totals = forward_state
    attend_float = accumulated / jnp.transpose(totals, (2, 0, 1))[..., None]
    log_totals = running + jnp.log(totals)
    mixed = attend_float.reshape(row_count, D).astype(bf16)
    middle = x_float + matrix_product(mixed, w_output)
    gain_two_float = gain_two.astype(f32)
    normed_two = normalize(middle, gain_two_float).astype(bf16)
    gate = matrix_product(normed_two, w_gate)
    upward = matrix_product(normed_two, w_up)
    hidden = swish_product(gate, upward).astype(bf16)
    outputs = (middle + matrix_product(hidden, w_down)).astype(bf16)
    feed_back = (
        lax.all_gather(gain_second, ("dp", "seq"), axis=0, tiled=True),
        lax.all_gather(gate_weight, ("dp", "seq"), axis=0, tiled=True),
        lax.all_gather(up_weight, ("dp", "seq"), axis=0, tiled=True),
        lax.all_gather(down_weight, ("dp", "seq"), axis=0, tiled=True),
    )
    attend_back = (
        lax.all_gather(gain_first, ("dp", "seq"), axis=0, tiled=True),
        lax.all_gather(query_weight, ("dp", "seq"), axis=0, tiled=True),
        lax.all_gather(key_weight, ("dp", "seq"), axis=0, tiled=True),
        lax.all_gather(value_weight, ("dp", "seq"), axis=0, tiled=True),
        lax.all_gather(output_weight, ("dp", "seq"), axis=0, tiled=True),
    )
    unused_gain_two, back_gate, back_up, back_down = feed_back
    unused_gain_one, back_query, back_key, back_value, back_output = attend_back
    cot_float = cotangent.astype(f32)
    cot_low = cot_float.astype(bf16)
    down_term = transposed_times(hidden, cot_low)
    grad_hidden = times_transposed(cot_low, back_down)
    unused_swish, swish_back = jax.vjp(swish_product, gate, upward)
    grad_gate, grad_up = swish_back(grad_hidden)
    grad_gate_low = grad_gate.astype(bf16)
    grad_up_low = grad_up.astype(bf16)
    gate_term = transposed_times(normed_two, grad_gate_low)
    up_term = transposed_times(normed_two, grad_up_low)
    grad_normed_two = times_transposed(grad_gate_low, back_gate) + times_transposed(
        grad_up_low, back_up
    )
    unused_norm_two, norm_two_back = jax.vjp(normalize, middle, gain_two_float)
    grad_middle_part, gain_two_term = norm_two_back(grad_normed_two)
    second_grad, gate_grad, up_grad, down_grad = (
        lax.psum_scatter(gain_two_term, ("dp", "seq"), scatter_dimension=0, tiled=True),
        lax.psum_scatter(gate_term, ("dp", "seq"), scatter_dimension=0, tiled=True),
        lax.psum_scatter(up_term, ("dp", "seq"), scatter_dimension=0, tiled=True),
        lax.psum_scatter(down_term, ("dp", "seq"), scatter_dimension=0, tiled=True),
    )
    grad_middle = cot_float + grad_middle_part
    middle_low = grad_middle.astype(bf16)
    output_term = transposed_times(mixed, middle_low)
    grad_mixed = times_transposed(middle_low, back_output).astype(bf16)
    dout_four = grad_mixed.reshape(row_count, KV_HEADS, group_size, HEAD)
    delta_rows = jnp.einsum("qgrd,qgrd->grq", dout_four.astype(f32), attend_float)

    def query_grad_block(allowed, keys_three, values_three):
        logits = (
            jnp.einsum("qgrd,kgd->grqk", query_four, keys_three, preferred_element_type=f32)
            * score_scale
        )
        logits = jnp.where(allowed, logits, -1e30)
        weights_block = jnp.where(allowed, jnp.exp(logits - log_totals[..., None]), 0.0)
        grad_weights = jnp.einsum(
            "qgrd,kgd->grqk", dout_four, values_three, preferred_element_type=f32
        )
        grad_logits = (weights_block * (grad_weights - delta_rows[..., None]) * score_scale).astype(
            bf16
        )
        return (weights_block, grad_logits)

    def query_step(state_in, pieces, first_key):
        keys_part, values_part, docs_part = pieces
        piece_rows = keys_part.shape[0]
        allowed = mask_for(docs_part, first_key, piece_rows)

        def query_compute(grad_query):
            keys_three = keys_part.reshape(piece_rows, KV_HEADS, HEAD)
            values_three = values_part.reshape(piece_rows, KV_HEADS, HEAD)
            unused_weights, grad_logits = query_grad_block(allowed, keys_three, values_three)
            return grad_query + jnp.einsum(
                "grqk,kgd->qgrd", grad_logits, keys_three, preferred_element_type=f32
            )

        return lax.cond(jnp.any(allowed), query_compute, keep_state, state_in)

    grad_query_rot = piece_fold(
        query_step,
        jnp.zeros((row_count, KV_HEADS, group_size, HEAD), f32),
        (
            lax.all_gather(key_rot, "seq", axis=0, tiled=True),
            lax.all_gather(value_low, "seq", axis=0, tiled=True),
            lax.all_gather(doc_ids, "seq", axis=0, tiled=True),
        ),
    )
    lse_rows = jnp.transpose(log_totals, (2, 0, 1)).reshape(row_count, HEADS)
    delta_flat = jnp.transpose(delta_rows, (2, 0, 1)).reshape(row_count, HEADS)
    lse_all, delta_all = (
        lax.all_gather(lse_rows, "seq", axis=0, tiled=True),
        lax.all_gather(delta_flat, "seq", axis=0, tiled=True),
    )
    keys_mine = key_rot.reshape(row_count, KV_HEADS, HEAD)
    values_mine = value_low.reshape(row_count, KV_HEADS, HEAD)

    def key_step(state_in, pieces, first_query):
        queries_part, dout_part, docs_part = pieces
        piece_rows = queries_part.shape[0]
        other_rows = first_query + jnp.arange(piece_rows, dtype=jnp.int32)
        allowed = (query_rows[None, :] <= other_rows[:, None]) & (
            doc_ids[None, :] == docs_part[:, None]
        )

        def key_compute(state_now):
            grad_keys, grad_values = state_now
            lse_part = lax.dynamic_slice_in_dim(lse_all, first_query, piece_rows, 0)
            delta_part = lax.dynamic_slice_in_dim(delta_all, first_query, piece_rows, 0)
            lse_three = jnp.transpose(lse_part.reshape(piece_rows, KV_HEADS, group_size), (1, 2, 0))
            delta_three = jnp.transpose(
                delta_part.reshape(piece_rows, KV_HEADS, group_size), (1, 2, 0)
            )
            queries_four = queries_part.reshape(piece_rows, KV_HEADS, group_size, HEAD)
            douts_four = dout_part.reshape(piece_rows, KV_HEADS, group_size, HEAD)
            logits = (
                jnp.einsum("qgrd,kgd->grqk", queries_four, keys_mine, preferred_element_type=f32)
                * score_scale
            )
            logits = jnp.where(allowed, logits, -1e30)
            weights_block = jnp.where(allowed, jnp.exp(logits - lse_three[..., None]), 0.0)
            grad_weights = jnp.einsum(
                "qgrd,kgd->grqk", douts_four, values_mine, preferred_element_type=f32
            )
            grad_logits = (
                weights_block * (grad_weights - delta_three[..., None]) * score_scale
            ).astype(bf16)
            grad_keys = grad_keys + jnp.einsum(
                "grqk,qgrd->kgd", grad_logits, queries_four, preferred_element_type=f32
            )
            grad_values = grad_values + jnp.einsum(
                "grqk,qgrd->kgd", weights_block.astype(bf16), douts_four, preferred_element_type=f32
            )
            return (grad_keys, grad_values)

        return lax.cond(jnp.any(allowed), key_compute, keep_state, state_in)

    key_init = (
        jnp.zeros((row_count, KV_HEADS, HEAD), f32),
        jnp.zeros((row_count, KV_HEADS, HEAD), f32),
    )
    grad_keys_three, grad_values_three = piece_fold(
        key_step,
        key_init,
        (
            lax.all_gather(query_rot, "seq", axis=0, tiled=True),
            lax.all_gather(grad_mixed, "seq", axis=0, tiled=True),
            lax.all_gather(doc_ids, "seq", axis=0, tiled=True),
        ),
    )
    grad_keys_mine = grad_keys_three.reshape(row_count, kv_width)
    grad_values_mine = grad_values_three.reshape(row_count, kv_width)
    grad_query_low = rotate(grad_query_rot.reshape(row_count, D), positions, HEADS, -1.0).astype(
        bf16
    )
    grad_key_low = rotate(grad_keys_mine, positions, KV_HEADS, -1.0).astype(bf16)
    grad_value_low = grad_values_mine.astype(bf16)
    query_term = transposed_times(normed, grad_query_low)
    key_term_all = transposed_times(normed, grad_key_low)
    value_term_all = transposed_times(normed, grad_value_low)
    grad_normed = (
        times_transposed(grad_query_low, back_query)
        + times_transposed(grad_key_low, back_key)
        + times_transposed(grad_value_low, back_value)
    )
    unused_norm_one, norm_one_back = jax.vjp(normalize, x_float, gain_one_float)
    grad_input_part, gain_one_term = norm_one_back(grad_normed)
    inputs_grad = (grad_middle + grad_input_part).astype(bf16)
    first_grad, query_grad, key_grad, value_grad, output_grad = (
        lax.psum_scatter(gain_one_term, ("dp", "seq"), scatter_dimension=0, tiled=True),
        lax.psum_scatter(query_term, ("dp", "seq"), scatter_dimension=0, tiled=True),
        lax.psum_scatter(key_term_all, ("dp", "seq"), scatter_dimension=0, tiled=True),
        lax.psum_scatter(value_term_all, ("dp", "seq"), scatter_dimension=0, tiled=True),
        lax.psum_scatter(output_term, ("dp", "seq"), scatter_dimension=0, tiled=True),
    )
    return (
        outputs,
        inputs_grad,
        first_grad,
        query_grad,
        key_grad,
        value_grad,
        output_grad,
        second_grad,
        gate_grad,
        up_grad,
        down_grad,
    )

AXES = ("y", "x", "zh", "zl", "c")
SEQUENCE = ("zh", "zl", "c")
PAIR = 2
LANES = 128
QUERY_COLS = PAIR * LANES
PAD_COLS = (PAIR + 2) * LANES
BLOCK = 256
MAIN = 3 * D // 4
REST = D - MAIN
f32 = jnp.float32
bf16 = jnp.bfloat16


def swap(value, axis):
    return lax.ppermute(value, axis, [(0, 1), (1, 0)])


def my_bit(axis):
    return lax.axis_index(axis)


def pick(value, index, axis):
    return lax.dynamic_index_in_dim(value, index, axis, keepdims=False)


def together(*values):
    return lax.optimization_barrier(values)


def paired(mine, other, bit, axis):
    low_first = my_bit(bit) == 0
    return jnp.stack(
        [jnp.where(low_first, mine, other), jnp.where(low_first, other, mine)], axis
    )


def gather_bit(value, bit, axis):
    return paired(value, swap(value, bit), bit, axis)


def halves(value, bit, axis):
    mine = my_bit(bit)
    return pick(value, mine, axis), swap(pick(value, 1 - mine, axis).astype(bf16), bit)


def total(pair):
    return pair[0].astype(f32) + pair[1].astype(f32)


def reduce_bit(value, bit, axis):
    return total(halves(value, bit, axis))


def across(value):
    pairs = []
    for i in range(32):
        y, x, zh, zl, c = (i >> 4) & 1, (i >> 3) & 1, (i >> 2) & 1, (i >> 1) & 1, i & 1
        pairs.append((i, c * 16 + zl * 8 + zh * 4 + x * 2 + y))
    return lax.ppermute(value, AXES, pairs)


def gather_rows(value):
    return lax.all_gather(value, SEQUENCE, axis=0, tiled=True)


def scatter_rows(value):
    return lax.psum_scatter(value, SEQUENCE, scatter_dimension=0, tiled=True)


def gather_line(value):
    value = gather_bit(gather_bit(gather_bit(value, "zh", 0), "zl", 1), "c", 2)
    return value.reshape(-1, value.shape[-1])


def scatter_line(value):
    value = value.reshape(2, 2, 2, value.shape[0] // 8, -1)
    return reduce_bit(reduce_bit(reduce_bit(value, "c", 2), "zl", 1), "zh", 0)


def gather_split(value):
    return gather_rows(value[:, :MAIN]), gather_line(value[:, MAIN:])


def scatter_split(main, rest):
    return scatter_rows(main), scatter_line(rest)


def joined(main, rest):
    return jnp.concatenate([main.astype(f32), rest], axis=-1)


def exchange(parts):
    return lax.all_to_all(parts, SEQUENCE, 0, 0, tiled=True)


def gather_yx(value):
    rows, cols = value.shape
    low, high = value[:, : cols // 2], value[:, cols // 2 :]
    low = gather_bit(gather_bit(low, "y", 0), "x", 1)
    high = gather_bit(gather_bit(high, "x", 0), "y", 0)
    return low.reshape(4 * rows, -1), high.reshape(4 * rows, -1)


def reduce_one(low, high):
    low = low.reshape(2, 2, -1, low.shape[-1])
    high = high.reshape(2, 2, -1, high.shape[-1])
    return (*halves(low, "y", 0), *halves(high, "x", 1))


def reduce_two(one):
    return (*halves(total(one[:2]), "x", 0), *halves(total(one[2:]), "y", 0))


def reduced(two):
    return jnp.concatenate([total(two[:2]), total(two[2:])], axis=-1)


def dot_nn(left, right):
    return jnp.dot(left, right, preferred_element_type=f32)


def dot_nt(left, right):
    return lax.dot_general(left, right, (((1,), (1,)), ((), ())), preferred_element_type=f32)


def dot_tn(left, right):
    return lax.dot_general(left, right, (((0,), (0,)), ((), ())), preferred_element_type=f32)


def whole(*shape):
    return pl.BlockSpec(shape, lambda i: (0,) * len(shape), pipeline_mode=pl.Buffered(1))


def rows_of(cols):
    return pl.BlockSpec((BLOCK, cols), lambda i: (i, 0))


def call(kernel, steps, in_specs, outs, scratch=(), vmem=60, flops=0):
    return pl.pallas_call(
        kernel,
        grid=(steps,),
        in_specs=in_specs,
        out_specs=[spec for spec, shape, kind in outs],
        out_shape=[jax.ShapeDtypeStruct(shape, kind) for spec, shape, kind in outs],
        scratch_shapes=list(scratch),
        compiler_params=pltpu.CompilerParams(vmem_limit_bytes=vmem * 1024 * 1024),
        cost_estimate=pl.CostEstimate(flops=flops, bytes_accessed=flops // 500, transcendentals=0),
        name=kernel.__name__,
    )


def turn(matrix, cosine, sine):
    return matrix * cosine + pltpu.roll(matrix, LANES // 2, 1) * sine


def head(h):
    return slice(h * LANES, (h + 1) * LANES)


SCALE = 1.0 / math.sqrt(HEAD)
HALF = HEAD // 2


def halves_of_heads(group, each):
    for h in range(each):
        for k in range(2):
            at = ((group * each + h) * 2 + k) * HALF
            to = h * LANES + k * (LANES // 2)
            yield slice(at, at + HALF), slice(to, to + HALF)


GROUPS = [((s & 1) << 2) | (s & 2) | (s >> 2) for s in range(8)]


def pack_heads(gain_ref, q_ref, k_ref, v_ref, out_ref):
    gain = gain_ref[...].astype(f32)
    out_ref[...] = jnp.zeros_like(out_ref)
    for ref, first, each in ((q_ref, 0, PAIR), (k_ref, PAIR, 1), (v_ref, PAIR + 1, 1)):
        scaled = ref[...].astype(f32) * gain
        for s, group in enumerate(GROUPS):
            for at, to in halves_of_heads(group, each):
                to = slice(first * LANES + to.start, first * LANES + to.stop)
                out_ref[s, :, to] = scaled[:, at].astype(bf16)


def unpack_heads(gain_ref, q_ref, k_ref, v_ref, in_ref, dq_ref, dk_ref, dv_ref, dgain_ref):
    gain = gain_ref[...].astype(f32)
    for ref, first, each in ((dq_ref, 0, PAIR), (dk_ref, PAIR, 1), (dv_ref, PAIR + 1, 1)):
        for s, group in enumerate(GROUPS):
            for at, to in halves_of_heads(group, each):
                to = slice(first * LANES + to.start, first * LANES + to.stop)
                ref[:, at] = in_ref[s, :, to].astype(f32) * gain
    sums = 0.0
    for ref, grad_ref in ((q_ref, dq_ref), (k_ref, dk_ref), (v_ref, dv_ref)):
        sums = sums + jnp.sum(ref[...].astype(f32) * grad_ref[...], axis=-1, keepdims=True)
    dgain_ref[...] = sums / gain


def feed_blocks():
    for t in range(8):
        for b in range(4):
            yield t, b, b * 8 + t


def pack_feed(gain_ref, g_ref, u_ref, out_ref):
    gain = gain_ref[...].astype(f32)
    for t, b, i in feed_blocks():
        out_ref[t, :, head(b)] = (g_ref[:, head(i)].astype(f32) * gain).astype(bf16)
        out_ref[t, :, head(4 + b)] = (u_ref[:, head(i)].astype(f32) * gain).astype(bf16)


def unpack_feed(gain_ref, g_ref, u_ref, in_ref, dg_ref, du_ref, dgain_ref):
    gain = gain_ref[...].astype(f32)
    sums = jnp.zeros((gain.shape[0], LANES), f32)
    for t, b, i in feed_blocks():
        gate = in_ref[t, :, head(b)].astype(f32) * gain
        up = in_ref[t, :, head(4 + b)].astype(f32) * gain
        dg_ref[:, head(i)] = gate
        du_ref[:, head(i)] = up
        sums = sums + g_ref[:, head(i)].astype(f32) * gate + u_ref[:, head(i)].astype(f32) * up
    dgain_ref[...] = jnp.sum(sums, axis=-1, keepdims=True) / gain


def project(
    x_ref, wq_ref, wkv_ref, freq_ref, hn_ref, q_ref, k_ref, v_ref, cos_ref, sin_ref, first_ref
):
    x = x_ref[:, :D].astype(f32)
    scale = lax.rsqrt(jnp.mean(x * x, axis=-1, keepdims=True) + norm_epsilon)
    normed = (x * scale).astype(bf16)
    hn_ref[...] = normed
    extra = x_ref[:, D:].astype(f32)
    place = extra[:, 0:1] * 128.0 + extra[:, 1:2]
    at = pl.program_id(0) * BLOCK + lax.broadcasted_iota(jnp.int32, place.shape, 0)
    first_ref[...] = at.astype(f32) - place
    angles = place * freq_ref[...]
    lane = lax.broadcasted_iota(jnp.int32, angles.shape, 1)
    cosine = jnp.cos(angles)
    sine = jnp.sin(angles)
    sine = jnp.where(lane < LANES // 2, -sine, sine)
    cos_ref[...] = cosine
    sin_ref[...] = sine
    full = dot_nn(normed, wq_ref[...])
    for h in range(PAIR):
        q_ref[:, head(h)] = turn(full[:, head(h)], cosine, sine).astype(bf16)
    full = dot_nn(normed, wkv_ref[...])
    k_ref[...] = turn(full[:, :LANES], cosine, sine).astype(bf16)
    v_ref[...] = full[:, LANES:].astype(bf16)


def allowed_pairs(first_ref, first, keys):
    shape = (BLOCK, keys)
    query_at = first + lax.broadcasted_iota(jnp.int32, shape, 0)
    key_at = lax.broadcasted_iota(jnp.int32, shape, 1)
    return (key_at <= query_at) & (key_at.astype(f32) >= first_ref[...])


def by_keys(keys_total, run):
    half = keys_total // BLOCK // 2
    pl.when(pl.program_id(0) < half)(lambda: run(keys_total // 2))
    pl.when(pl.program_id(0) >= half)(lambda: run(keys_total))


def each_head(run):
    def one(h, nothing):
        run(h, pl.ds(pl.multiple_of(h * LANES, LANES), LANES))
        return nothing

    lax.fori_loop(0, PAIR, one, 0)


def attend(q_ref, k_ref, v_ref, first_ref, w_ref, a_ref, lse_ref, o_ref):
    first = pl.program_id(0) * BLOCK

    def run(keys):
        def one(h, cols):
            allowed = allowed_pairs(first_ref, first, keys)
            logits = dot_nt(q_ref[:, cols], k_ref[:keys, :]) * SCALE
            logits = jnp.where(allowed, logits, -1e30)
            top = jnp.max(logits, axis=-1, keepdims=True)
            weights = jnp.exp(logits - top)
            count = jnp.sum(weights, axis=-1, keepdims=True)
            mixed = dot_nn(weights.astype(bf16), v_ref[:keys, :]) / count
            a_ref[:, cols] = mixed.astype(bf16)
            lse_ref[h] = top + jnp.log(count)

        each_head(one)

    by_keys(k_ref.shape[0], run)
    o_ref[...] = dot_nn(a_ref[...], w_ref[...]).astype(bf16)


def attend_back(
    main_ref, rest_ref, w_ref, q_ref, k_ref, v_ref, a_ref, lse_ref, first_ref, cos_ref, sin_ref,
    dq_ref, dkv_ref, dk_acc, dv_acc, do_acc
):
    step = pl.program_id(0)
    first = step * BLOCK
    rows = pl.ds(pl.multiple_of(first, BLOCK), BLOCK)

    @pl.when(step == 0)
    def _():
        dk_acc[...] = jnp.zeros_like(dk_acc)
        dv_acc[...] = jnp.zeros_like(dv_acc)

    grad_mixed = dot_nt(main_ref[...], w_ref[:, :MAIN]) + dot_nt(rest_ref[...], w_ref[:, MAIN:])
    do_acc[...] = grad_mixed.astype(bf16)

    def run(keys):
        def one(h, cols):
            allowed = allowed_pairs(first_ref, first, keys)
            query, grad = q_ref[:, cols], do_acc[:, cols]
            delta = jnp.sum(
                grad.astype(f32) * a_ref[:, cols].astype(f32), axis=-1, keepdims=True
            )
            logits = dot_nt(query, k_ref[:keys, :]) * SCALE
            logits = jnp.where(allowed, logits, -1e30)
            weights = jnp.exp(logits - lse_ref[h])
            grad_weights = dot_nt(grad, v_ref[:keys, :])
            grad_logits = (weights * (grad_weights - delta) * SCALE).astype(bf16)
            dq = dot_nn(grad_logits, k_ref[:keys, :])
            dq_ref[:, cols] = turn(dq, cos_ref[rows, :], -sin_ref[rows, :]).astype(bf16)
            dk_acc[:keys, :] += dot_tn(grad_logits, query)
            dv_acc[:keys, :] += dot_tn(weights.astype(bf16), grad)

        each_head(one)

    by_keys(k_ref.shape[0], run)

    @pl.when(step == pl.num_programs(0) - 1)
    def _():
        dkv_ref[:, :LANES] = turn(dk_acc[...], cos_ref[...], -sin_ref[...]).astype(bf16)
        dkv_ref[:, LANES:] = dv_acc[...].astype(bf16)


def feed(
    main_ref, rest_ref, c_main_ref, c_rest_ref, wg_ref, wu_ref, low_ref, high_ref,
    hn_ref, f_ref, dg_ref, du_ref, o_main_ref, o_rest_ref, e_ref
):
    middle = D // 2
    hn_ref[:, :MAIN] = main_ref[...]
    hn_ref[:, MAIN:] = rest_ref[...]
    gate = dot_nn(hn_ref[...], wg_ref[...])
    up = dot_nn(hn_ref[...], wu_ref[...])
    sig = 1.0 / (1.0 + jnp.exp(-gate))
    swish = gate * sig
    inner = (swish * up).astype(bf16)
    f_ref[...] = inner
    o_main_ref[:, :middle] = dot_nn(inner, low_ref[...]).astype(bf16)
    high = dot_nn(inner, high_ref[...]).astype(bf16)
    o_main_ref[:, middle:] = high[:, : MAIN - middle]
    o_rest_ref[...] = high[:, MAIN - middle :]
    grad = dot_nt(c_main_ref[:, :middle], low_ref[...])
    grad = grad + dot_nt(c_main_ref[:, middle:], high_ref[:, : MAIN - middle])
    grad = grad + dot_nt(c_rest_ref[...], high_ref[:, MAIN - middle :])
    dg_ref[...] = (grad * up * sig * (1.0 + gate * (1.0 - sig))).astype(bf16)
    du_ref[...] = (grad * swish).astype(bf16)
    back = dot_nt(dg_ref[...], wg_ref[...]) + dot_nt(du_ref[...], wu_ref[...])
    e_ref[...] = back.astype(bf16)


def inverse_norm(values):
    return lax.rsqrt(jnp.mean(values * values, axis=-1, keepdims=True) + norm_epsilon)


def norm_back(values, inverse, grad):
    return inverse * grad - values * inverse**3 * jnp.mean(grad * values, axis=-1, keepdims=True)


def body_fast(
    inputs,
    cotangent,
    doc_ids,
    positions,
    gain_first,
    query_weight,
    key_weight,
    value_weight,
    output_weight,
    gain_second,
    gate_weight,
    up_weight,
    down_weight,
):
    rows = inputs.shape[0]
    own = query_weight.shape[0]
    hidden_block = down_weight.shape[0]
    width = 4 * hidden_block
    total_rows = 8 * rows
    steps = total_rows // BLOCK
    gain_one = gain_first.reshape(own, 1)
    gain_two = gain_second.reshape(own, 1)

    marks = jnp.stack([positions // 128, positions % 128], axis=1).astype(bf16)
    marks = jnp.pad(marks, ((0, 0), (0, LANES - 2)))
    marked = jnp.concatenate([inputs, marks], axis=1)

    heads_in = [whole(own, 1), whole(own, D), whole(own, D // 2), whole(own, D // 2)]
    feed_in = [whole(own, 1), whole(own, 8 * width), whole(own, 8 * width)]
    (parts,) = call(
        pack_heads, 1, heads_in, [(whole(8, own, PAD_COLS), (8, own, PAD_COLS), bf16)]
    )(gain_one, query_weight, key_weight, value_weight)
    (both,) = call(
        pack_feed, 1, feed_in, [(whole(8, own, 2 * width), (8, own, 2 * width), bf16)]
    )(gain_two, gate_weight, up_weight)
    rows_all = gather_rows(marked)
    w_out = gather_bit(gather_bit(output_weight, "c", 0), "zl", 0)
    parts, both, w_out, cotangent = together(exchange(parts), both, w_out, cotangent)
    cot_main, cot_rest = gather_rows(cotangent[:, :MAIN]), cotangent[:, MAIN:]
    parts = parts.reshape(8 * own, PAD_COLS)
    w_query, w_kv = parts[:, :QUERY_COLS], parts[:, QUERY_COLS:]
    w_query, w_kv = together(gather_bit(w_query, "y", 0), gather_bit(w_kv, "x", 0))
    w_query = gather_bit(w_query, "x", 1).reshape(D, QUERY_COLS)
    w_kv = gather_bit(w_kv, "y", 0).reshape(D, 2 * LANES)
    w_out = across(w_out)
    rows_all, w_query, w_kv, w_out, both, cot_rest = together(
        rows_all, w_query, w_kv, w_out, both, cot_rest
    )
    w_out = jnp.pad(w_out, ((0, 0), (0, 0), (0, LANES // 2 - own), (0, 0)))
    w_out = w_out.reshape(QUERY_COLS, D)

    lane = jnp.arange(LANES) % (LANES // 2)
    freq = rotary_base ** (-lane.astype(f32) * 2.0 / HEAD)
    freq = jnp.where(lane < HALF, freq, 0.0).reshape(1, LANES)

    head_rows = pl.BlockSpec((PAIR, BLOCK, 1), lambda i: (0, i, 0))

    def rows_out(cols, kind):
        return (rows_of(cols), (total_rows, cols), kind)

    normed, query, key, value, cosine, sine, row_first = call(
        project,
        steps,
        [rows_of(D + LANES), whole(D, QUERY_COLS), whole(D, 2 * LANES), whole(1, LANES)],
        [
            rows_out(D, bf16),
            rows_out(QUERY_COLS, bf16),
            rows_out(LANES, bf16),
            rows_out(LANES, bf16),
            rows_out(LANES, f32),
            rows_out(LANES, f32),
            rows_out(1, f32),
        ],
        flops=3 << 30,
    )(rows_all, w_query, w_kv, freq)
    mixed, lse, term = call(
        attend,
        steps,
        [
            rows_of(QUERY_COLS),
            whole(total_rows, LANES),
            whole(total_rows, LANES),
            rows_of(1),
            whole(QUERY_COLS, D),
        ],
        [
            rows_out(QUERY_COLS, bf16),
            (head_rows, (PAIR, total_rows, 1), f32),
            rows_out(D, bf16),
        ],
        flops=6 << 30,
    )(query, key, value, row_first, w_out)
    term, both, cot_main, cot_rest, down_weight = together(
        term, exchange(both), cot_main, gather_bit(gather_bit(cot_rest, "zh", 0), "zl", 1), down_weight
    )
    attended = scatter_rows(term)
    both = both.reshape(8 * own, 2 * width)
    feed_low, feed_high, down_low, down_high = together(
        gather_bit(both[:, :width], "y", 0),
        gather_bit(both[:, width:], "x", 0),
        gather_bit(down_weight[:, : D // 2], "y", 0),
        gather_bit(down_weight[:, D // 2 :], "x", 0),
    )
    w_gate, w_up = gather_bit(feed_low, "x", 1), gather_bit(feed_high, "y", 0)
    attended, w_gate, w_up, down_low, down_high, cot_rest = together(
        attended, w_gate, w_up, down_low, down_high, gather_bit(cot_rest, "c", 2)
    )
    cot_rest = cot_rest.reshape(total_rows, REST)
    w_gate, w_up = w_gate.reshape(D, width), w_up.reshape(D, width)
    x_float = inputs.astype(f32)
    middle = x_float + attended.astype(f32)

    inverse_two = inverse_norm(middle)
    main, rest = gather_split((middle * inverse_two).astype(bf16))
    w_low = gather_bit(down_low, "x", 1).reshape(width, D // 2)
    w_high = gather_bit(down_high, "y", 0).reshape(width, D // 2)
    main, rest, w_low, w_high = together(main, rest, w_low, w_high)
    normed_two, inner, grad_gate, grad_up, *terms = call(
        feed,
        steps,
        [
            rows_of(MAIN),
            rows_of(REST),
            rows_of(MAIN),
            rows_of(REST),
            whole(D, width),
            whole(D, width),
            whole(width, D // 2),
            whole(width, D // 2),
        ],
        [
            rows_out(D, bf16),
            rows_out(width, bf16),
            rows_out(width, bf16),
            rows_out(width, bf16),
            rows_out(MAIN, bf16),
            rows_out(REST, bf16),
            rows_out(D, bf16),
        ],
    )(main, rest, cot_main, cot_rest, w_gate, w_up, w_low, w_high)
    normed_two, inner, *terms = together(normed_two, inner, *terms)
    out_term, back_two = terms[:2], scatter_rows(terms[2])
    feed_one = reduce_one(
        dot_tn(normed_two, grad_gate).astype(bf16), dot_tn(normed_two, grad_up).astype(bf16)
    )
    down_one = reduce_one(
        dot_tn(inner, cot_main[:, : D // 2]).astype(bf16),
        jnp.concatenate(
            [dot_tn(inner, cot_main[:, D // 2 :]), dot_tn(inner, cot_rest)], axis=-1
        ).astype(bf16),
    )
    back_two, *rest = together(back_two, *feed_one, *down_one)
    feed_one, down_one = rest[:4], rest[4:]
    cot_float = cotangent.astype(f32)
    grad_middle = cot_float + norm_back(middle, inverse_two, back_two.astype(f32))
    middle_all = gather_split(grad_middle.astype(bf16))
    feed_two, down_two = reduce_two(feed_one), reduce_two(down_one)
    feed_two = together(*feed_two)
    both_sum = exchange(reduced(feed_two).astype(bf16).reshape(8, own, 2 * width))
    rest = together(both_sum, *middle_all, *out_term, *down_two)
    both_sum, middle_all, out_term, down_two = rest[0], rest[1:3], rest[3:5], rest[5:]
    outputs = scatter_split(*out_term)

    grad_query, grad_kv = call(
        attend_back,
        steps,
        [
            rows_of(MAIN),
            rows_of(REST),
            whole(QUERY_COLS, D),
            rows_of(QUERY_COLS),
            whole(total_rows, LANES),
            whole(total_rows, LANES),
            rows_of(QUERY_COLS),
            head_rows,
            rows_of(1),
            whole(total_rows, LANES),
            whole(total_rows, LANES),
        ],
        [
            rows_out(QUERY_COLS, bf16),
            (whole(total_rows, 2 * LANES), (total_rows, 2 * LANES), bf16),
        ],
        scratch=[
            pltpu.VMEM((total_rows, LANES), f32),
            pltpu.VMEM((total_rows, LANES), f32),
            pltpu.VMEM((BLOCK, QUERY_COLS), bf16),
        ],
        flops=6 << 30,
    )(*middle_all, w_out, query, key, value, mixed, lse, row_first, cosine, sine)
    first_term = (dot_nt(grad_query, w_query) + dot_nt(grad_kv, w_kv)).astype(bf16)
    head_one = reduce_one(
        dot_tn(normed, grad_query).astype(bf16), dot_tn(normed, grad_kv).astype(bf16)
    )
    head_two = reduce_two(together(*head_one))
    first_term, mixed, out_main, *rest = together(
        first_term, mixed, outputs[0], *head_two, *down_two
    )
    head_two, down_two = rest[:4], rest[4:]
    first_sum = scatter_rows(first_term).astype(f32)
    head_term = exchange(reduced(head_two).astype(bf16).reshape(8, own, PAD_COLS))
    out_part = jnp.concatenate([dot_tn(mixed, part) for part in middle_all], axis=-1)
    out_part = out_part.astype(bf16).reshape(2, 2, LANES // 2, D)[:, :, :own]
    head_term, out_rest, *out_pair = together(
        head_term, outputs[1], *halves(out_part, "y", 1)
    )
    out_pair = halves(total(out_pair), "x", 0)
    output_grad = across(total(out_pair).astype(bf16)).astype(f32)
    down_grad = reduced(down_two)
    outputs = (middle + joined(out_main, out_rest)).astype(bf16)
    inputs_grad = (grad_middle + norm_back(x_float, inverse_norm(x_float), first_sum)).astype(bf16)

    wide = (whole(own, 8 * width), (own, 8 * width), f32)
    column = (whole(own, 1), (own, 1), f32)
    gate_grad, up_grad, second_grad = call(
        unpack_feed,
        1,
        [*feed_in, whole(8, own, 2 * width)],
        [wide, wide, column],
    )(gain_two, gate_weight, up_weight, both_sum)
    query_grad, key_grad, value_grad, first_grad = call(
        unpack_heads,
        1,
        [*heads_in, whole(8, own, PAD_COLS)],
        [
            (whole(own, D), (own, D), f32),
            (whole(own, D // 2), (own, D // 2), f32),
            (whole(own, D // 2), (own, D // 2), f32),
            column,
        ],
    )(gain_one, query_weight, key_weight, value_weight, head_term)
    return (
        outputs,
        inputs_grad,
        first_grad.reshape(own),
        query_grad,
        key_grad,
        value_grad,
        output_grad,
        second_grad.reshape(own),
        gate_grad,
        up_grad,
        down_grad,
    )


def solution(mesh):
    shape = dict(mesh.shape)
    step, axes = body, ("dp", "seq")
    if shape["dp"] == 4 and shape["seq"] == KV_HEADS:
        step, axes = body_fast, AXES
        mesh = Mesh(mesh.devices.reshape(2, 2, 2, 2, 2), AXES)
    wide, line = P(axes, None), P(axes)
    return jax.shard_map(
        step,
        mesh=mesh,
        in_specs=(wide, wide, line, line, line, wide, wide, wide, wide, line, wide, wide, wide),
        out_specs=(wide, wide, line, wide, wide, wide, wide, line, wide, wide, wide),
        check_vma=False,
    )
```
